32 devices in a mesh: dp: 16 (over z, x, core), tensor: 2 (over y).
Axes of the slice: x: 2, y: 2, z: 4, core: 2. Of those that a mesh axis runs over, the one named last changes fastest.
Arguments:
- layer_input: bfloat16 [8192, 2048], P('dp'), may hold values from -6 to 6
- cotangent: bfloat16 [8192, 2048], P('dp', 'tensor'), may hold values from -6 to 6
- attention_norm_gain: float32 [2048], replicated, may hold values from 0.1 to 1.9
- expert_norm_gain: float32 [2048], replicated, may hold values from 0.1 to 1.9
- query_norm_gain: float32 [128], replicated, may hold values from 0.1 to 1.9
- key_norm_gain: float32 [128], replicated, may hold values from 0.1 to 1.9
- query_weight_matrix: bfloat16 [2048, 2048], P(None, 'tensor'), may hold values from -0.125 to 0.125
- key_weight_matrix: bfloat16 [2048, 2048], P(None, 'tensor'), may hold values from -0.125 to 0.125
- value_weight_matrix: bfloat16 [2048, 2048], P(None, 'tensor'), may hold values from -0.125 to 0.125
- output_weight_matrix: bfloat16 [2048, 2048], P('tensor'), may hold values from -0.75 to 0.75
- adapter_projection_down: bfloat16 [3, 8, 2048, 16], replicated, may hold values from -0.125 to 0.125
- adapter_projection_up: bfloat16 [3, 8, 16, 2048], P(None, None, None, 'tensor'), may hold values from -1.5 to 1.5
- adapter_output_down: bfloat16 [8, 2048, 16], P(None, 'tensor'), may hold values from -0.75 to 0.75
- adapter_output_up: bfloat16 [8, 16, 2048], replicated, may hold values from -1.5 to 1.5
- router: bfloat16 [2048, 64], replicated, may hold values from -0.0625 to 0.0625
- expert_gate_weight: bfloat16 [64, 2048, 1024], P('dp', None, 'tensor'), may hold values from -0.125 to 0.125
- expert_up_weight: bfloat16 [64, 2048, 1024], P('dp', None, 'tensor'), may hold values from -0.125 to 0.125
- expert_down_weight: bfloat16 [64, 1024, 2048], P('dp', 'tensor'), may hold values from -1 to 1
- segments: int32 [16, 512], P('dp'), may hold values from 0 to 15, never falling along the last dimension, each value on 1 to 256 neighbouring positions
- sequence_adapter_index: int32 [16], P('dp'), may hold values from 0 to 7
- routes: int32 [8192, 8], P('dp'), may hold values from 0 to 63, all different within a row; in each aligned block of 512 rows (0 to 511, 512 to 1023, ...) at most 80 rows name the same one
Outputs:
- layer_out: bfloat16 [8192, 2048], P('dp', 'tensor')
- grad_input: float32 [8192, 2048], P('dp', 'tensor')
- grad_down_qkv: float32 [3, 8, 2048, 16], replicated
- grad_up_qkv: float32 [3, 8, 16, 2048], P(None, None, None, 'tensor')
- grad_down_out: float32 [8, 2048, 16], P(None, 'tensor')
- grad_up_out: float32 [8, 16, 2048], P(None, None, 'tensor')
The draws below stay inside these ranges and needn't reach their ends.
Inputs may be any that keep to these rules, and one draw needn't show every extreme that they name: `routes`: each row names 8 different experts. Among the rows of one index of dp no expert is named by more than 80 rows, a bound that some block reaches. `segments`: within a sequence the document numbers never fall; a document holds at most 256 positions, and one holds exactly that many.
All inputs are finite; a program needn't handle non-finite values.
Results may differ from the reference program's by a relative error of at most 0.02.
Values may be sent and summed in bfloat16 or wider, within the bound.
No kernel may reach another device: no remote copies, remote signals or barrier semaphores. Data moves between devices by JAX's collectives and lax.ppermute only.
A program may use at most 320 MiB of HBM per device.

```python
import math
import jax
import jax.numpy as jnp
import numpy as np
from jax import lax

MODEL_WIDTH = 2048
HEAD_COUNT = 16
HEAD_WIDTH = 128
EFF = 1024
TOP = 8
LEN = 512
DOCS = 16
ADAPTER_RANK = 16
ADAPTER_CHOICES = 8
TOK_DEV = 512
SEQUENCES = 16
TOKENS = 8192
EXPERTS = 64
CAP = 80
N_DP = 16


def touch_ends(result, stream_key, low, top_value):
    longest = result.shape.index(max(result.shape))
    spots = []
    for shift in (0, 1):
        where = [jax.random.randint(jax.random.fold_in(stream_key, axis), (), 0, length) for axis, length in enumerate(result.shape)]
        where[longest] = (where[longest] + shift) % result.shape[longest]
        spots.append(tuple(where))
    return result.at[spots[0]].set(low).at[spots[1]].set(top_value)


def steps_of(stream_key, shape, pieces, smallest, high):
    gain, own = 1.0, jax.random.fold_in(stream_key, 6)
    for axis_at, parts in pieces:
        steps = jnp.exp(jax.random.uniform(jax.random.fold_in(own, axis_at), (parts,), jnp.float32, smallest / len(pieces), high / len(pieces)))
        gain = gain * jnp.repeat(steps, shape[axis_at] // parts).reshape([-1 if axis == axis_at else 1 for axis in range(len(shape))])
    return gain


def length_profile(count, total, bound, slope):
    loads = [(1 << 20) // math.isqrt(grade ** slope) + 1 for grade in range(2, count + 1)]
    rest, holding = total - bound - (count - 1), [1] * (count - 1)
    while rest > 0:
        movable = [i for i in range(count - 1) if holding[i] < bound]
        whole, remaining = sum([loads[i] for i in movable]), rest
        for i in movable:
            more = min(bound - holding[i], max(1, remaining * loads[i] // whole), rest)
            holding[i] = holding[i] + more
            rest = rest - more
    return np.array([bound] + holding)


def ragged(stream_key, number_of, total, most, slope):
    if number_of == 2:
        one = jax.random.randint(stream_key, (), max(1, total - most), min(most, total - 1) + 1)
        return jnp.stack([one, total - one])
    lengths = jnp.asarray(length_profile(number_of, total, most, slope), jnp.int32)
    pairs = (number_of - 1) // 2
    donor, receiver = lengths[1:1 + 2 * pairs:2], lengths[2:2 + 2 * pairs:2]
    slack = jnp.minimum(donor - 1, most - receiver)
    moved = jax.random.randint(jax.random.fold_in(stream_key, 1), (pairs,), 0, 1 << 20) % (slack + 1)
    lengths = lengths.at[1:1 + 2 * pairs:2].set(donor - moved).at[2:2 + 2 * pairs:2].set(receiver + moved)
    return lengths[jax.random.permutation(jax.random.fold_in(stream_key, 2), number_of)]


def deal_out(stream_key, own, number, rows, count, top, bound, slope):
    order = jax.random.permutation(stream_key, count)
    crowded, ordinary = portions_of(count, rows * top, bound, slope, True), portions_of(count, rows * top, bound, slope, False)
    places = jnp.arange(count)

    def named(sizes, turn):
        used = int((sizes > 0).sum())
        fixed = max(1, used // 4)
        passed = fixed + (places - fixed + turn * (used - fixed)) % max(1, count - fixed)
        return jnp.zeros((count,), jnp.int32).at[order[jnp.where(places < fixed, places, passed)]].set(jnp.asarray(sizes, jnp.int32))

    sizes = jnp.where(number % 4 == 0, named(crowded, number // 4), named(ordinary, number - number // 4 - 1))
    mixed = jax.random.permutation(jax.random.fold_in(own, 3), count)
    giver, receiver = mixed[0:count // 2 * 2:2], mixed[1:count // 2 * 2:2]
    margin = jnp.minimum(sizes[giver] - 1, bound - sizes[receiver]) // 2
    margin = jnp.where((giver == order[0]) | (receiver == order[0]) | (sizes[receiver] == 0), 0, jnp.maximum(margin, 0))
    passed = jax.random.randint(jax.random.fold_in(own, 4), (count // 2,), 0, 1 << 20) % (margin + 1)
    sizes = sizes.at[giver].add(-passed).at[receiver].add(passed)
    members = jnp.searchsorted(jnp.cumsum(sizes), jnp.arange(rows * top), side="right").astype(jnp.int32)
    grid = members.reshape(top, rows).T
    grid = grid[jax.random.permutation(jax.random.fold_in(own, 1), rows)]
    turn = jax.random.randint(jax.random.fold_in(own, 2), (rows, 1), 0, top)
    return jnp.take_along_axis(grid, (jnp.arange(top)[None, :] + turn) % top, axis=1)


def portions_of(count, total, reach, lean, full):
    weights = [(1 << 20) // math.isqrt(grade ** lean) + 1 for grade in range(1, count + 1)]
    largest = reach if full else min(reach, max(-(-total // count), total * weights[0] // sum(weights)))
    least = 1 if total - largest >= count - 1 else 0
    given, surplus = [largest] + [least] * (count - 1), total - largest - least * (count - 1)
    while surplus > 0:
        free = [i for i in range(1, count) if given[i] < largest] or [i for i in range(1, count) if given[i] < reach]
        mass, remaining = sum([weights[i] for i in free]), surplus
        for i in free:
            extra = min(reach - given[i], max(1, remaining * weights[i] // mass), surplus)
            given[i] = given[i] + extra
            surplus = surplus - extra
    return np.array(given)


def scatter_about(own_key, dims, width, limit, pieces=(), held_as=jnp.bfloat16):
    factor_of = steps_of(own_key, dims, pieces, -0.22, 0.18) if pieces else 1.0
    values = jax.random.normal(own_key, dims, jnp.float32) * width * factor_of
    return jnp.minimum(jnp.maximum(values, -limit), limit).astype(held_as)


def setup_inputs(seed: int = 0) -> dict:
    key_list = jax.random.split(jax.random.key(seed), 22)
    layer_input = scatter_about(key_list[0], (TOKENS, MODEL_WIDTH), 1.0, 6.0, ((0, 16),))
    cotangent = scatter_about(key_list[1], (TOKENS, MODEL_WIDTH), 1.0, 6.0, ((0, 16), (1, 2)))
    attention_norm_gain = jnp.clip(1.0 + 0.18 * jax.random.normal(key_list[2], (MODEL_WIDTH,), jnp.float32), 0.1, 1.9)
    expert_norm_gain = jnp.clip(1.0 + 0.18 * jax.random.normal(key_list[3], (MODEL_WIDTH,), jnp.float32), 0.1, 1.9)
    query_norm_gain = jnp.clip(1.0 + 0.18 * jax.random.normal(key_list[4], (HEAD_WIDTH,), jnp.float32), 0.1, 1.9)
    key_norm_gain = jnp.clip(1.0 + 0.18 * jax.random.normal(key_list[5], (HEAD_WIDTH,), jnp.float32), 0.1, 1.9)
    query_weight_matrix = scatter_about(key_list[6], (MODEL_WIDTH, HEAD_COUNT * HEAD_WIDTH), MODEL_WIDTH ** -0.5, 0.125, ((1, 2),))
    key_weight_matrix = scatter_about(key_list[7], (MODEL_WIDTH, HEAD_COUNT * HEAD_WIDTH), MODEL_WIDTH ** -0.5, 0.125, ((1, 2),))
    value_weight_matrix = scatter_about(key_list[8], (MODEL_WIDTH, HEAD_COUNT * HEAD_WIDTH), MODEL_WIDTH ** -0.5, 0.125, ((1, 2),))
    output_weight_matrix = scatter_about(key_list[9], (HEAD_COUNT * HEAD_WIDTH, MODEL_WIDTH), (max(HEAD_COUNT * HEAD_WIDTH // 32, 1)) ** -0.5, 0.75, ((0, 2),))
    adapter_projection_down = scatter_about(key_list[10], (3, ADAPTER_CHOICES, MODEL_WIDTH, ADAPTER_RANK), MODEL_WIDTH ** -0.5, 0.125)
    adapter_projection_up = scatter_about(key_list[11], (3, ADAPTER_CHOICES, ADAPTER_RANK, HEAD_COUNT * HEAD_WIDTH), ADAPTER_RANK ** -0.5, 1.5, ((3, 2),))
    adapter_output_down = scatter_about(key_list[12], (ADAPTER_CHOICES, HEAD_COUNT * HEAD_WIDTH, ADAPTER_RANK), (max(HEAD_COUNT * HEAD_WIDTH // 32, 1)) ** -0.5, 0.75, ((1, 2),))
    adapter_output_up = scatter_about(key_list[13], (ADAPTER_CHOICES, ADAPTER_RANK, MODEL_WIDTH), ADAPTER_RANK ** -0.5, 1.5)
    router = scatter_about(key_list[14], (MODEL_WIDTH, EXPERTS), (4 * MODEL_WIDTH) ** -0.5, 0.0625)
    expert_gate_weight = scatter_about(key_list[15], (EXPERTS, MODEL_WIDTH, EFF), MODEL_WIDTH ** -0.5, 0.125, ((0, 16), (2, 2)))
    expert_up_weight = scatter_about(key_list[16], (EXPERTS, MODEL_WIDTH, EFF), MODEL_WIDTH ** -0.5, 0.125, ((0, 16), (2, 2)))
    expert_down_weight = scatter_about(key_list[17], (EXPERTS, EFF, MODEL_WIDTH), (max(EFF // 32, 1)) ** -0.5, 1.0, ((0, 16), (1, 2)))
    segments = jax.vmap(lambda own: jnp.searchsorted(jnp.cumsum(ragged(own, DOCS, LEN, LEN // 2, 2)), jnp.arange(LEN), side="right"))(jax.random.split(key_list[18], SEQUENCES)).reshape((SEQUENCES, LEN)).astype(jnp.int32)
    sequence_adapter_index = touch_ends(jax.random.randint(key_list[19], (SEQUENCES,), 0, ADAPTER_CHOICES), jax.random.fold_in(key_list[19], 1), 0, ADAPTER_CHOICES - 1).astype(jnp.int32)
    routes_keys = jax.random.split(jax.random.fold_in(key_list[20], 1), TOKENS // TOK_DEV)
    routes_turns = jax.random.permutation(jax.random.fold_in(key_list[20], 3), TOKENS // TOK_DEV)
    routes = jax.vmap(lambda own, number: deal_out(jax.random.fold_in(key_list[20], 2), own, number, TOK_DEV, EXPERTS, TOP, CAP, 1))(routes_keys, routes_turns).reshape((TOKENS, TOP))
    return dict(layer_input=layer_input, cotangent=cotangent, attention_norm_gain=attention_norm_gain, expert_norm_gain=expert_norm_gain, query_norm_gain=query_norm_gain, key_norm_gain=key_norm_gain, query_weight_matrix=query_weight_matrix, key_weight_matrix=key_weight_matrix, value_weight_matrix=value_weight_matrix, output_weight_matrix=output_weight_matrix, adapter_projection_down=adapter_projection_down, adapter_projection_up=adapter_projection_up, adapter_output_down=adapter_output_down, adapter_output_up=adapter_output_up, router=router, expert_gate_weight=expert_gate_weight, expert_up_weight=expert_up_weight, expert_down_weight=expert_down_weight, segments=segments, sequence_adapter_index=sequence_adapter_index, routes=routes)


highest = lax.Precision.HIGHEST
norm_eps = 1e-05
head_eps = 1e-06
rope_base = 50000.0

@jax.custom_vjp
def low(v):
    return lax.optimization_barrier(v.astype(jnp.bfloat16)).astype(jnp.float32)

@jax.custom_vjp
def low_back(v):
    return v

def low_keep(v):
    return (low(v), None)

def low_pass(kept, grad):
    return (grad,)

def back_keep(v):
    return (v, None)

def back_low(kept, grad):
    return (low(grad),)
low.defvjp(low_keep, low_pass)
low_back.defvjp(back_keep, back_low)

def matmul(left_mat, right_mat):
    return jnp.dot(left_mat, right_mat, precision=highest, preferred_element_type=jnp.float32)

def rms_scale(values, gain_vec, epsilon):
    return values * lax.rsqrt(lax.optimization_barrier(jnp.mean(values * values, axis=-1, keepdims=True)) + epsilon) * gain_vec

def rotate(values, positions):
    half_dim = values.shape[-1] // 2
    inverse = rope_base ** (-(jnp.arange(half_dim, dtype=jnp.float32) * 2.0 / values.shape[-1]))
    angles = positions.astype(jnp.float32)[:, None, None] * inverse[None, None, :]
    cosine = jnp.cos(angles)
    sine_val = jnp.sin(angles)
    first_half = values[..., :half_dim]
    second_half = values[..., half_dim:]
    return jnp.concatenate([first_half * cosine - second_half * sine_val, second_half * cosine + first_half * sine_val], axis=-1)

def attend(packed):
    queries, keys, values, doc_ids = packed
    scores = jnp.einsum('qhd,khd->hqk', queries, keys, precision=highest) * HEAD_WIDTH ** (-0.5)
    scores = low_back(scores)
    same_doc = doc_ids[:, None] == doc_ids[None, :]
    scores = jnp.where(same_doc[None], scores, -1e+30)
    top_score = lax.optimization_barrier(jnp.max(scores, axis=-1, keepdims=True))
    exp_scores = jnp.exp(scores - top_score)
    prob_rows = low(exp_scores / lax.optimization_barrier(jnp.sum(exp_scores, axis=-1, keepdims=True)))
    return jnp.einsum('hqk,khd->qhd', prob_rows, values, precision=highest)

def reference(layer_input, cotangent, attention_norm_gain, expert_norm_gain, query_norm_gain, key_norm_gain, query_weight_matrix, key_weight_matrix, value_weight_matrix, output_weight_matrix, adapter_projection_down, adapter_projection_up, adapter_output_down, adapter_output_up, router, expert_gate_weight, expert_up_weight, expert_down_weight, segments, sequence_adapter_index, routes):
    device_lane_count = ADAPTER_CHOICES * ADAPTER_RANK
    token_ids = jnp.arange(TOKENS, dtype=jnp.int32)
    seq_of = token_ids // LEN
    positions = token_ids % LEN
    token_adapter = sequence_adapter_index[seq_of]
    adapter_mask = (token_adapter[:, None] == (jnp.arange(device_lane_count, dtype=jnp.int32) // ADAPTER_RANK)[None, :]).astype(jnp.float32)
    flat_routes = routes.reshape(-1)
    route_hot = (flat_routes[:, None] == jnp.arange(EXPERTS, dtype=jnp.int32)[None, :]).astype(jnp.int32)
    slot_of = lax.optimization_barrier(jnp.sum((jnp.cumsum(route_hot, axis=0, dtype=jnp.int32) - route_hot) * route_hot, axis=1, dtype=jnp.int32))
    expert_cap = N_DP * CAP
    slot_place = (flat_routes * expert_cap + slot_of).astype(jnp.int32)
    flat_count = TOKENS * TOP
    source = jnp.full((EXPERTS * expert_cap,), flat_count, jnp.int32).at[slot_place].set(jnp.arange(flat_count, dtype=jnp.int32)).reshape(EXPERTS, expert_cap)
    attn_gain32 = attention_norm_gain.astype(jnp.float32)
    moe_gain32 = expert_norm_gain.astype(jnp.float32)
    query_gain32 = query_norm_gain.astype(jnp.float32)
    key_gain32 = key_norm_gain.astype(jnp.float32)
    w_proj = [query_weight_matrix.astype(jnp.float32), key_weight_matrix.astype(jnp.float32), value_weight_matrix.astype(jnp.float32)]
    w_output32 = output_weight_matrix.astype(jnp.float32)
    router32 = router.astype(jnp.float32)
    gate_all = expert_gate_weight.astype(jnp.float32)
    up_all = expert_up_weight.astype(jnp.float32)
    down_all = expert_down_weight.astype(jnp.float32)

    def forward_layer(hidden32, down_qkv, up_qkv, down_out, up_out):
        normed = low(rms_scale(hidden32, attn_gain32, norm_eps))

        def project(projection_index):
            down_factor_rows = down_qkv[projection_index].transpose(1, 0, 2).reshape(MODEL_WIDTH, device_lane_count)
            latent = low(low_back(matmul(normed, down_factor_rows)))
            return matmul(normed, w_proj[projection_index]) + matmul(latent * adapter_mask, up_qkv[projection_index].reshape(device_lane_count, HEAD_COUNT * HEAD_WIDTH))
        query_raw = low_back(project(0))
        key_raw = low_back(project(1))
        value_raw = low_back(project(2))
        queries = low(rotate(rms_scale(query_raw.reshape(TOKENS, HEAD_COUNT, HEAD_WIDTH), query_gain32, head_eps), positions))
        keys = low(rotate(rms_scale(key_raw.reshape(TOKENS, HEAD_COUNT, HEAD_WIDTH), key_gain32, head_eps), positions))
        values = low(value_raw.reshape(TOKENS, HEAD_COUNT, HEAD_WIDTH))

        def per_seq(array_in):
            return array_in.reshape(SEQUENCES, LEN, HEAD_COUNT, HEAD_WIDTH)
        attended = lax.map(jax.checkpoint(attend), (per_seq(queries), per_seq(keys), per_seq(values), segments))
        attended = low(low_back(attended.reshape(TOKENS, HEAD_COUNT * HEAD_WIDTH)))
        latent_out = low(low_back(matmul(attended, down_out.transpose(1, 0, 2).reshape(HEAD_COUNT * HEAD_WIDTH, device_lane_count))))
        branch = low_back(matmul(attended, w_output32) + matmul(latent_out * adapter_mask, up_out.reshape(device_lane_count, MODEL_WIDTH)))
        mixed_rows = hidden32 + branch
        moe_in = low(rms_scale(mixed_rows, moe_gain32, norm_eps))
        logits = low_back(matmul(moe_in, router32))
        chosen = jnp.take_along_axis(logits, routes, axis=1)
        chosen_top = lax.optimization_barrier(jnp.max(chosen, axis=1, keepdims=True))
        chosen_exp = jnp.exp(chosen - chosen_top)
        gate_vals = chosen_exp / lax.optimization_barrier(jnp.sum(chosen_exp, axis=1, keepdims=True))
        padded = jnp.concatenate([moe_in, jnp.zeros((1, MODEL_WIDTH), moe_in.dtype)], axis=0)

        def expert(packed):
            source_ids, gate_mat, up_mat, down_mat = packed
            rows_in = padded[source_ids // TOP]
            pre_gate = low_back(matmul(rows_in, gate_mat))
            pre_up = low_back(matmul(rows_in, up_mat))
            hidden = low(low_back(pre_gate * jax.nn.sigmoid(pre_gate) * pre_up))
            return low(low_back(matmul(hidden, down_mat)))
        expert_out = lax.map(jax.checkpoint(expert), (source, gate_all, up_all, down_all))
        route_out = expert_out.reshape(EXPERTS * expert_cap, MODEL_WIDTH)[slot_place].reshape(TOKENS, TOP, MODEL_WIDTH)
        return mixed_rows + lax.optimization_barrier(jnp.sum(gate_vals[:, :, None] * route_out, axis=1))
    layer_result, backward_pullback = jax.vjp(forward_layer, layer_input.astype(jnp.float32), adapter_projection_down.astype(jnp.float32), adapter_projection_up.astype(jnp.float32), adapter_output_down.astype(jnp.float32), adapter_output_up.astype(jnp.float32))
    gradients = backward_pullback(cotangent.astype(jnp.float32))
    return (layer_result.astype(jnp.bfloat16), gradients[0], gradients[1], gradients[2], gradients[3], gradients[4])
```

```python
import functools

import jax
import jax.numpy as jnp
from jax import lax
from jax.experimental import pallas as pl
from jax.experimental.pallas import tpu as pltpu
from jax.sharding import PartitionSpec as P

MODEL_WIDTH = 2048
HEAD_WIDTH = 128
TOP = 8
LEN = 512
ADAPTER_RANK = 16
ADAPTER_CHOICES = 8
QUAD = 4

norm_eps = 1e-05
head_eps = 1e-06
rope_base = 50000.0
half_type = jnp.bfloat16
VMEM_LIMIT = 56 * 1024 * 1024


def rms_scale(values, gain_vec, epsilon):
    return (
        values * lax.rsqrt(jnp.mean(values * values, axis=-1, keepdims=True) + epsilon) * gain_vec
    )


def rotate(values, positions):
    half_dim = values.shape[-1] // 2
    inverse = rope_base ** (-(jnp.arange(half_dim, dtype=jnp.float32) * 2.0 / values.shape[-1]))
    angles = positions.astype(jnp.float32)[:, None, None] * inverse[None, None, :]
    cosine = jnp.cos(angles)
    sine_val = jnp.sin(angles)
    first_half = values[..., :half_dim]
    second_half = values[..., half_dim:]
    return jnp.concatenate(
        [
            first_half * cosine - second_half * sine_val,
            second_half * cosine + first_half * sine_val,
        ],
        axis=-1,
    )


def head_prep(projected, gain_vec, positions):
    shaped = projected.reshape(projected.shape[0], projected.shape[1] // HEAD_WIDTH, HEAD_WIDTH)
    return rotate(rms_scale(shaped, gain_vec, head_eps), positions)


def down_factor_layout(adapter_down_factor):
    return adapter_down_factor.transpose(1, 0, 2).reshape(
        adapter_down_factor.shape[1], adapter_down_factor.shape[0] * adapter_down_factor.shape[2]
    )


def nt_dot(left, right):
    return lax.dot_general(
        left, right, (((1,), (1,)), ((), ())), preferred_element_type=jnp.float32
    )


def start_blocks(block_refs, buffer_ref, sems, flip):
    for b in range(QUAD):
        for r in range(2):
            pltpu.make_async_copy(
                block_refs[2 * b + r], buffer_ref.at[b, r ^ flip], sems.at[b, r]
            ).start()


def wait_block(block_refs, buffer_ref, sems, b):
    for r in range(2):
        pltpu.make_async_copy(block_refs[0], buffer_ref.at[b, r], sems.at[b, r]).wait()


def pick_rows(place_ref, buffer_ref, rows_ref, b, experts, cap, tile):
    toks = buffer_ref.shape[2]
    slot = lax.broadcasted_iota(jnp.int32, (cap, toks), 0)
    picks = jnp.concatenate(
        [jnp.where(slot == place_ref[b, e], 1.0, 0.0) for e in range(experts)], axis=0
    ).astype(half_type)
    half = buffer_ref.shape[3]
    for h in range(2):
        for start in range(0, half, tile):
            rows = jnp.dot(
                picks,
                buffer_ref[b, h, :, start : start + tile],
                preferred_element_type=jnp.float32,
            ).astype(half_type)
            for e in range(experts):
                rows_ref[e, h, b, :, start : start + tile] = rows[e * cap : (e + 1) * cap]


def add_rows(target_ref, rows_ref, out_ref, b, flip, experts, cap, tile):
    target = target_ref[b]
    toks = target.shape[0]
    lane = lax.broadcasted_iota(jnp.int32, (toks, experts * cap), 1)
    hit = lane == target[:, 0:1]
    for e in range(1, experts):
        hit = jnp.logical_or(hit, lane == target[:, e : e + 1])
    spread = jnp.where(hit, 1.0, 0.0).astype(half_type)
    half = rows_ref.shape[4]
    for h in range(2):
        for start in range(0, half, tile):
            rows = jnp.concatenate(
                [rows_ref[e, h, b, :, start : start + tile] for e in range(experts)], axis=0
            )
            out_ref[0, h ^ flip, :, start : start + tile] = jnp.dot(
                spread, rows, preferred_element_type=jnp.float32
            ).astype(half_type)


def grad_rows_kernel(experts, cap, flip_ref, place_ref, down_ref, *refs):
    block_refs = refs[: 2 * QUAD]
    out_ref, buffer_ref, rows_ref, sems = refs[2 * QUAD :]
    step = pl.program_id(0)
    half = buffer_ref.shape[3]

    @pl.when(step == 0)
    def _():
        start_blocks(block_refs, buffer_ref, sems, flip_ref[0])

    @pl.when(step < QUAD)
    def _():
        wait_block(block_refs, buffer_ref, sems, step)
        pick_rows(place_ref, buffer_ref, rows_ref, step, experts, cap, 512)

    @pl.when(step >= QUAD)
    def _():
        e = step - QUAD
        total = nt_dot(rows_ref[e, 0].reshape(QUAD * cap, half), down_ref[0, :, :half])
        total += nt_dot(rows_ref[e, 1].reshape(QUAD * cap, half), down_ref[0, :, half:])
        out_ref[0] = total.astype(half_type)


def expert_kernel(experts, cap, flip_ref, place_ref, gate_ref, target_ref, wg_ref, wu_ref, dh_ref, *refs):
    block_refs = refs[: 2 * QUAD]
    send_ref, keep_ref, hidden_ref, dgate_ref, buffer_ref, rows_ref, sems = refs[2 * QUAD :]
    step = pl.program_id(0)
    half = buffer_ref.shape[3]
    toks = buffer_ref.shape[2]

    @pl.when(step == 0)
    def _():
        start_blocks(block_refs, buffer_ref, sems, flip_ref[0])

    @pl.when(step < QUAD)
    def _():
        wait_block(block_refs, buffer_ref, sems, step)
        pick_rows(place_ref, buffer_ref, rows_ref, step, experts, cap, 512)

    @pl.when(jnp.logical_and(step >= QUAD, step < QUAD + experts))
    def _():
        e = step - QUAD
        first = rows_ref[e, 0].reshape(QUAD * cap, half)
        second = rows_ref[e, 1].reshape(QUAD * cap, half)
        pre_gate = jnp.dot(first, wg_ref[0, :half], preferred_element_type=jnp.float32)
        pre_gate += jnp.dot(second, wg_ref[0, half:], preferred_element_type=jnp.float32)
        pre_up = jnp.dot(first, wu_ref[0, :half], preferred_element_type=jnp.float32)
        pre_up += jnp.dot(second, wu_ref[0, half:], preferred_element_type=jnp.float32)
        sig = lax.logistic(pre_gate)
        silu = pre_gate * sig
        act = silu * pre_up
        d_raw = dh_ref[0].astype(jnp.float32)
        slot = lax.broadcasted_iota(jnp.int32, (cap, toks), 0)
        gate_parts = []
        for b in range(QUAD):
            hit = slot == place_ref[b, e]
            gate_parts.append(
                jnp.sum(jnp.where(hit, gate_ref[b, e], 0.0), axis=1, keepdims=True)
            )
        gate_col = jnp.concatenate(gate_parts, axis=0)
        hidden_ref[0] = (act * gate_col).astype(half_type)
        d_col = jnp.sum(act * d_raw, axis=1, keepdims=True)
        for b in range(QUAD):
            hit = slot == place_ref[b, e]
            dgate_ref[e, b] = jnp.sum(
                jnp.where(hit, d_col[b * cap : (b + 1) * cap], 0.0), axis=0, keepdims=True
            )
        d_hidden = d_raw * gate_col
        d_up = (d_hidden * silu).astype(half_type)
        d_gate = (d_hidden * pre_up * (sig * (1.0 + pre_gate * (1.0 - sig)))).astype(half_type)
        for h in range(2):
            d_in = nt_dot(d_gate, wg_ref[0, h * half : (h + 1) * half])
            d_in += nt_dot(d_up, wu_ref[0, h * half : (h + 1) * half])
            rows_ref[e, h] = d_in.astype(half_type).reshape(QUAD, cap, half)

    for which, out_ref in ((0, send_ref), (1, keep_ref)):
        first_step = QUAD + experts + 2 * which

        @pl.when(jnp.logical_and(step >= first_step, step < first_step + 2))
        def _():
            b = 2 * (step - first_step) + 1 - which
            add_rows(target_ref, rows_ref, out_ref, b, flip_ref[0], experts, cap, 512)


def output_kernel(experts, cap, flip_ref, target_ref, down_ref, hidden_ref, send_ref, keep_ref, rows_ref):
    step = pl.program_id(0)
    half = rows_ref.shape[4]

    @pl.when(step < experts)
    def _():
        for h in range(2):
            out = jnp.dot(
                hidden_ref[0],
                down_ref[0, :, h * half : (h + 1) * half],
                preferred_element_type=jnp.float32,
            )
            rows_ref[step, h] = out.astype(half_type).reshape(QUAD, cap, half)

    for which, out_ref in ((0, send_ref), (1, keep_ref)):
        first_step = experts + 2 * which

        @pl.when(jnp.logical_and(step >= first_step, step < first_step + 2))
        def _():
            b = 2 * (step - first_step) + 1 - which
            add_rows(target_ref, rows_ref, out_ref, b, flip_ref[0], experts, cap, 512)


def whole(shape):
    return pl.BlockSpec(shape, lambda i, *_: (0,) * len(shape), pipeline_mode=pl.Buffered(1))


def per_step(shape, first, count):
    return pl.BlockSpec(
        (1,) + shape[1:], lambda i, *_: (jnp.clip(i - first, 0, count - 1),) + (0,) * (len(shape) - 1)
    )


def block_scratch(toks, half, experts, cap, with_buffer):
    rows = pltpu.VMEM((experts, 2, QUAD, cap, half), half_type)
    if not with_buffer:
        return [rows]
    return [
        pltpu.VMEM((QUAD, 2, toks, half), half_type),
        rows,
        pltpu.SemaphoreType.DMA((QUAD, 2)),
    ]


def call_grad_rows(flip, place, down, halves, cap):
    experts, hidden_units, width = down.shape
    toks, half = halves[0].shape
    rows = QUAD * cap
    return pl.pallas_call(
        functools.partial(grad_rows_kernel, experts, cap),
        out_shape=jax.ShapeDtypeStruct((experts, rows, hidden_units), half_type),
        grid_spec=pltpu.PrefetchScalarGridSpec(
            num_scalar_prefetch=1,
            grid=(QUAD + experts,),
            in_specs=[whole(place.shape), per_step(down.shape, QUAD, experts)]
            + [pl.BlockSpec(memory_space=pl.ANY)] * (2 * QUAD),
            out_specs=per_step((experts, rows, hidden_units), QUAD, experts),
            scratch_shapes=block_scratch(toks, half, experts, cap, True),
        ),
        compiler_params=pltpu.CompilerParams(
            dimension_semantics=("arbitrary",), vmem_limit_bytes=VMEM_LIMIT
        ),
        cost_estimate=pl.CostEstimate(
            flops=2 * experts * rows * width * (toks + hidden_units),
            bytes_accessed=2 * (down.size + 2 * QUAD * toks * half + experts * rows * hidden_units),
            transcendentals=0,
        ),
        name="grad_rows",
    )(flip, place, down, *halves)


def call_experts(flip, place, gate, target, gate_w, up_w, d_raw, halves, cap):
    experts, width, hidden_units = gate_w.shape
    toks, half = halves[0].shape
    rows = QUAD * cap
    blocks = (2, 2, toks, half)
    return pl.pallas_call(
        functools.partial(expert_kernel, experts, cap),
        out_shape=(
            jax.ShapeDtypeStruct(blocks, half_type),
            jax.ShapeDtypeStruct(blocks, half_type),
            jax.ShapeDtypeStruct((experts, rows, hidden_units), half_type),
            jax.ShapeDtypeStruct((experts, QUAD, 1, toks), jnp.float32),
        ),
        grid_spec=pltpu.PrefetchScalarGridSpec(
            num_scalar_prefetch=1,
            grid=(2 * QUAD + experts,),
            in_specs=[
                whole(place.shape),
                whole(gate.shape),
                whole(target.shape),
                per_step(gate_w.shape, QUAD, experts),
                per_step(up_w.shape, QUAD, experts),
                per_step(d_raw.shape, QUAD, experts),
            ]
            + [pl.BlockSpec(memory_space=pl.ANY)] * (2 * QUAD),
            out_specs=(
                per_step(blocks, QUAD + experts, 2),
                per_step(blocks, QUAD + experts + 2, 2),
                per_step((experts, rows, hidden_units), QUAD, experts),
                whole((experts, QUAD, 1, toks)),
            ),
            scratch_shapes=block_scratch(toks, half, experts, cap, True),
        ),
        compiler_params=pltpu.CompilerParams(
            dimension_semantics=("arbitrary",), vmem_limit_bytes=VMEM_LIMIT
        ),
        cost_estimate=pl.CostEstimate(
            flops=4 * experts * rows * width * (toks + 2 * hidden_units),
            bytes_accessed=2 * (2 * gate_w.size + 4 * QUAD * toks * half),
            transcendentals=experts * rows * hidden_units,
        ),
        name="experts",
    )(flip, place, gate, target, gate_w, up_w, d_raw, *halves)


def call_output(flip, target, down, hidden, cap, half):
    experts, hidden_units, width = down.shape
    toks = target.shape[1]
    rows = QUAD * cap
    blocks = (2, 2, toks, half)
    return pl.pallas_call(
        functools.partial(output_kernel, experts, cap),
        out_shape=(
            jax.ShapeDtypeStruct(blocks, half_type),
            jax.ShapeDtypeStruct(blocks, half_type),
        ),
        grid_spec=pltpu.PrefetchScalarGridSpec(
            num_scalar_prefetch=1,
            grid=(QUAD + experts,),
            in_specs=[
                whole(target.shape),
                per_step(down.shape, 0, experts),
                per_step(hidden.shape, 0, experts),
            ],
            out_specs=(per_step(blocks, experts, 2), per_step(blocks, experts + 2, 2)),
            scratch_shapes=block_scratch(toks, half, experts, cap, False),
        ),
        compiler_params=pltpu.CompilerParams(
            dimension_semantics=("arbitrary",), vmem_limit_bytes=VMEM_LIMIT
        ),
        cost_estimate=pl.CostEstimate(
            flops=2 * experts * rows * width * (toks + hidden_units),
            bytes_accessed=2 * (down.size + 2 * QUAD * toks * half),
            transcendentals=0,
        ),
        name="outputs",
    )(flip, target, down, hidden)


def swap(values, data_count, bit):
    return lax.ppermute(values, "dp", [(i, i ^ bit) for i in range(data_count)])


def onward(values, data_count):
    return lax.ppermute(values, "dp", [(i, (i + QUAD) % data_count) for i in range(data_count)])


def other_side(values):
    return lax.ppermute(values, "tensor", [(0, 1), (1, 0)])


def gather_groups(first, second, data_count, pair):
    groups = []
    for j in range(data_count // QUAD):
        core_first = swap(first, data_count, 1)
        core_second = swap(second, data_count, 1)
        across_first = swap(first, data_count, 2)
        across_second = other_side(across_first) if pair else swap(second, data_count, 2)
        groups.append(
            [
                first,
                second,
                core_first,
                core_second,
                across_first,
                across_second,
                swap(across_first, data_count, 1),
                swap(across_second, data_count, 1),
            ]
        )
        if j + 1 < data_count // QUAD:
            first = onward(first, data_count)
            second = onward(second, data_count)
    return groups


def plus(left, right):
    return (left.astype(jnp.float32) + right.astype(jnp.float32)).astype(half_type)


def reduce_group(send, keep, data_count, pair):
    got = swap(send, data_count, 1)
    if pair:
        away = plus(keep[1, 1], got[1, 1])
        near = keep[1, 0].astype(jnp.float32) + got[1, 0].astype(jnp.float32)
        near = (near + other_side(away).astype(jnp.float32)).astype(half_type)
        first = (
            keep[0, 0].astype(jnp.float32)
            + got[0, 0].astype(jnp.float32)
            + swap(near, data_count, 2).astype(jnp.float32)
        ).astype(half_type)
        return first, plus(keep[0, 1], got[0, 1])
    across = plus(keep[1], got[1])
    total = (
        keep[0].astype(jnp.float32)
        + got[0].astype(jnp.float32)
        + swap(across, data_count, 2).astype(jnp.float32)
    ).astype(half_type)
    return total[0], total[1]


def reduce_groups(parts, data_count, pair):
    sums = [reduce_group(send, keep, data_count, pair) for send, keep in parts]
    count = len(sums)
    first, second = sums[1 % count]
    for j in range(2, count + 1):
        first = plus(onward(first, data_count), sums[j % count][0])
        second = plus(onward(second, data_count), sums[j % count][1])
    return first, second


def local(
    layer_input,
    cotangent,
    attention_norm_gain,
    expert_norm_gain,
    query_norm_gain,
    key_norm_gain,
    query_weight_matrix,
    key_weight_matrix,
    value_weight_matrix,
    output_weight_matrix,
    adapter_projection_down,
    adapter_projection_up,
    adapter_output_down,
    adapter_output_up,
    router,
    expert_gate_weight,
    expert_up_weight,
    expert_down_weight,
    segments,
    sequence_adapter_index,
    routes,
):
    tok_count = layer_input.shape[0]
    tensor_count = lax.axis_size("tensor")
    data_count = lax.axis_size("dp")
    pair = tensor_count == 2
    ring_count = data_count // QUAD
    col_width = MODEL_WIDTH // tensor_count
    half_width = MODEL_WIDTH // 2
    side = lax.axis_index("tensor")
    col_start = side * col_width
    place_dp = lax.axis_index("dp")
    flip = side.astype(jnp.int32) if pair else jnp.int32(0)
    flip_arr = flip.reshape(1)
    shard_local_width = query_weight_matrix.shape[1]
    local_heads = shard_local_width // HEAD_WIDTH
    local_experts = expert_gate_weight.shape[0]
    expert_total = local_experts * data_count
    capacity = 5 * tok_count * TOP // (4 * expert_total)
    device_lane_count = ADAPTER_CHOICES * ADAPTER_RANK
    score_scale = HEAD_WIDTH ** (-0.5)
    token_ids = jnp.arange(tok_count, dtype=jnp.int32)

    def to_sides(full):
        if pair:
            low_cols, high_cols = full[:, :half_width], full[:, half_width:]
            return (
                jnp.where(flip == 0, low_cols, high_cols),
                jnp.where(flip == 0, high_cols, low_cols),
            )
        return full[:, :half_width], full[:, half_width:]

    def from_sides(first, second):
        if pair:
            return jnp.concatenate(
                [jnp.where(flip == 0, first, second), jnp.where(flip == 0, second, first)], axis=1
            )
        return jnp.concatenate([first, second], axis=1)

    routes_t = routes.T
    expert_ids = jnp.arange(expert_total, dtype=jnp.int32)
    chosen_mask = jnp.any(routes_t[:, None, :] == expert_ids[None, :, None], axis=0)
    earlier = (token_ids[:, None] < token_ids[None, :]).astype(half_type)
    rank = jnp.dot(chosen_mask.astype(half_type), earlier, preferred_element_type=jnp.float32)
    place_own = jnp.where(chosen_mask, rank, -1.0).astype(jnp.int32)
    place_all = lax.all_to_all(
        place_own.reshape(data_count, local_experts, tok_count), "dp", 0, 0, tiled=True
    )
    ring_at, quad_at = place_dp // QUAD, place_dp % QUAD
    group_ids = jnp.arange(data_count, dtype=jnp.int32)
    order = ((ring_at - group_ids // QUAD) % ring_count) * QUAD + (quad_at ^ (group_ids % QUAD))
    place_all = place_all[order]
    target_all = jnp.where(
        place_all >= 0,
        place_all + capacity * jnp.arange(local_experts, dtype=jnp.int32)[None, :, None],
        -1,
    ).transpose(0, 2, 1)

    def group_of(values, j):
        return values[j * QUAD : (j + 1) * QUAD]

    if pair:
        g_first = cotangent
        g_second = other_side(cotangent)
    else:
        g_full = lax.all_gather(cotangent, "tensor", axis=1, tiled=True)
        g_first, g_second = g_full[:, :half_width], g_full[:, half_width:]
    g_groups = gather_groups(g_first, g_second, data_count, pair)
    d_raw = [
        call_grad_rows(
            flip_arr,
            group_of(place_all, j)[:, :, None, :],
            expert_down_weight,
            g_groups[j],
            capacity,
        )
        for j in range(ring_count)
    ]

    seq_of = token_ids // LEN
    positions = token_ids % LEN
    seq_hot = seq_of[:, None] == jnp.arange(tok_count // LEN, dtype=jnp.int32)[None, :]
    token_adapter = jnp.sum(jnp.where(seq_hot, sequence_adapter_index[None, :], 0), axis=1)
    adapter_mask = (
        token_adapter[:, None]
        == (jnp.arange(device_lane_count, dtype=jnp.int32) // ADAPTER_RANK)[None, :]
    )
    mask_float = adapter_mask.astype(jnp.float32)
    mask_half = adapter_mask.astype(half_type)
    doc_flat = segments.reshape(-1) + 16 * 1024 * seq_of
    hidden32 = layer_input.astype(jnp.float32)
    normed32, norm1_back = jax.vjp(
        lambda values: rms_scale(values, attention_norm_gain, norm_eps), hidden32
    )
    normed = normed32.astype(half_type)
    w_proj = [query_weight_matrix, key_weight_matrix, value_weight_matrix]
    down_factor_rows = [
        down_factor_layout(adapter_projection_down[projection_index])
        for projection_index in range(3)
    ]
    up_factor_rows = [
        adapter_projection_up[projection_index].reshape(device_lane_count, shard_local_width)
        for projection_index in range(3)
    ]
    latents = []
    raw_proj = []
    for projection_index in range(3):
        latent = jnp.dot(
            normed, down_factor_rows[projection_index], preferred_element_type=jnp.float32
        ).astype(half_type)
        latents.append(latent * mask_half)
        raw_proj.append(
            jnp.dot(normed, w_proj[projection_index], preferred_element_type=jnp.float32)
            + jnp.dot(
                latent * mask_half,
                up_factor_rows[projection_index],
                preferred_element_type=jnp.float32,
            )
        )
    query_f, query_back = jax.vjp(
        lambda projected: head_prep(projected, query_norm_gain, positions), raw_proj[0]
    )
    key_f, key_back = jax.vjp(
        lambda projected: head_prep(projected, key_norm_gain, positions), raw_proj[1]
    )
    queries = query_f.astype(half_type)
    keys = key_f.astype(half_type)
    values = raw_proj[2].reshape(tok_count, local_heads, HEAD_WIDTH).astype(half_type)

    same_doc = (doc_flat[:, None] == doc_flat[None, :])[None]

    def block_scores():
        scores = (
            jnp.einsum("qhd,khd->hqk", queries, keys, preferred_element_type=jnp.float32)
            * score_scale
        )
        return jnp.where(same_doc, scores, -1e30)

    scores = block_scores()
    top_score = jnp.max(scores, axis=-1, keepdims=True)
    exp_scores = jnp.exp(scores - top_score)
    row_total = jnp.sum(exp_scores, axis=-1, keepdims=True)
    prob_half = (exp_scores / row_total).astype(half_type)
    attended = jnp.einsum("hqk,khd->qhd", prob_half, values, preferred_element_type=jnp.float32)
    log_totals = top_score[..., 0] + jnp.log(row_total[..., 0])
    attended = attended.reshape(tok_count, shard_local_width).astype(half_type)
    output_down_rows = down_factor_layout(adapter_output_down)
    output_up_rows = adapter_output_up.reshape(device_lane_count, MODEL_WIDTH)
    proj_part = jnp.dot(attended, output_weight_matrix, preferred_element_type=jnp.float32)
    latent_part = jnp.dot(attended, output_down_rows, preferred_element_type=jnp.float32)

    def tensor_sum(part):
        part = part.astype(half_type)
        if pair:
            return part.astype(jnp.float32) + other_side(part).astype(jnp.float32)
        return lax.psum(part, "tensor").astype(jnp.float32)

    attn_total = tensor_sum(proj_part)
    latent_total = tensor_sum(latent_part)
    latent_out = latent_total.astype(half_type) * mask_half
    mixed_rows = (
        hidden32
        + attn_total
        + jnp.dot(latent_out, output_up_rows, preferred_element_type=jnp.float32)
    )
    moe_in32, norm2_back = jax.vjp(
        lambda values: rms_scale(values, expert_norm_gain, norm_eps), mixed_rows
    )
    moe_in = moe_in32.astype(half_type)
    x_groups = gather_groups(*to_sides(moe_in), data_count, pair)

    logits_t = lax.dot_general(
        router, moe_in, (((0,), (1,)), ((), ())), preferred_element_type=jnp.float32
    )
    top_logit = jnp.max(jnp.where(chosen_mask, logits_t, -jnp.inf), axis=0, keepdims=True)
    gate_exp = jnp.where(chosen_mask, jnp.exp(jnp.minimum(logits_t - top_logit, 0.0)), 0.0)
    gates_t = gate_exp / jnp.sum(gate_exp, axis=0, keepdims=True)
    gates_all = lax.all_to_all(
        gates_t.reshape(data_count, local_experts, tok_count), "dp", 0, 0, tiled=True
    )[order]

    grad_parts = []
    out_hidden = []
    d_gate_parts = []
    for j in range(ring_count):
        send, keep, hidden, d_gate = call_experts(
            flip_arr,
            group_of(place_all, j)[:, :, None, :],
            group_of(gates_all, j)[:, :, None, :],
            group_of(target_all, j),
            expert_gate_weight,
            expert_up_weight,
            d_raw[j],
            x_groups[j],
            capacity,
        )
        grad_parts.append((send, keep))
        out_hidden.append(hidden)
        d_gate_parts.append(d_gate[:, :, 0, :].transpose(1, 0, 2))

    d_gate_all = jnp.concatenate(d_gate_parts, axis=0)
    back_order = ((ring_at - group_ids // QUAD) % ring_count) * QUAD + (
        quad_at ^ (group_ids % QUAD)
    )
    d_gate_home = lax.all_to_all(d_gate_all[back_order], "dp", 0, 0, tiled=True)
    d_gate_home = d_gate_home.reshape(expert_total, tok_count)
    if pair:
        d_gate_home = d_gate_home + other_side(d_gate_home)
    else:
        d_gate_home = lax.psum(d_gate_home, "tensor")
    weighted = gates_t * d_gate_home
    grad_logits_t = (
        gates_t * (d_gate_home - jnp.sum(weighted, axis=0, keepdims=True))
    ).astype(half_type)

    grad_first, grad_second = reduce_groups(grad_parts, data_count, pair)
    if pair:
        got_first = other_side(grad_first)
        got_second = other_side(grad_second)
        full_first = grad_first.astype(jnp.float32) + got_second.astype(jnp.float32)
        full_second = grad_second.astype(jnp.float32) + got_first.astype(jnp.float32)
        grad_moe_expert = from_sides(full_first, full_second)
        grad_full = from_sides(g_first, g_second).astype(jnp.float32)
    else:
        grad_moe_expert = lax.psum(from_sides(grad_first, grad_second), "tensor").astype(
            jnp.float32
        )
        grad_full = g_full.astype(jnp.float32)
    grad_moe_in = grad_moe_expert + lax.dot_general(
        grad_logits_t, router, (((0,), (1,)), ((), ())), preferred_element_type=jnp.float32
    )

    out_parts = [
        call_output(
            flip_arr,
            group_of(target_all, j),
            expert_down_weight,
            out_hidden[j],
            capacity,
            half_width,
        )
        for j in range(ring_count)
    ]
    out_first, out_second = reduce_groups(out_parts, data_count, pair)
    if pair:
        moe_cols = out_first.astype(jnp.float32) + other_side(out_second).astype(jnp.float32)
    else:
        moe_cols = lax.psum_scatter(
            from_sides(out_first, out_second), "tensor", scatter_dimension=1, tiled=True
        ).astype(jnp.float32)
    mixed_cols = lax.dynamic_slice_in_dim(mixed_rows, col_start, col_width, 1)
    layer_out = (mixed_cols + moe_cols).astype(half_type)

    grad_mixed = grad_full + norm2_back(grad_moe_in)[0]
    grad_branch = grad_mixed.astype(half_type)
    grad_latent_out = (
        jnp.einsum("td,ad->ta", grad_branch, output_up_rows, preferred_element_type=jnp.float32)
        * mask_float
    ).astype(half_type)
    branch_cols = lax.dynamic_slice_in_dim(grad_branch, col_start, col_width, 1)
    grad_up_out = jnp.einsum(
        "ta,td->ad", latent_out, branch_cols, preferred_element_type=jnp.float32
    ).reshape(ADAPTER_CHOICES, ADAPTER_RANK, col_width)
    grad_attended = jnp.einsum(
        "td,cd->tc", grad_branch, output_weight_matrix, preferred_element_type=jnp.float32
    )
    grad_attended = grad_attended + jnp.einsum(
        "ta,ca->tc", grad_latent_out, output_down_rows, preferred_element_type=jnp.float32
    )
    grad_heads = grad_attended.astype(half_type).reshape(tok_count, local_heads, HEAD_WIDTH)
    grad_down_out = jnp.einsum(
        "tc,ta->ca", attended, grad_latent_out, preferred_element_type=jnp.float32
    )
    grad_down_out = grad_down_out.reshape(
        shard_local_width, ADAPTER_CHOICES, ADAPTER_RANK
    ).transpose(1, 0, 2)

    prob_block = jnp.where(same_doc, jnp.exp(block_scores() - log_totals[:, :, None]), 0.0)
    grad_prob = jnp.einsum("qhd,khd->hqk", grad_heads, values, preferred_element_type=jnp.float32)
    row_delta = jnp.sum(prob_block * grad_prob, axis=-1, keepdims=True)
    grad_scores = (prob_block * (grad_prob - row_delta)).astype(half_type)
    grad_queries = (
        jnp.einsum("hqk,khd->qhd", grad_scores, keys, preferred_element_type=jnp.float32)
        * score_scale
    )
    grad_keys = (
        jnp.einsum("hqk,qhd->khd", grad_scores, queries, preferred_element_type=jnp.float32)
        * score_scale
    )
    grad_values = jnp.einsum(
        "hqk,qhd->khd",
        prob_block.astype(half_type),
        grad_heads,
        preferred_element_type=jnp.float32,
    ).reshape(tok_count, shard_local_width)
    grad_raw = [
        query_back(grad_queries)[0].astype(half_type),
        key_back(grad_keys)[0].astype(half_type),
        grad_values.astype(half_type),
    ]
    grad_normed_part = jnp.zeros((tok_count, MODEL_WIDTH), jnp.float32)
    latent_parts = []
    for projection_index in range(3):
        grad_normed_part = grad_normed_part + jnp.einsum(
            "tc,dc->td",
            grad_raw[projection_index],
            w_proj[projection_index],
            preferred_element_type=jnp.float32,
        )
        latent_parts.append(
            jnp.einsum(
                "tc,ac->ta",
                grad_raw[projection_index],
                up_factor_rows[projection_index],
                preferred_element_type=jnp.float32,
            )
        )
    grad_latent_sum = tensor_sum(jnp.stack(latent_parts))
    grad_normed = tensor_sum(grad_normed_part)
    grad_latent = (grad_latent_sum * mask_float[None]).astype(half_type)
    grad_down_list = []
    grad_up_list = []
    for projection_index in range(3):
        grad_normed = grad_normed + jnp.einsum(
            "ta,da->td",
            grad_latent[projection_index],
            down_factor_rows[projection_index],
            preferred_element_type=jnp.float32,
        )
        grad_down = jnp.einsum(
            "td,ta->da", normed, grad_latent[projection_index], preferred_element_type=jnp.float32
        )
        grad_down_list.append(
            grad_down.reshape(MODEL_WIDTH, ADAPTER_CHOICES, ADAPTER_RANK).transpose(1, 0, 2)
        )
        grad_up = jnp.einsum(
            "ta,tc->ac",
            latents[projection_index],
            grad_raw[projection_index],
            preferred_element_type=jnp.float32,
        )
        grad_up_list.append(grad_up.reshape(ADAPTER_CHOICES, ADAPTER_RANK, shard_local_width))
    grad_hidden_in = grad_mixed + norm1_back(grad_normed)[0]
    grad_input = lax.dynamic_slice_in_dim(grad_hidden_in, col_start, col_width, 1)
    summed = (
        lax.psum(jnp.stack(grad_down_list).astype(jnp.bfloat16), "dp").astype(jnp.float32),
        lax.psum(jnp.stack(grad_up_list).astype(jnp.bfloat16), "dp").astype(jnp.float32),
        lax.psum(grad_down_out.astype(jnp.bfloat16), "dp").astype(jnp.float32),
        lax.psum(grad_up_out.astype(jnp.bfloat16), "dp").astype(jnp.float32),
    )
    return (layer_out, grad_input, summed[0], summed[1], summed[2], summed[3])


def solution(mesh):
    return jax.shard_map(
        local,
        mesh=mesh,
        in_specs=(
            P("dp", None),
            P("dp", "tensor"),
            P(),
            P(),
            P(),
            P(),
            P(None, "tensor"),
            P(None, "tensor"),
            P(None, "tensor"),
            P("tensor", None),
            P(),
            P(None, None, None, "tensor"),
            P(None, "tensor", None),
            P(),
            P(),
            P("dp", None, "tensor"),
            P("dp", None, "tensor"),
            P("dp", "tensor", None),
            P("dp", None),
            P("dp"),
            P("dp", None),
        ),
        out_specs=(
            P("dp", "tensor"),
            P("dp", "tensor"),
            P(),
            P(None, None, None, "tensor"),
            P(None, "tensor", None),
            P(None, None, "tensor"),
        ),
        check_vma=False,
    )
```

```python
import functools

import jax
import jax.numpy as jnp
from jax import lax
from jax.experimental import pallas as pl
from jax.experimental.pallas import tpu as pltpu
from jax.sharding import PartitionSpec as P

MODEL_WIDTH = 2048
HEAD_WIDTH = 128
TOP = 8
LEN = 512
ADAPTER_RANK = 16
ADAPTER_CHOICES = 8
QUAD = 4

norm_eps = 1e-05
head_eps = 1e-06
rope_base = 50000.0
half_type = jnp.bfloat16
VMEM_LIMIT = 56 * 1024 * 1024


def rms_scale(values, gain_vec, epsilon):
    return (
        values * lax.rsqrt(jnp.mean(values * values, axis=-1, keepdims=True) + epsilon) * gain_vec
    )


def rotate(values, positions):
    half_dim = values.shape[-1] // 2
    inverse = rope_base ** (-(jnp.arange(half_dim, dtype=jnp.float32) * 2.0 / values.shape[-1]))
    angles = positions.astype(jnp.float32)[:, None, None] * inverse[None, None, :]
    cosine = jnp.cos(angles)
    sine_val = jnp.sin(angles)
    first_half = values[..., :half_dim]
    second_half = values[..., half_dim:]
    return jnp.concatenate(
        [
            first_half * cosine - second_half * sine_val,
            second_half * cosine + first_half * sine_val,
        ],
        axis=-1,
    )


def head_prep(projected, gain_vec, positions):
    shaped = projected.reshape(projected.shape[0], projected.shape[1] // HEAD_WIDTH, HEAD_WIDTH)
    return rotate(rms_scale(shaped, gain_vec, head_eps), positions)


def nt_dot(left, right):
    return lax.dot_general(
        left, right, (((1,), (1,)), ((), ())), preferred_element_type=jnp.float32
    )


def start_blocks(pieces, buffer_ref, sems, flip):
    for b in range(QUAD):
        for r in range(2):
            pltpu.make_async_copy(
                pieces[2 * b + r], buffer_ref.at[b, r ^ flip], sems.at[b, r]
            ).start()


def wait_block(pieces, buffer_ref, sems, b):
    for r in range(2):
        pltpu.make_async_copy(pieces[0], buffer_ref.at[b, r], sems.at[b, r]).wait()


def pick_rows(place_ref, buffer_ref, rows_ref, b, experts, cap, tile):
    toks = buffer_ref.shape[2]
    slot = lax.broadcasted_iota(jnp.int32, (cap, toks), 0)
    picks = jnp.concatenate(
        [jnp.where(slot == place_ref[b, e], 1.0, 0.0) for e in range(experts)], axis=0
    ).astype(half_type)
    half = buffer_ref.shape[3]
    for h in range(2):
        for start in range(0, half, tile):
            rows = jnp.dot(
                picks,
                buffer_ref[b, h, :, start : start + tile],
                preferred_element_type=jnp.float32,
            ).astype(half_type)
            for e in range(experts):
                rows_ref[e, h, b, :, start : start + tile] = rows[e * cap : (e + 1) * cap]


def add_rows(target_ref, rows_ref, out_ref, b, flip, experts, cap, tile):
    target = target_ref[b]
    toks = target.shape[0]
    lane = lax.broadcasted_iota(jnp.int32, (toks, experts * cap), 1)
    hit = lane == target[:, 0:1]
    for e in range(1, experts):
        hit = jnp.logical_or(hit, lane == target[:, e : e + 1])
    spread = jnp.where(hit, 1.0, 0.0).astype(half_type)
    half = rows_ref.shape[4]
    for h in range(2):
        for start in range(0, half, tile):
            rows = jnp.concatenate(
                [rows_ref[e, h, b, :, start : start + tile] for e in range(experts)], axis=0
            )
            out_ref[0, h ^ flip, :, start : start + tile] = jnp.dot(
                spread, rows, preferred_element_type=jnp.float32
            ).astype(half_type)


def grad_rows_kernel(
    experts, cap, flip_ref, block_ids, place_ref, down_ref, all_ref, out_ref, buffer_ref, rows_ref, sems
):
    block_refs = [all_ref.at[block_ids[b], r] for b in range(QUAD) for r in range(2)]
    step = pl.program_id(0)
    half = buffer_ref.shape[3]

    @pl.when(step == 0)
    def _():
        start_blocks(block_refs, buffer_ref, sems, flip_ref[0])

    @pl.when(step < QUAD)
    def _():
        wait_block(block_refs, buffer_ref, sems, step)
        pick_rows(place_ref, buffer_ref, rows_ref, step, experts, cap, 512)

    @pl.when(step >= QUAD)
    def _():
        e = step - QUAD
        total = nt_dot(rows_ref[e, 0].reshape(QUAD * cap, half), down_ref[0, :, :half])
        total += nt_dot(rows_ref[e, 1].reshape(QUAD * cap, half), down_ref[0, :, half:])
        out_ref[0] = total.astype(half_type)


def expert_kernel(
    experts,
    cap,
    flip_ref,
    place_ref,
    gate_ref,
    target_ref,
    wg_ref,
    wu_ref,
    dh_ref,
    own_first_ref,
    own_second_ref,
    core_first_ref,
    core_second_ref,
    across_first_ref,
    across_second_ref,
    far_first_ref,
    far_second_ref,
    send_ref,
    keep_ref,
    hidden_ref,
    dgate_ref,
    buffer_ref,
    rows_ref,
    sems,
):
    block_refs = [
        own_first_ref,
        own_second_ref,
        core_first_ref,
        core_second_ref,
        across_first_ref,
        across_second_ref,
        far_first_ref,
        far_second_ref,
    ]
    step = pl.program_id(0)
    half = buffer_ref.shape[3]
    toks = buffer_ref.shape[2]

    @pl.when(step == 0)
    def _():
        start_blocks(block_refs, buffer_ref, sems, flip_ref[0])

    @pl.when(step < QUAD)
    def _():
        wait_block(block_refs, buffer_ref, sems, step)
        pick_rows(place_ref, buffer_ref, rows_ref, step, experts, cap, 512)

    @pl.when(jnp.logical_and(step >= QUAD, step < QUAD + experts))
    def _():
        e = step - QUAD
        first = rows_ref[e, 0].reshape(QUAD * cap, half)
        second = rows_ref[e, 1].reshape(QUAD * cap, half)
        pre_gate = jnp.dot(first, wg_ref[0, :half], preferred_element_type=jnp.float32)
        pre_gate += jnp.dot(second, wg_ref[0, half:], preferred_element_type=jnp.float32)
        pre_up = jnp.dot(first, wu_ref[0, :half], preferred_element_type=jnp.float32)
        pre_up += jnp.dot(second, wu_ref[0, half:], preferred_element_type=jnp.float32)
        sig = lax.logistic(pre_gate)
        silu = pre_gate * sig
        act = silu * pre_up
        d_raw = dh_ref[0].astype(jnp.float32)
        slot = lax.broadcasted_iota(jnp.int32, (cap, toks), 0)
        gate_parts = []
        for b in range(QUAD):
            hit = slot == place_ref[b, e]
            gate_parts.append(
                jnp.sum(jnp.where(hit, gate_ref[b, e], 0.0), axis=1, keepdims=True)
            )
        gate_col = jnp.concatenate(gate_parts, axis=0)
        hidden_ref[0] = (act * gate_col).astype(half_type)
        d_col = jnp.sum(act * d_raw, axis=1, keepdims=True)
        for b in range(QUAD):
            hit = slot == place_ref[b, e]
            dgate_ref[e, b] = jnp.sum(
                jnp.where(hit, d_col[b * cap : (b + 1) * cap], 0.0), axis=0, keepdims=True
            )
        d_hidden = d_raw * gate_col
        d_up = (d_hidden * silu).astype(half_type)
        d_gate = (d_hidden * pre_up * (sig * (1.0 + pre_gate * (1.0 - sig)))).astype(half_type)
        for h in range(2):
            d_in = nt_dot(d_gate, wg_ref[0, h * half : (h + 1) * half])
            d_in += nt_dot(d_up, wu_ref[0, h * half : (h + 1) * half])
            rows_ref[e, h] = d_in.astype(half_type).reshape(QUAD, cap, half)

    for which, out_ref in ((0, send_ref), (1, keep_ref)):
        first_step = QUAD + experts + 2 * which

        @pl.when(jnp.logical_and(step >= first_step, step < first_step + 2))
        def _():
            b = 2 * (step - first_step) + 1 - which
            add_rows(target_ref, rows_ref, out_ref, b, flip_ref[0], experts, cap, 512)


def output_kernel(experts, cap, flip_ref, target_ref, down_ref, hidden_ref, send_ref, keep_ref, rows_ref):
    step = pl.program_id(0)
    half = rows_ref.shape[4]

    @pl.when(step < experts)
    def _():
        for h in range(2):
            out = jnp.dot(
                hidden_ref[0],
                down_ref[0, :, h * half : (h + 1) * half],
                preferred_element_type=jnp.float32,
            )
            rows_ref[step, h] = out.astype(half_type).reshape(QUAD, cap, half)

    for which, out_ref in ((0, send_ref), (1, keep_ref)):
        first_step = experts + 2 * which

        @pl.when(jnp.logical_and(step >= first_step, step < first_step + 2))
        def _():
            b = 2 * (step - first_step) + 1 - which
            add_rows(target_ref, rows_ref, out_ref, b, flip_ref[0], experts, cap, 512)


def whole(shape):
    return pl.BlockSpec(shape, lambda i, *_: (0,) * len(shape), pipeline_mode=pl.Buffered(1))


def per_step(shape, first, count):
    return pl.BlockSpec(
        (1,) + shape[1:], lambda i, *_: (jnp.clip(i - first, 0, count - 1),) + (0,) * (len(shape) - 1)
    )


def block_scratch(toks, half, experts, cap, with_buffer):
    rows = pltpu.VMEM((experts, 2, QUAD, cap, half), half_type)
    if not with_buffer:
        return [rows]
    return [
        pltpu.VMEM((QUAD, 2, toks, half), half_type),
        rows,
        pltpu.SemaphoreType.DMA((QUAD, 2)),
    ]


def call_grad_rows(flip, block_ids, place, down, blocks, cap):
    experts, hidden_units, width = down.shape
    toks, half = blocks.shape[2:]
    rows = QUAD * cap
    return pl.pallas_call(
        functools.partial(grad_rows_kernel, experts, cap),
        out_shape=jax.ShapeDtypeStruct((experts, rows, hidden_units), half_type),
        grid_spec=pltpu.PrefetchScalarGridSpec(
            num_scalar_prefetch=2,
            grid=(QUAD + experts,),
            in_specs=[
                whole(place.shape),
                per_step(down.shape, QUAD, experts),
                pl.BlockSpec(memory_space=pl.ANY),
            ],
            out_specs=per_step((experts, rows, hidden_units), QUAD, experts),
            scratch_shapes=block_scratch(toks, half, experts, cap, True),
        ),
        compiler_params=pltpu.CompilerParams(
            dimension_semantics=("arbitrary",), vmem_limit_bytes=VMEM_LIMIT
        ),
        cost_estimate=pl.CostEstimate(flops=1, bytes_accessed=1, transcendentals=0),
        name="grad_rows",
    )(flip, block_ids, place, down, blocks)


def call_experts(flip, place, gate, target, gate_w, up_w, d_raw, pieces, cap):
    experts, width, hidden_units = gate_w.shape
    toks, half = pieces[0].shape
    rows = QUAD * cap
    blocks = (2, 2, toks, half)
    return pl.pallas_call(
        functools.partial(expert_kernel, experts, cap),
        out_shape=(
            jax.ShapeDtypeStruct(blocks, half_type),
            jax.ShapeDtypeStruct(blocks, half_type),
            jax.ShapeDtypeStruct((experts, rows, hidden_units), half_type),
            jax.ShapeDtypeStruct((experts, QUAD, 1, toks), jnp.float32),
        ),
        grid_spec=pltpu.PrefetchScalarGridSpec(
            num_scalar_prefetch=1,
            grid=(2 * QUAD + experts,),
            in_specs=[
                whole(place.shape),
                whole(gate.shape),
                whole(target.shape),
                per_step(gate_w.shape, QUAD, experts),
                per_step(up_w.shape, QUAD, experts),
                per_step(d_raw.shape, QUAD, experts),
            ]
            + [pl.BlockSpec(memory_space=pl.ANY)] * len(pieces),
            out_specs=(
                per_step(blocks, QUAD + experts, 2),
                per_step(blocks, QUAD + experts + 2, 2),
                per_step((experts, rows, hidden_units), QUAD, experts),
                whole((experts, QUAD, 1, toks)),
            ),
            scratch_shapes=block_scratch(toks, half, experts, cap, True),
        ),
        compiler_params=pltpu.CompilerParams(
            dimension_semantics=("arbitrary",), vmem_limit_bytes=VMEM_LIMIT
        ),
        cost_estimate=pl.CostEstimate(flops=1, bytes_accessed=1, transcendentals=0),
        name="experts",
    )(flip, place, gate, target, gate_w, up_w, d_raw, *pieces)


def call_output(flip, target, down, hidden, cap, half):
    experts, hidden_units, width = down.shape
    toks = target.shape[1]
    rows = QUAD * cap
    blocks = (2, 2, toks, half)
    return pl.pallas_call(
        functools.partial(output_kernel, experts, cap),
        out_shape=(
            jax.ShapeDtypeStruct(blocks, half_type),
            jax.ShapeDtypeStruct(blocks, half_type),
        ),
        grid_spec=pltpu.PrefetchScalarGridSpec(
            num_scalar_prefetch=1,
            grid=(QUAD + experts,),
            in_specs=[
                whole(target.shape),
                per_step(down.shape, 0, experts),
                per_step(hidden.shape, 0, experts),
            ],
            out_specs=(per_step(blocks, experts, 2), per_step(blocks, experts + 2, 2)),
            scratch_shapes=block_scratch(toks, half, experts, cap, False),
        ),
        compiler_params=pltpu.CompilerParams(
            dimension_semantics=("arbitrary",), vmem_limit_bytes=VMEM_LIMIT
        ),
        cost_estimate=pl.CostEstimate(
            flops=4 * experts * rows * width * (toks + hidden_units),
            bytes_accessed=2 * (down.size + 2 * QUAD * toks * half),
            transcendentals=0,
        ),
        name="outputs",
    )(flip, target, down, hidden)


def swap(values, data_count, bit):
    return lax.ppermute(values, "dp", [(i, i ^ bit) for i in range(data_count)])


def onward(values, data_count):
    return lax.ppermute(values, "dp", [(i, (i + QUAD) % data_count) for i in range(data_count)])


def other_side(values):
    return lax.ppermute(values, "tensor", [(0, 1), (1, 0)])


def fence(*values):
    return lax.optimization_barrier(values)


def plus(*terms):
    total = terms[0].astype(jnp.float32)
    for term in terms[1:]:
        total = total + term.astype(jnp.float32)
    return total.astype(half_type)


def local(
    layer_input,
    cotangent,
    attention_norm_gain,
    expert_norm_gain,
    query_norm_gain,
    key_norm_gain,
    query_weight_matrix,
    key_weight_matrix,
    value_weight_matrix,
    output_weight_matrix,
    adapter_projection_down,
    adapter_projection_up,
    adapter_output_down,
    adapter_output_up,
    router,
    expert_gate_weight,
    expert_up_weight,
    expert_down_weight,
    segments,
    sequence_adapter_index,
    routes,
):
    tok_count = layer_input.shape[0]
    tensor_count = lax.axis_size("tensor")
    data_count = lax.axis_size("dp")
    pair = tensor_count == 2
    ring_count = data_count // QUAD
    col_width = MODEL_WIDTH // tensor_count
    half_width = MODEL_WIDTH // 2
    side = lax.axis_index("tensor")
    col_start = side * col_width
    place_dp = lax.axis_index("dp")
    flip = side.astype(jnp.int32) if pair else jnp.int32(0)
    flip_arr = flip.reshape(1)
    shard_local_width = query_weight_matrix.shape[1]
    local_heads = shard_local_width // HEAD_WIDTH
    local_experts = expert_gate_weight.shape[0]
    expert_total = local_experts * data_count
    capacity = 5 * tok_count * TOP // (4 * expert_total)
    score_scale = HEAD_WIDTH ** (-0.5)
    token_ids = jnp.arange(tok_count, dtype=jnp.int32)
    positions = token_ids % LEN

    def to_sides(full):
        if pair:
            low_cols, high_cols = full[:, :half_width], full[:, half_width:]
            return (
                jnp.where(flip == 0, low_cols, high_cols),
                jnp.where(flip == 0, high_cols, low_cols),
            )
        return full[:, :half_width], full[:, half_width:]

    def from_sides(first, second):
        if pair:
            return jnp.concatenate(
                [jnp.where(flip == 0, first, second), jnp.where(flip == 0, second, first)], axis=1
            )
        return jnp.concatenate([first, second], axis=1)

    routes_t = routes.T
    expert_ids = jnp.arange(expert_total, dtype=jnp.int32)
    chosen_mask = jnp.any(routes_t[:, None, :] == expert_ids[None, :, None], axis=0)
    earlier = (token_ids[:, None] < token_ids[None, :]).astype(half_type)
    rank = jnp.dot(chosen_mask.astype(half_type), earlier, preferred_element_type=jnp.float32)
    place_own = jnp.where(chosen_mask, rank, -1.0).astype(jnp.int32)
    place_all = lax.all_to_all(
        place_own.reshape(data_count, local_experts, tok_count), "dp", 0, 0, tiled=True
    )
    ring_at, quad_at = place_dp // QUAD, place_dp % QUAD
    group_ids = jnp.arange(data_count, dtype=jnp.int32)
    order = ((ring_at - group_ids // QUAD) % ring_count) * QUAD + (quad_at ^ (group_ids % QUAD))
    place_all = place_all[order]
    target_all = jnp.where(
        place_all >= 0,
        place_all + capacity * jnp.arange(local_experts, dtype=jnp.int32)[None, :, None],
        -1,
    ).transpose(0, 2, 1)

    def group_of(values, j):
        return values[j * QUAD : (j + 1) * QUAD]

    if pair:
        g_first = cotangent
        g_second = other_side(cotangent)
    else:
        g_full = lax.all_gather(cotangent, "tensor", axis=1, tiled=True)
        g_first, g_second = g_full[:, :half_width], g_full[:, half_width:]
    adapter = sequence_adapter_index[0]

    def own_adapter(factors, axis):
        return lax.dynamic_index_in_dim(factors, adapter, axis, keepdims=False)

    down_rows = own_adapter(adapter_projection_down.transpose(0, 1, 3, 2), 1)
    down_rows = down_rows.reshape(3 * ADAPTER_RANK, MODEL_WIDTH)
    up_rows = own_adapter(adapter_projection_up, 1)
    out_down_rows = own_adapter(adapter_output_down.transpose(0, 2, 1), 0)
    out_up_rows = own_adapter(adapter_output_up, 0)
    doc_flat = segments.reshape(-1)
    hidden32 = layer_input.astype(jnp.float32)
    hidden_scale = lax.rsqrt(
        jnp.mean(hidden32 * hidden32, axis=-1, keepdims=True) + norm_eps
    )
    normed = (hidden32 * hidden_scale * attention_norm_gain).astype(half_type)
    w_proj = [query_weight_matrix, key_weight_matrix, value_weight_matrix]
    latents = nt_dot(normed, down_rows).astype(half_type)
    latents = [latents[:, p * ADAPTER_RANK : (p + 1) * ADAPTER_RANK] for p in range(3)]
    raw_proj = [
        jnp.dot(normed, w_proj[p], preferred_element_type=jnp.float32)
        + jnp.dot(latents[p], up_rows[p], preferred_element_type=jnp.float32)
        for p in range(3)
    ]
    g_blocks, raw_proj[2] = fence(jnp.stack([g_first, g_second]), raw_proj[2])
    g_all = lax.all_gather(g_blocks, "dp", axis=0)
    query_f, query_back = jax.vjp(
        lambda projected: head_prep(projected, query_norm_gain, positions), raw_proj[0]
    )
    key_f, key_back = jax.vjp(
        lambda projected: head_prep(projected, key_norm_gain, positions), raw_proj[1]
    )
    queries, place_all, target_all = lax.optimization_barrier(
        (query_f.astype(half_type), place_all, target_all)
    )
    keys = key_f.astype(half_type)
    values = raw_proj[2].reshape(tok_count, local_heads, HEAD_WIDTH).astype(half_type)

    same_doc = (doc_flat[:, None] == doc_flat[None, :])[None]

    def block_scores():
        scores = (
            jnp.einsum("qhd,khd->hqk", queries, keys, preferred_element_type=jnp.float32)
            * score_scale
        )
        return jnp.where(same_doc, scores, -1e30)

    scores = block_scores()
    top_score = jnp.max(scores, axis=-1, keepdims=True)
    exp_scores = jnp.exp(scores - top_score)
    row_total = jnp.sum(exp_scores, axis=-1, keepdims=True)
    prob_half = (exp_scores / row_total).astype(half_type)
    attended = jnp.einsum("hqk,khd->qhd", prob_half, values, preferred_element_type=jnp.float32)
    log_totals = top_score[..., 0] + jnp.log(row_total[..., 0])
    attended = attended.reshape(tok_count, shard_local_width).astype(half_type)
    proj_part = jnp.dot(attended, output_weight_matrix, preferred_element_type=jnp.float32)
    latent_part = nt_dot(attended, out_down_rows)

    def tensor_sum(part):
        if pair:
            return part.astype(jnp.float32) + other_side(part).astype(jnp.float32)
        return lax.psum(part, "tensor").astype(jnp.float32)

    def own_columns(part):
        if pair:
            first, second = to_sides(part)
            return first.astype(jnp.float32) + other_side(second.astype(half_type)).astype(
                jnp.float32
            )
        return lax.psum_scatter(
            part.astype(half_type), "tensor", scatter_dimension=1, tiled=True
        ).astype(jnp.float32)

    def columns_of(full):
        if pair:
            return to_sides(full)[0]
        return lax.dynamic_slice_in_dim(full, col_start, col_width, full.ndim - 1)

    def both_halves(cols):
        if pair:
            return cols, other_side(cols)
        full = lax.all_gather(cols, "tensor", axis=1, tiled=True)
        return full[:, :half_width], full[:, half_width:]

    attn_cols = own_columns(proj_part)
    latent_total = tensor_sum(latent_part.astype(half_type))
    latent_out = latent_total.astype(half_type)
    mixed_cols = (
        columns_of(layer_input).astype(jnp.float32)
        + attn_cols
        + jnp.dot(latent_out, columns_of(out_up_rows), preferred_element_type=jnp.float32)
    )
    expert_gain_cols = columns_of(expert_norm_gain[None, :])
    square_sum = tensor_sum(jnp.sum(mixed_cols * mixed_cols, axis=1, keepdims=True))
    mixed_scale = lax.rsqrt(square_sum / MODEL_WIDTH + norm_eps)
    moe_cols_in = (mixed_cols * mixed_scale * expert_gain_cols).astype(half_type)

    def gates_of(first, second):
        moe_in = from_sides(first, second)
        logits_t = lax.dot_general(
            router, moe_in, (((0,), (1,)), ((), ())), preferred_element_type=jnp.float32
        )
        top_logit = jnp.max(jnp.where(chosen_mask, logits_t, -jnp.inf), axis=0, keepdims=True)
        gate_exp = jnp.where(chosen_mask, jnp.exp(jnp.minimum(logits_t - top_logit, 0.0)), 0.0)
        return gate_exp / jnp.sum(gate_exp, axis=0, keepdims=True)

    def grad_rows_of(k, places):
        return call_grad_rows(
            flip_arr,
            group_of(order, k),
            group_of(places, k)[:, :, None, :],
            expert_down_weight,
            g_all,
            capacity,
        )

    def experts_of(k, d_raw, pieces):
        return call_experts(
            flip_arr,
            group_of(place_all, k)[:, :, None, :],
            group_of(gates_all, k)[:, :, None, :],
            group_of(target_all, k),
            expert_gate_weight,
            expert_up_weight,
            d_raw,
            pieces,
            capacity,
        )

    def outputs_of(k, hidden):
        return call_output(
            flip_arr,
            group_of(target_all, k),
            expert_down_weight,
            hidden,
            capacity,
            half_width,
        )

    quads = ring_count
    own0, own1, core0, core1 = ([None] * quads for _ in range(4))
    af, asec, ff, fs = ([None] * quads for _ in range(4))
    d_raw = [None] * quads
    send, keep, hidden, d_gate = ([None] * quads for _ in range(4))
    got, near, side_got, sums = ([None] * quads for _ in range(4))
    work_order = [(i + 1) % quads for i in range(quads)]
    sides_by_tensor = [pair and j != quads - 1 for j in range(quads)]
    places = place_all

    def move_first(j):
        own0[j + 1] = onward(own0[j], data_count)

    def move_second(j):
        own1[j + 1] = onward(own1[j], data_count)

    def send_across(j):
        af[j] = swap(own0[j], data_count, 2)
        core0[j] = swap(own0[j], data_count, 1)

    def send_rest(j):
        asec[j] = other_side(af[j]) if sides_by_tensor[j] else swap(own1[j], data_count, 2)
        core1[j] = swap(own1[j], data_count, 1)
        ff[j] = swap(af[j], data_count, 1)

    def send_last(j):
        fs[j] = swap(asec[j], data_count, 1)

    def run_experts(k):
        pieces = [own0[k], own1[k], core0[k], core1[k], af[k], asec[k], ff[k], fs[k]]
        send[k], keep[k], hidden[k], d_gate[k] = experts_of(k, d_raw[k], pieces)

    def sum_cores(k):
        got[k] = swap(send[k], data_count, 1)

    def sum_sides(k):
        if pair:
            near[k] = plus(keep[k][1, 0], got[k][1, 0])
            side_got[k] = other_side(plus(keep[k][1, 1], got[k][1, 1]))
        else:
            near[k] = plus(keep[k][1], got[k][1])

    def sum_across(k):
        if pair:
            arrived = swap(plus(near[k], side_got[k]), data_count, 2)
            first = plus(keep[k][0, 0], got[k][0, 0], arrived)
            sums[k] = jnp.stack([first, plus(keep[k][0, 1], got[k][0, 1])])
        else:
            sums[k] = plus(keep[k][0], got[k][0], swap(near[k], data_count, 2))

    def step_end(*more):
        groups = (
            own0, own1, core0, core1, af, asec, ff, fs, d_raw,
            send, keep, hidden, d_gate, got, near, side_got, sums,
        )
        fenced = fence(groups, more)
        for old, fresh in zip(groups, fenced[0]):
            old[:] = fresh
        return fenced[1]

    own0[0] = moe_cols_in if pair else both_halves(moe_cols_in)[0]
    own1[0] = both_halves(moe_cols_in)[1]
    move_first(0)
    send_across(0)
    step_end()
    gates_t = gates_of(own0[0], own1[0])
    move_second(0)
    send_rest(0)
    send_across(1)
    (gates_t,) = step_end(gates_t)
    gates_all = lax.all_gather(gates_t.reshape(data_count, local_experts, tok_count), "dp", axis=0)
    gates_all = lax.dynamic_index_in_dim(gates_all, place_dp, 1, keepdims=False)[order]
    move_first(1)
    send_rest(1)
    send_last(0)
    step_end()
    move_second(1)
    send_across(2)
    send_last(1)
    d_raw[1], d_raw[2] = grad_rows_of(1, places), grad_rows_of(2, places)
    (places,) = step_end(places)
    move_first(2)
    send_rest(2)
    run_experts(1)
    step_end()
    move_second(2)
    send_across(3)
    send_last(2)
    sum_cores(1)
    run_experts(2)
    step_end()
    send_rest(3)
    sum_sides(1)
    sum_cores(2)
    d_raw[3], d_raw[0] = grad_rows_of(3, places), grad_rows_of(0, places)
    step_end()
    send_last(3)
    sum_across(1)
    sum_sides(2)
    run_experts(3)
    step_end()
    total = onward(sums[1], data_count)
    sum_across(2)
    sum_cores(3)
    run_experts(0)
    (total,) = step_end(plus(total, sums[2]))
    out_send, out_keep, out_got, out_sums = ([None] * quads for _ in range(4))

    def out_near(k):
        return plus(out_keep[k][1], out_got[k][1])

    def out_sum(k, arrived):
        return plus(out_keep[k][0], out_got[k][0], arrived)

    passed = onward(total, data_count)
    sum_sides(3)
    sum_cores(0)
    out_send[1], out_keep[1] = outputs_of(1, hidden[1])
    out_send[2], out_keep[2] = outputs_of(2, hidden[2])
    out_send, out_keep = step_end(out_send, out_keep)
    sum_across(3)
    sum_sides(0)
    out_got[1] = swap(out_send[1], data_count, 1)
    out_got[2] = swap(out_send[2], data_count, 1)
    out_send[3], out_keep[3] = outputs_of(3, hidden[3])
    out_send[0], out_keep[0] = outputs_of(0, hidden[0])
    d_gate_all = jnp.concatenate([values[:, :, 0, :].transpose(1, 0, 2) for values in d_gate], axis=0)
    d_gate_all = lax.all_gather(d_gate_all, "dp", axis=0)
    total, out_send, out_keep, out_got = step_end(
        plus(passed, sums[3]), out_send, out_keep, out_got
    )
    passed = onward(total, data_count)
    sum_across(0)
    out_across = swap(out_near(1), data_count, 2)
    out_got[3] = swap(out_send[3], data_count, 1)
    out_got[0] = swap(out_send[0], data_count, 1)
    sender = jnp.arange(data_count, dtype=jnp.int32)
    mine = ((sender // QUAD - ring_at) % ring_count) * QUAD + ((sender % QUAD) ^ quad_at)
    d_gate_home = jnp.take_along_axis(d_gate_all, mine[:, None, None, None], axis=1)
    d_gate_home = d_gate_home.reshape(expert_total, tok_count)
    total, out_keep, out_got, out_across, d_gate_home = step_end(
        plus(passed, sums[0]), out_keep, out_got, out_across, d_gate_home
    )
    d_gate_home = tensor_sum(d_gate_home)
    if pair:
        grad_moe_cols = total[0].astype(jnp.float32) + other_side(total[1]).astype(jnp.float32)
    else:
        grad_moe_cols = own_columns(from_sides(total[0], total[1]))
    out_passed = onward(out_sum(1, out_across), data_count)
    out_next = swap(out_near(2), data_count, 2)
    d_gate_home, grad_moe_cols, out_got, out_keep = step_end(
        d_gate_home, grad_moe_cols, out_got, out_keep
    )

    weighted = gates_t * d_gate_home
    grad_logits_t = (
        gates_t * (d_gate_home - jnp.sum(weighted, axis=0, keepdims=True))
    ).astype(half_type)
    router_cols = router.T
    grad_moe_cols = grad_moe_cols + lax.dot_general(
        grad_logits_t,
        columns_of(router_cols),
        (((0,), (0,)), ((), ())),
        preferred_element_type=jnp.float32,
    )
    along = tensor_sum(
        jnp.sum(mixed_cols * expert_gain_cols * grad_moe_cols, axis=1, keepdims=True)
    )
    grad_mixed_cols = (
        cotangent.astype(jnp.float32)
        + expert_gain_cols * mixed_scale * grad_moe_cols
        - mixed_cols * (mixed_scale * mixed_scale * mixed_scale * (along / MODEL_WIDTH))
    )
    branch_cols = grad_mixed_cols.astype(half_type)
    grad_branch = from_sides(*both_halves(branch_cols))
    out_total = plus(out_passed, out_sum(2, out_next))
    grad_branch, out_total, out_got, out_keep = fence(grad_branch, out_total, out_got, out_keep)

    out_passed = onward(out_total, data_count)
    out_third = swap(out_near(3), data_count, 2)

    grad_latent_out = nt_dot(grad_branch, out_up_rows).astype(half_type)
    grad_up_out = lax.dot_general(
        latent_out, branch_cols, (((0,), (0,)), ((), ())), preferred_element_type=jnp.float32
    )
    grad_attended = nt_dot(grad_branch, output_weight_matrix) + jnp.dot(
        grad_latent_out, out_down_rows, preferred_element_type=jnp.float32
    )
    grad_heads = grad_attended.astype(half_type).reshape(tok_count, local_heads, HEAD_WIDTH)
    grad_down_out = lax.dot_general(
        grad_latent_out, attended, (((0,), (0,)), ((), ())), preferred_element_type=jnp.float32
    )

    prob_block = jnp.where(same_doc, jnp.exp(block_scores() - log_totals[:, :, None]), 0.0)
    grad_prob = jnp.einsum("qhd,khd->hqk", grad_heads, values, preferred_element_type=jnp.float32)
    row_delta = jnp.sum(prob_block * grad_prob, axis=-1, keepdims=True)
    grad_scores = (prob_block * (grad_prob - row_delta)).astype(half_type)
    out_total = plus(out_passed, out_sum(3, out_third))
    grad_scores, out_total = fence(grad_scores, out_total)
    out_passed = onward(out_total, data_count)
    out_fourth = swap(out_near(0), data_count, 2)
    grad_queries = (
        jnp.einsum("hqk,khd->qhd", grad_scores, keys, preferred_element_type=jnp.float32)
        * score_scale
    )
    grad_keys = (
        jnp.einsum("hqk,qhd->khd", grad_scores, queries, preferred_element_type=jnp.float32)
        * score_scale
    )
    grad_values = jnp.einsum(
        "hqk,qhd->khd",
        prob_block.astype(half_type),
        grad_heads,
        preferred_element_type=jnp.float32,
    ).reshape(tok_count, shard_local_width)
    grad_raw = [
        query_back(grad_queries)[0].astype(half_type),
        key_back(grad_keys)[0].astype(half_type),
        grad_values.astype(half_type),
    ]
    latent_parts = jnp.concatenate([nt_dot(grad_raw[p], up_rows[p]) for p in range(3)], axis=1)
    grad_latent = tensor_sum(latent_parts.astype(half_type)).astype(half_type)
    grad_up = [
        lax.dot_general(
            latents[p], grad_raw[p], (((0,), (0,)), ((), ())), preferred_element_type=jnp.float32
        )
        for p in range(3)
    ]
    grad_down = lax.dot_general(
        grad_latent, normed, (((0,), (0,)), ((), ())), preferred_element_type=jnp.float32
    )
    number = jnp.full((ADAPTER_RANK, shard_local_width), adapter.astype(half_type))
    first_part = jnp.concatenate(
        [grad_down_out.astype(half_type), grad_up_out.astype(half_type), number]
        + [part.astype(half_type) for part in grad_up],
        axis=0,
    )
    second_part = grad_down.astype(half_type)
    first_part, second_part = fence(first_part, second_part)
    first_all = lax.all_gather(first_part, "dp", axis=0)
    second_all = lax.all_gather(second_part, "dp", axis=0)
    numbers = first_all[:, 2 * ADAPTER_RANK, 0].astype(jnp.float32)
    holds = numbers[None, :] == jnp.arange(ADAPTER_CHOICES, dtype=jnp.float32)[:, None]
    holds = holds.astype(half_type)

    def by_adapter(parts):
        return jnp.einsum("as,src->arc", holds, parts, preferred_element_type=jnp.float32)

    first_sum = by_adapter(first_all)
    second_sum = by_adapter(second_all)

    def rows_at(i):
        return first_sum[:, i * ADAPTER_RANK : (i + 1) * ADAPTER_RANK]

    sum_down_qkv = jnp.stack(
        [second_sum[:, p * ADAPTER_RANK : (p + 1) * ADAPTER_RANK] for p in range(3)]
    ).transpose(0, 1, 3, 2)
    sum_up_qkv = jnp.stack([rows_at(3 + p) for p in range(3)])

    grad_normed_part = nt_dot(grad_raw[0], w_proj[0])
    grad_normed_part += nt_dot(grad_raw[1], w_proj[1])
    grad_normed_part += nt_dot(grad_raw[2], w_proj[2])
    grad_normed_cols = own_columns(grad_normed_part)
    out_total = plus(out_passed, out_sum(0, out_fourth))
    grad_normed_cols, out_total = fence(grad_normed_cols, out_total)
    if pair:
        moe_cols = out_total[0].astype(jnp.float32) + other_side(out_total[1]).astype(jnp.float32)
    else:
        moe_cols = own_columns(from_sides(out_total[0], out_total[1]))
    layer_out = (mixed_cols + moe_cols).astype(half_type)
    grad_normed_cols += jnp.dot(
        grad_latent, columns_of(down_rows), preferred_element_type=jnp.float32
    )
    attention_gain_cols = columns_of(attention_norm_gain[None, :])
    hidden_cols = columns_of(layer_input).astype(jnp.float32)
    along_in = tensor_sum(
        jnp.sum(hidden_cols * attention_gain_cols * grad_normed_cols, axis=1, keepdims=True)
    )
    grad_input = (
        grad_mixed_cols
        + attention_gain_cols * hidden_scale * grad_normed_cols
        - hidden_cols * (hidden_scale * hidden_scale * hidden_scale * (along_in / MODEL_WIDTH))
    )
    return (
        layer_out,
        grad_input,
        sum_down_qkv,
        sum_up_qkv,
        rows_at(0).transpose(0, 2, 1),
        rows_at(1),
    )


def solution(mesh):
    return jax.shard_map(
        local,
        mesh=mesh,
        in_specs=(
            P("dp", None),
            P("dp", "tensor"),
            P(),
            P(),
            P(),
            P(),
            P(None, "tensor"),
            P(None, "tensor"),
            P(None, "tensor"),
            P("tensor", None),
            P(),
            P(None, None, None, "tensor"),
            P(None, "tensor", None),
            P(),
            P(),
            P("dp", None, "tensor"),
            P("dp", None, "tensor"),
            P("dp", "tensor", None),
            P("dp", None),
            P("dp"),
            P("dp", None),
        ),
        out_specs=(
            P("dp", "tensor"),
            P("dp", "tensor"),
            P(),
            P(None, None, None, "tensor"),
            P(None, "tensor", None),
            P(None, None, "tensor"),
        ),
        check_vma=False,
    )
```

```python
import functools

import jax
import jax.numpy as jnp
from jax import lax
from jax.experimental import pallas as pl
from jax.experimental.pallas import tpu as pltpu
from jax.sharding import PartitionSpec as P

MODEL_WIDTH = 2048
HEAD_WIDTH = 128
TOP = 8
LEN = 512
ADAPTER_RANK = 16
ADAPTER_CHOICES = 8
QUAD = 4

norm_eps = 1e-05
head_eps = 1e-06
rope_base = 50000.0
half_type = jnp.bfloat16
VMEM_LIMIT = 56 * 1024 * 1024


def rotation(positions):
    half_dim = HEAD_WIDTH // 2
    inverse = rope_base ** (-(jnp.arange(half_dim, dtype=jnp.float32) * 2.0 / HEAD_WIDTH))
    angles = positions.astype(jnp.float32)[:, None] * inverse[None, :]
    cosine, sine = jnp.cos(angles), jnp.sin(angles)
    return (
        jnp.concatenate([cosine, cosine], axis=1),
        jnp.concatenate([-sine, sine], axis=1),
    )


def nt_dot(left, right):
    return lax.dot_general(
        left, right, (((1,), (1,)), ((), ())), preferred_element_type=jnp.float32
    )


def tn_dot(left, right):
    return lax.dot_general(
        left, right, (((0,), (0,)), ((), ())), preferred_element_type=jnp.float32
    )


def head_prep(raw, gain, cosine, sine):
    scale = lax.rsqrt(jnp.mean(raw * raw, axis=-1, keepdims=True) + head_eps)
    scaled = raw * scale * gain
    return scaled * cosine + pltpu.roll(scaled, HEAD_WIDTH // 2, 1) * sine


def head_prep_back(grad, raw, gain, cosine, sine):
    scale = lax.rsqrt(jnp.mean(raw * raw, axis=-1, keepdims=True) + head_eps)
    turned = (grad * cosine - pltpu.roll(grad, HEAD_WIDTH // 2, 1) * sine) * gain
    along = jnp.mean(raw * turned, axis=-1, keepdims=True)
    return scale * turned - raw * (scale * scale * scale * along)


def masked_exp(queries, keys, docs_col, docs_row):
    scores = nt_dot(queries, keys) * HEAD_WIDTH ** (-0.5)
    scores = jnp.where(docs_col == docs_row, scores, -1e30)
    exp_scores = jnp.exp(scores - jnp.max(scores, axis=-1, keepdims=True))
    return exp_scores, jnp.sum(exp_scores, axis=-1, keepdims=True)


def attend_kernel(
    raw_q, raw_k, raw_v, cosine, sine, gain_q, gain_k, docs_col, docs_row, out, queries, keys, values
):
    q = head_prep(raw_q[...], gain_q[...], cosine[...], sine[...]).astype(half_type)
    k = head_prep(raw_k[...], gain_k[...], cosine[...], sine[...]).astype(half_type)
    v = raw_v[...].astype(half_type)
    queries[...], keys[...], values[...] = q, k, v
    exp_scores, total = masked_exp(q, k, docs_col[...], docs_row[...])
    probs = (exp_scores / total).astype(half_type)
    out[...] = jnp.dot(probs, v, preferred_element_type=jnp.float32).astype(half_type)


def attend_back_kernel(
    raw_q, raw_k, queries, keys, values, grad, cosine, sine, gain_q, gain_k, docs_col, docs_row,
    grad_q, grad_k, grad_v,
):
    q, k, v, g = queries[...], keys[...], values[...], grad[...]
    score_scale = HEAD_WIDTH ** (-0.5)
    exp_scores, total = masked_exp(q, k, docs_col[...], docs_row[...])
    probs = exp_scores / total
    grad_v[...] = tn_dot(probs.astype(half_type), g).astype(half_type)
    grad_probs = nt_dot(g, v)
    delta = jnp.sum(probs * grad_probs, axis=-1, keepdims=True)
    grad_scores = (probs * (grad_probs - delta)).astype(half_type)
    d_q = jnp.dot(grad_scores, k, preferred_element_type=jnp.float32) * score_scale
    d_k = tn_dot(grad_scores, q) * score_scale
    grad_q[...] = head_prep_back(d_q, raw_q[...], gain_q[...], cosine[...], sine[...]).astype(
        half_type
    )
    grad_k[...] = head_prep_back(d_k, raw_k[...], gain_k[...], cosine[...], sine[...]).astype(
        half_type
    )


def call_heads(kernel, name, by_head, shared, out_count):
    toks, width = by_head[0].shape
    head = pl.BlockSpec((toks, HEAD_WIDTH), lambda h: (0, h))
    return pl.pallas_call(
        kernel,
        out_shape=[jax.ShapeDtypeStruct((toks, width), half_type)] * out_count,
        grid=(width // HEAD_WIDTH,),
        in_specs=[head] * len(by_head)
        + [pl.BlockSpec(v.shape, lambda h: (0, 0)) for v in shared],
        out_specs=[head] * out_count,
        compiler_params=pltpu.CompilerParams(
            dimension_semantics=("arbitrary",), vmem_limit_bytes=VMEM_LIMIT
        ),
        cost_estimate=pl.CostEstimate(
            flops=10 * toks * toks * width, bytes_accessed=8 * toks * width, transcendentals=toks * toks
        ),
        name=name,
    )(*by_head, *shared)


def start_blocks(pieces, buffer_ref, sems, flip):
    for b in range(QUAD):
        for r in range(2):
            pltpu.make_async_copy(
                pieces[2 * b + r], buffer_ref.at[b, r ^ flip], sems.at[b, r]
            ).start()


def wait_block(pieces, buffer_ref, sems, b):
    for r in range(2):
        pltpu.make_async_copy(pieces[0], buffer_ref.at[b, r], sems.at[b, r]).wait()


def pick_rows(place_ref, half_at, rows_ref, b, experts, cap, tile):
    toks = half_at(0).shape[0]
    slot = lax.broadcasted_iota(jnp.int32, (cap, toks), 0)
    picks = jnp.concatenate(
        [jnp.where(slot == place_ref[b, e], 1.0, 0.0) for e in range(experts)], axis=0
    ).astype(half_type)
    half = rows_ref.shape[4]
    for h in range(rows_ref.shape[1]):
        for start in range(0, half, tile):
            rows = jnp.dot(
                picks,
                half_at(h)[:, start : start + tile],
                preferred_element_type=jnp.float32,
            ).astype(half_type)
            for e in range(experts):
                rows_ref[e, h, b, :, start : start + tile] = rows[e * cap : (e + 1) * cap]


def add_rows(target_ref, rows_ref, out_ref, b, flip, experts, cap, tile):
    target = target_ref[b]
    toks = target.shape[0]
    lane = lax.broadcasted_iota(jnp.int32, (toks, experts * cap), 1)
    hit = lane == target[:, 0:1]
    for e in range(1, experts):
        hit = jnp.logical_or(hit, lane == target[:, e : e + 1])
    spread = jnp.where(hit, 1.0, 0.0).astype(half_type)
    half = rows_ref.shape[4]
    for h in range(2):
        for start in range(0, half, tile):
            rows = jnp.concatenate(
                [rows_ref[e, h, b, :, start : start + tile] for e in range(experts)], axis=0
            )
            out_ref[0, h ^ flip, :toks, start : start + tile] = jnp.dot(
                spread, rows, preferred_element_type=jnp.float32
            ).astype(half_type)


def add_gates(dgate_ref, out_ref, b, device, experts):
    toks, half = dgate_ref.shape[3], out_ref.shape[3]
    extra = out_ref.shape[2] - toks
    per_row = half // toks
    row = lax.broadcasted_iota(jnp.int32, (extra, half), 0)
    values = jnp.zeros((extra, half), jnp.float32)
    for i in range(experts // per_row):
        line = jnp.concatenate(
            [dgate_ref[i * per_row + n, b] for n in range(per_row)], axis=1
        )
        values = jnp.where(row == device * (experts // per_row) + i, line, values)
    for h in range(2):
        out_ref[0, h, toks:, :] = values.astype(half_type)


def grad_rows_kernel(experts, cap, block_ids, place_ref, down_ref, block_ref, out_ref, rows_ref):
    step = pl.program_id(0)
    sides, blocks, part = rows_ref.shape[1], rows_ref.shape[2], rows_ref.shape[4]

    @pl.when(step < blocks)
    def _():
        pick_rows(
            place_ref,
            lambda h: block_ref.at[0, h],
            rows_ref,
            step,
            experts,
            cap,
            min(part, 512),
        )

    @pl.when(step >= blocks)
    def _():
        e = step - blocks
        total = nt_dot(rows_ref[e, 0].reshape(blocks * cap, part), down_ref[0, :, :part])
        for h in range(1, sides):
            total += nt_dot(
                rows_ref[e, h].reshape(blocks * cap, part),
                down_ref[0, :, h * part : (h + 1) * part],
            )
        out_ref[0] = total.astype(half_type)


def expert_kernel(
    experts,
    cap,
    flip_ref,
    place_ref,
    gate_ref,
    target_ref,
    wg_ref,
    wu_ref,
    dh_ref,
    own_first_ref,
    own_second_ref,
    core_first_ref,
    core_second_ref,
    across_first_ref,
    across_second_ref,
    far_first_ref,
    far_second_ref,
    send_ref,
    keep_ref,
    hidden_ref,
    buffer_ref,
    rows_ref,
    dgate_ref,
    sems,
):
    block_refs = [
        own_first_ref,
        own_second_ref,
        core_first_ref,
        core_second_ref,
        across_first_ref,
        across_second_ref,
        far_first_ref,
        far_second_ref,
    ]
    step = pl.program_id(0)
    half = buffer_ref.shape[3]
    toks = buffer_ref.shape[2]

    @pl.when(step == 0)
    def _():
        start_blocks(block_refs, buffer_ref, sems, flip_ref[0])

    @pl.when(step < QUAD)
    def _():
        wait_block(block_refs, buffer_ref, sems, step)
        pick_rows(
            place_ref, lambda h: buffer_ref.at[step, h], rows_ref, step, experts, cap, 512
        )

    @pl.when(jnp.logical_and(step >= QUAD, step < QUAD + experts))
    def _():
        e = step - QUAD
        first = rows_ref[e, 0].reshape(QUAD * cap, half)
        second = rows_ref[e, 1].reshape(QUAD * cap, half)
        pre_gate = jnp.dot(first, wg_ref[0, :half], preferred_element_type=jnp.float32)
        pre_gate += jnp.dot(second, wg_ref[0, half:], preferred_element_type=jnp.float32)
        pre_up = jnp.dot(first, wu_ref[0, :half], preferred_element_type=jnp.float32)
        pre_up += jnp.dot(second, wu_ref[0, half:], preferred_element_type=jnp.float32)
        sig = lax.logistic(pre_gate)
        silu = pre_gate * sig
        act = silu * pre_up
        d_raw = dh_ref[0].astype(jnp.float32)
        slot = lax.broadcasted_iota(jnp.int32, (cap, toks), 0)
        gate_parts = []
        for b in range(QUAD):
            hit = slot == place_ref[b, e]
            gate_parts.append(
                jnp.sum(jnp.where(hit, gate_ref[b, e], 0.0), axis=1, keepdims=True)
            )
        gate_col = jnp.concatenate(gate_parts, axis=0)
        hidden_ref[0] = (act * gate_col).astype(half_type)
        d_col = jnp.sum(act * d_raw, axis=1, keepdims=True)
        for b in range(QUAD):
            hit = slot == place_ref[b, e]
            dgate_ref[e, b] = jnp.sum(
                jnp.where(hit, d_col[b * cap : (b + 1) * cap], 0.0), axis=0, keepdims=True
            )
        d_hidden = d_raw * gate_col
        d_up = (d_hidden * silu).astype(half_type)
        d_gate = (d_hidden * pre_up * (sig * (1.0 + pre_gate * (1.0 - sig)))).astype(half_type)
        for h in range(2):
            d_in = nt_dot(d_gate, wg_ref[0, h * half : (h + 1) * half])
            d_in += nt_dot(d_up, wu_ref[0, h * half : (h + 1) * half])
            rows_ref[e, h] = d_in.astype(half_type).reshape(QUAD, cap, half)

    for which, out_ref in ((0, send_ref), (1, keep_ref)):
        first_step = QUAD + experts + 2 * which

        @pl.when(jnp.logical_and(step >= first_step, step < first_step + 2))
        def _():
            b = 2 * (step - first_step) + 1 - which
            add_rows(target_ref, rows_ref, out_ref, b, flip_ref[0], experts, cap, 512)
            add_gates(dgate_ref, out_ref, b, flip_ref[1], experts)


def output_kernel(experts, cap, flip_ref, target_ref, down_ref, hidden_ref, send_ref, keep_ref, rows_ref):
    step = pl.program_id(0)
    half = rows_ref.shape[4]

    @pl.when(step < experts)
    def _():
        for h in range(2):
            out = jnp.dot(
                hidden_ref[0],
                down_ref[0, :, h * half : (h + 1) * half],
                preferred_element_type=jnp.float32,
            )
            rows_ref[step, h] = out.astype(half_type).reshape(QUAD, cap, half)

    for which, out_ref in ((0, send_ref), (1, keep_ref)):
        first_step = experts + 2 * which

        @pl.when(jnp.logical_and(step >= first_step, step < first_step + 2))
        def _():
            b = 2 * (step - first_step) + 1 - which
            add_rows(target_ref, rows_ref, out_ref, b, flip_ref[0], experts, cap, 512)


def whole(shape):
    return pl.BlockSpec(shape, lambda i, *_: (0,) * len(shape), pipeline_mode=pl.Buffered(1))


def per_step(shape, first, count):
    return pl.BlockSpec(
        (1,) + shape[1:], lambda i, *_: (jnp.clip(i - first, 0, count - 1),) + (0,) * (len(shape) - 1)
    )


def call_grad_rows(block_ids, place, down, blocks, cap):
    experts, hidden_units, width = down.shape
    count, sides, toks, half = blocks.shape
    rows = count * cap
    return pl.pallas_call(
        functools.partial(grad_rows_kernel, experts, cap),
        out_shape=jax.ShapeDtypeStruct((experts, rows, hidden_units), half_type),
        grid_spec=pltpu.PrefetchScalarGridSpec(
            num_scalar_prefetch=1,
            grid=(count + experts,),
            in_specs=[
                whole(place.shape),
                per_step(down.shape, count, experts),
                pl.BlockSpec(
                    (1, sides, toks, half),
                    lambda i, ids: (ids[jnp.minimum(i, count - 1)], 0, 0, 0),
                ),
            ],
            out_specs=per_step((experts, rows, hidden_units), count, experts),
            scratch_shapes=[pltpu.VMEM((experts, sides, count, cap, half), half_type)],
        ),
        compiler_params=pltpu.CompilerParams(
            dimension_semantics=("arbitrary",), vmem_limit_bytes=VMEM_LIMIT
        ),
        cost_estimate=pl.CostEstimate(
            flops=4 * experts * rows * width * (toks + hidden_units),
            bytes_accessed=2 * (down.size + blocks.size + experts * rows * hidden_units),
            transcendentals=0,
        ),
        name="grad_rows",
    )(block_ids, place, down, blocks)


def call_experts(group, flip, place, gate, target, gate_w, up_w, d_raw, pieces, cap, extra):
    experts, width, hidden_units = gate_w.shape
    toks, half = pieces[0].shape
    rows = QUAD * cap
    blocks = (2, 2, toks + extra, half)
    return pl.pallas_call(
        functools.partial(expert_kernel, experts, cap),
        out_shape=(
            jax.ShapeDtypeStruct(blocks, half_type),
            jax.ShapeDtypeStruct(blocks, half_type),
            jax.ShapeDtypeStruct((experts, rows, hidden_units), half_type),
        ),
        grid_spec=pltpu.PrefetchScalarGridSpec(
            num_scalar_prefetch=1,
            grid=(2 * QUAD + experts,),
            in_specs=[
                whole(place.shape),
                whole(gate.shape),
                whole(target.shape),
                per_step(gate_w.shape, QUAD, experts),
                per_step(up_w.shape, QUAD, experts),
                pl.BlockSpec(
                    (1, rows, hidden_units),
                    lambda i, *_: (jnp.clip(i - QUAD, 0, experts - 1), group, 0),
                ),
            ]
            + [pl.BlockSpec(memory_space=pl.ANY)] * len(pieces),
            out_specs=(
                per_step(blocks, QUAD + experts, 2),
                per_step(blocks, QUAD + experts + 2, 2),
                per_step((experts, rows, hidden_units), QUAD, experts),
            ),
            scratch_shapes=[
                pltpu.VMEM((QUAD, 2, toks, half), half_type),
                pltpu.VMEM((experts, 2, QUAD, cap, half), half_type),
                pltpu.VMEM((experts, QUAD, 1, toks), jnp.float32),
                pltpu.SemaphoreType.DMA((QUAD, 2)),
            ],
        ),
        compiler_params=pltpu.CompilerParams(
            dimension_semantics=("arbitrary",), vmem_limit_bytes=VMEM_LIMIT
        ),
        cost_estimate=pl.CostEstimate(
            flops=6 * experts * rows * width * (toks + 2 * hidden_units),
            bytes_accessed=2 * (2 * gate_w.size + 4 * QUAD * toks * half),
            transcendentals=experts * rows * hidden_units,
        ),
        name="experts",
    )(flip, place, gate, target, gate_w, up_w, d_raw, *pieces)


def call_output(flip, target, down, hidden, cap, half):
    experts, hidden_units, width = down.shape
    toks = target.shape[1]
    rows = QUAD * cap
    blocks = (2, 2, toks, half)
    return pl.pallas_call(
        functools.partial(output_kernel, experts, cap),
        out_shape=(
            jax.ShapeDtypeStruct(blocks, half_type),
            jax.ShapeDtypeStruct(blocks, half_type),
        ),
        grid_spec=pltpu.PrefetchScalarGridSpec(
            num_scalar_prefetch=1,
            grid=(QUAD + experts,),
            in_specs=[
                whole(target.shape),
                per_step(down.shape, 0, experts),
                per_step(hidden.shape, 0, experts),
            ],
            out_specs=(per_step(blocks, experts, 2), per_step(blocks, experts + 2, 2)),
            scratch_shapes=[pltpu.VMEM((experts, 2, QUAD, cap, half), half_type)],
        ),
        compiler_params=pltpu.CompilerParams(
            dimension_semantics=("arbitrary",), vmem_limit_bytes=VMEM_LIMIT
        ),
        cost_estimate=pl.CostEstimate(
            flops=4 * experts * rows * width * (toks + hidden_units),
            bytes_accessed=2 * (down.size + 2 * QUAD * toks * half),
            transcendentals=0,
        ),
        name="outputs",
    )(flip, target, down, hidden)


def swap(values, data_count, bit):
    return lax.ppermute(values, "dp", [(i, i ^ bit) for i in range(data_count)])


def onward(values, data_count):
    return lax.ppermute(values, "dp", [(i, (i + QUAD) % data_count) for i in range(data_count)])


def other_side(values):
    return lax.ppermute(values, "tensor", [(0, 1), (1, 0)])


def fence(*values):
    return lax.optimization_barrier(values)


def plus(*terms):
    total = terms[0].astype(jnp.float32)
    for term in terms[1:]:
        total = total + term.astype(jnp.float32)
    return total.astype(half_type)


def local(
    layer_input,
    cotangent,
    attention_norm_gain,
    expert_norm_gain,
    query_norm_gain,
    key_norm_gain,
    query_weight_matrix,
    key_weight_matrix,
    value_weight_matrix,
    output_weight_matrix,
    adapter_projection_down,
    adapter_projection_up,
    adapter_output_down,
    adapter_output_up,
    router,
    expert_gate_weight,
    expert_up_weight,
    expert_down_weight,
    segments,
    sequence_adapter_index,
    routes,
):
    tok_count = layer_input.shape[0]
    tensor_count = lax.axis_size("tensor")
    data_count = lax.axis_size("dp")
    pair = tensor_count == 2
    ring_count = data_count // QUAD
    col_width = MODEL_WIDTH // tensor_count
    half_width = MODEL_WIDTH // 2
    side = lax.axis_index("tensor")
    col_start = side * col_width
    place_dp = lax.axis_index("dp")
    flip = side.astype(jnp.int32) if pair else jnp.int32(0)
    flip_arr = jnp.stack([flip, place_dp.astype(jnp.int32)])
    shard_local_width = query_weight_matrix.shape[1]
    local_experts = expert_gate_weight.shape[0]
    expert_total = local_experts * data_count
    capacity = 5 * tok_count * TOP // (4 * expert_total)
    token_ids = jnp.arange(tok_count, dtype=jnp.int32)
    positions = token_ids % LEN

    def to_sides(full):
        if pair:
            low_cols, high_cols = full[:, :half_width], full[:, half_width:]
            return (
                jnp.where(flip == 0, low_cols, high_cols),
                jnp.where(flip == 0, high_cols, low_cols),
            )
        return full[:, :half_width], full[:, half_width:]

    def from_sides(first, second):
        if pair:
            return jnp.concatenate(
                [jnp.where(flip == 0, first, second), jnp.where(flip == 0, second, first)], axis=1
            )
        return jnp.concatenate([first, second], axis=1)

    routes_t = routes.T
    expert_ids = jnp.arange(expert_total, dtype=jnp.int32)
    chosen_mask = jnp.any(routes_t[:, None, :] == expert_ids[None, :, None], axis=0)
    earlier = (token_ids[:, None] < token_ids[None, :]).astype(half_type)
    rank = jnp.dot(chosen_mask.astype(half_type), earlier, preferred_element_type=jnp.float32)
    place_own = jnp.where(chosen_mask, rank, -1.0).astype(jnp.int32)
    number = jnp.broadcast_to(sequence_adapter_index[:1, None], (data_count, 1, tok_count))
    place_own = jnp.concatenate(
        [place_own.reshape(data_count, local_experts, tok_count), number], axis=1
    )
    place_all = lax.all_to_all(place_own, "dp", 0, 0, tiled=True)
    numbers = place_all[:, local_experts, 0]
    place_all = place_all[:, :local_experts]
    ring_at, quad_at = place_dp // QUAD, place_dp % QUAD
    group_ids = jnp.arange(data_count, dtype=jnp.int32)
    order = ((ring_at - group_ids // QUAD) % ring_count) * QUAD + (quad_at ^ (group_ids % QUAD))
    place_all = place_all[order]
    target_all = jnp.where(
        place_all >= 0,
        place_all + capacity * jnp.arange(local_experts, dtype=jnp.int32)[None, :, None],
        -1,
    ).transpose(0, 2, 1)

    def group_of(values, j):
        return values[j * QUAD : (j + 1) * QUAD]

    adapter = sequence_adapter_index[0]

    def own_adapter(factors, axis):
        return lax.dynamic_index_in_dim(factors, adapter, axis, keepdims=False)

    down_rows = own_adapter(adapter_projection_down.transpose(0, 1, 3, 2), 1)
    down_rows = down_rows.reshape(3 * ADAPTER_RANK, MODEL_WIDTH)
    up_rows = own_adapter(adapter_projection_up, 1)
    out_down_rows = own_adapter(adapter_output_down.transpose(0, 2, 1), 0)
    out_up_rows = own_adapter(adapter_output_up, 0)
    doc_flat = segments.reshape(-1)
    hidden32 = layer_input.astype(jnp.float32)
    hidden_scale = lax.rsqrt(
        jnp.mean(hidden32 * hidden32, axis=-1, keepdims=True) + norm_eps
    )
    normed = (hidden32 * hidden_scale * attention_norm_gain).astype(half_type)
    w_proj = [query_weight_matrix, key_weight_matrix, value_weight_matrix]
    latents = nt_dot(normed, down_rows).astype(half_type)
    latents = [latents[:, p * ADAPTER_RANK : (p + 1) * ADAPTER_RANK] for p in range(3)]
    raw_proj = [
        jnp.dot(normed, w_proj[p], preferred_element_type=jnp.float32)
        + jnp.dot(latents[p], up_rows[p], preferred_element_type=jnp.float32)
        for p in range(3)
    ]
    g_all = lax.all_gather(cotangent, ("dp", "tensor"), axis=0)
    g_all = g_all.reshape(data_count, tensor_count, tok_count, col_width)
    raw_proj[0], place_all, target_all = fence(raw_proj[0], place_all, target_all)
    head_shared = [
        *rotation(positions),
        query_norm_gain[None, :],
        key_norm_gain[None, :],
        doc_flat[:, None],
        doc_flat[None, :],
    ]
    attended, queries, keys, values = call_heads(
        attend_kernel, "attend", raw_proj, head_shared, 4
    )
    proj_part = jnp.dot(attended, output_weight_matrix, preferred_element_type=jnp.float32)
    latent_part = nt_dot(attended, out_down_rows)

    def tensor_sum(part):
        if pair:
            return part.astype(jnp.float32) + other_side(part).astype(jnp.float32)
        return lax.psum(part, "tensor").astype(jnp.float32)

    def split_columns(part):
        if pair:
            mine, theirs = to_sides(part)
            return mine.astype(jnp.float32), theirs.astype(half_type)
        return None, part.astype(half_type)

    def join_columns(mine, theirs):
        if pair:
            return mine + other_side(theirs).astype(jnp.float32)
        return lax.psum_scatter(theirs, "tensor", scatter_dimension=1, tiled=True).astype(
            jnp.float32
        )

    def own_columns(part):
        return join_columns(*split_columns(part))

    def columns_of(full):
        if pair:
            return to_sides(full)[0]
        return lax.dynamic_slice_in_dim(full, col_start, col_width, full.ndim - 1)

    def both_halves(cols):
        if pair:
            return cols, other_side(cols)
        full = lax.all_gather(cols, "tensor", axis=1, tiled=True)
        return full[:, :half_width], full[:, half_width:]

    attn_cols = own_columns(proj_part)
    latent_total = tensor_sum(latent_part.astype(half_type))
    latent_out = latent_total.astype(half_type)
    mixed_cols = (
        columns_of(layer_input).astype(jnp.float32)
        + attn_cols
        + jnp.dot(latent_out, columns_of(out_up_rows), preferred_element_type=jnp.float32)
    )
    expert_gain_cols = columns_of(expert_norm_gain[None, :])
    square_sum = tensor_sum(jnp.sum(mixed_cols * mixed_cols, axis=1, keepdims=True))
    mixed_scale = lax.rsqrt(square_sum / MODEL_WIDTH + norm_eps)
    moe_cols_in = (mixed_cols * mixed_scale * expert_gain_cols).astype(half_type)

    def gates_of(first, second):
        moe_in = from_sides(first, second)
        logits_t = lax.dot_general(
            router, moe_in, (((0,), (1,)), ((), ())), preferred_element_type=jnp.float32
        )
        top_logit = jnp.max(jnp.where(chosen_mask, logits_t, -jnp.inf), axis=0, keepdims=True)
        gate_exp = jnp.where(chosen_mask, jnp.exp(jnp.minimum(logits_t - top_logit, 0.0)), 0.0)
        return gate_exp / jnp.sum(gate_exp, axis=0, keepdims=True)

    def experts_of(k, pieces):
        return call_experts(
            k,
            flip_arr,
            group_of(place_all, k)[:, :, None, :],
            group_of(gates_all, k)[:, :, None, :],
            group_of(target_all, k),
            expert_gate_weight,
            expert_up_weight,
            d_raw[0],
            pieces,
            capacity,
            expert_total * tok_count // half_width,
        )

    def outputs_of(k, hidden):
        return call_output(
            flip_arr,
            group_of(target_all, k),
            expert_down_weight,
            hidden,
            capacity,
            half_width,
        )

    quads = ring_count
    own0, own1, core0, core1 = ([None] * quads for _ in range(4))
    af, asec, ff, fs = ([None] * quads for _ in range(4))
    d_raw = [None]
    sides_by_tensor = [pair and j != quads - 1 for j in range(quads)]
    hidden = [None] * quads

    def make_sums():
        return {
            name: [None] * quads for name in ("send", "keep", "got", "near", "side_got", "first")
        }

    grads, outs = make_sums(), make_sums()

    def move_first(j):
        own0[j + 1] = onward(own0[j], data_count)

    def move_second(j):
        own1[j + 1] = onward(own1[j], data_count)

    def send_across(j):
        af[j] = swap(own0[j], data_count, 2)
        core0[j] = swap(own0[j], data_count, 1)

    def send_rest(j):
        asec[j] = (
            other_side(af[j]) if sides_by_tensor[j] else swap(own1[j], data_count, 2)
        )
        core1[j] = swap(own1[j], data_count, 1)
        ff[j] = swap(af[j], data_count, 1)

    def send_last(j):
        fs[j] = swap(asec[j], data_count, 1)

    def run_experts(k):
        pieces = [own0[k], own1[k], core0[k], core1[k], af[k], asec[k], ff[k], fs[k]]
        grads["send"][k], grads["keep"][k], hidden[k] = experts_of(k, pieces)

    def run_outputs(k):
        outs["send"][k], outs["keep"][k] = outputs_of(k, hidden[k])

    def sum_cores(sums, k):
        sums["got"][k] = swap(sums["send"][k], data_count, 1)

    def sum_sides(sums, k):
        keep, got = sums["keep"][k], sums["got"][k]
        away = plus(keep[1, 1], got[1, 1])
        sums["side_got"][k] = other_side(away) if pair else swap(away, data_count, 2)
        sums["near"][k] = plus(keep[1, 0], got[1, 0])

    def sum_across(sums, k):
        keep, got, near = sums["keep"][k], sums["got"][k], sums["near"][k]
        if pair:
            near = plus(near, sums["side_got"][k])
        sums["first"][k] = plus(keep[0, 0], got[0, 0], swap(near, data_count, 2))

    def second_of(sums, k):
        terms = [sums["keep"][k][0, 1], sums["got"][k][0, 1]]
        return terms if pair else terms + [sums["side_got"][k]]

    def onward_sum(*terms):
        return onward(plus(*terms), data_count)

    def step_end(*more):
        groups = (
            own0, own1, core0, core1, af, asec, ff, fs, d_raw, hidden,
            *grads.values(), *outs.values(),
        )
        fenced = fence(groups, more)
        for old, fresh in zip(groups, fenced[0]):
            old[:] = fresh
        return fenced[1]

    own0[0] = moe_cols_in if pair else both_halves(moe_cols_in)[0]
    own1[0] = both_halves(moe_cols_in)[1]
    move_first(0)
    send_across(0)
    step_end()
    gates_t = gates_of(own0[0], own1[0])
    move_second(0)
    send_rest(0)
    send_across(1)
    (gates_t,) = step_end(gates_t)
    gates_all = lax.all_to_all(
        gates_t.reshape(data_count, local_experts, tok_count), "dp", 0, 0, tiled=True
    )[order]
    move_first(1)
    send_rest(1)
    send_last(0)
    step_end()
    move_second(1)
    send_across(2)
    send_last(1)
    d_raw[0] = call_grad_rows(
        order, place_all[:, :, None, :], expert_down_weight, g_all, capacity
    )
    (gates_all,) = step_end(gates_all)
    move_first(2)
    send_rest(2)
    run_experts(1)
    step_end()
    move_second(2)
    send_across(3)
    send_last(2)
    sum_cores(grads, 1)
    run_experts(0)
    step_end()
    send_rest(3)
    sum_sides(grads, 1)
    sum_cores(grads, 0)
    run_experts(2)
    step_end()
    send_last(3)
    sum_across(grads, 1)
    sum_sides(grads, 0)
    sum_cores(grads, 2)
    second = onward_sum(*second_of(grads, 1))
    run_experts(3)
    (second,) = step_end(second)
    sum_sides(grads, 2)
    sum_across(grads, 0)
    sum_cores(grads, 3)
    first = onward(grads["first"][1], data_count)
    second = onward_sum(second, *second_of(grads, 2))
    run_outputs(1)
    first, second = step_end(first, second)
    sum_sides(grads, 3)
    sum_across(grads, 2)
    second = onward_sum(second, *second_of(grads, 3))
    sum_cores(outs, 1)
    run_outputs(2)
    first, second = step_end(first, second)
    first = onward_sum(first, grads["first"][2])
    second = plus(second, *second_of(grads, 0))
    sum_across(grads, 3)
    sum_cores(outs, 2)
    sum_sides(outs, 1)
    run_outputs(3)
    first, second = step_end(first, second)
    first = onward_sum(first, grads["first"][3])
    sum_cores(outs, 3)
    sum_across(outs, 1)
    run_outputs(0)
    if pair:
        from_other = other_side(second).astype(jnp.float32)
        grad_moe_cols = first.astype(jnp.float32) + grads["first"][0].astype(jnp.float32) + from_other
    else:
        first = plus(first, grads["first"][0])
        grad_gates = tensor_sum(first[tok_count:])
        grad_moe_cols = own_columns(from_sides(first[:tok_count], second[:tok_count]))
        grad_moe_cols = jnp.pad(grad_moe_cols, ((0, 0), (0, half_width - col_width)))
        grad_moe_cols = jnp.concatenate([grad_moe_cols, grad_gates], axis=0)
    (grad_moe_cols,) = step_end(grad_moe_cols)
    sum_cores(outs, 0)
    sum_sides(outs, 2)
    out_second = onward_sum(*second_of(outs, 1))
    d_gate_home = grad_moe_cols[tok_count:].reshape(expert_total, tok_count)
    grad_moe_cols = grad_moe_cols[:tok_count, :col_width]

    weighted = gates_t * d_gate_home
    grad_logits_t = (
        gates_t * (d_gate_home - jnp.sum(weighted, axis=0, keepdims=True))
    ).astype(half_type)
    router_cols = router.T
    grad_moe_cols = grad_moe_cols + lax.dot_general(
        grad_logits_t,
        columns_of(router_cols),
        (((0,), (0,)), ((), ())),
        preferred_element_type=jnp.float32,
    )
    along = tensor_sum(
        jnp.sum(mixed_cols * expert_gain_cols * grad_moe_cols, axis=1, keepdims=True)
    )
    grad_mixed_cols = (
        cotangent.astype(jnp.float32)
        + expert_gain_cols * mixed_scale * grad_moe_cols
        - mixed_cols * (mixed_scale * mixed_scale * mixed_scale * (along / MODEL_WIDTH))
    )
    branch_cols = grad_mixed_cols.astype(half_type)
    branch_cols, out_second = step_end(branch_cols, out_second)
    sum_across(outs, 2)
    out_second = onward_sum(out_second, *second_of(outs, 2))
    grad_branch = from_sides(*both_halves(branch_cols))
    grad_branch, out_second = step_end(grad_branch, out_second)
    sum_sides(outs, 3)
    out_first = onward(outs["first"][1], data_count)

    grad_latent_out = nt_dot(grad_branch, out_up_rows).astype(half_type)
    grad_up_out = lax.dot_general(
        latent_out, branch_cols, (((0,), (0,)), ((), ())), preferred_element_type=jnp.float32
    )
    grad_attended = nt_dot(grad_branch, output_weight_matrix) + jnp.dot(
        grad_latent_out, out_down_rows, preferred_element_type=jnp.float32
    )
    grad_heads = grad_attended.astype(half_type)
    grad_down_out = lax.dot_general(
        grad_latent_out, attended, (((0,), (0,)), ((), ())), preferred_element_type=jnp.float32
    )

    grad_raw = call_heads(
        attend_back_kernel,
        "attend_back",
        [raw_proj[0], raw_proj[1], queries, keys, values, grad_heads],
        head_shared,
        3,
    )
    grad_raw, out_first = step_end(grad_raw, out_first)
    sum_sides(outs, 0)
    sum_across(outs, 3)
    out_first = onward_sum(out_first, outs["first"][2])
    latent_parts = jnp.concatenate([nt_dot(grad_raw[p], up_rows[p]) for p in range(3)], axis=1)
    grad_latent = tensor_sum(latent_parts.astype(half_type)).astype(half_type)
    grad_up = [
        lax.dot_general(
            latents[p], grad_raw[p], (((0,), (0,)), ((), ())), preferred_element_type=jnp.float32
        )
        for p in range(3)
    ]
    grad_down = lax.dot_general(
        grad_latent, normed, (((0,), (0,)), ((), ())), preferred_element_type=jnp.float32
    )
    parts = [grad_down_out, grad_up_out] + grad_up
    parts += [
        grad_down[:, i * shard_local_width : (i + 1) * shard_local_width]
        for i in range(tensor_count)
    ]
    parts = jnp.concatenate([part.astype(half_type) for part in parts], axis=0)
    parts_all = lax.all_gather(parts, "dp", axis=0)
    holds = numbers[None, :] == jnp.arange(ADAPTER_CHOICES, dtype=jnp.int32)[:, None]
    adapter_sums = jnp.einsum(
        "as,src->arc", holds.astype(half_type), parts_all, preferred_element_type=jnp.float32
    )

    def rows_at(i):
        return adapter_sums[:, i * ADAPTER_RANK : (i + 1) * ADAPTER_RANK]

    sum_up_qkv = jnp.stack([rows_at(2 + p) for p in range(3)])
    sum_down_qkv = jnp.stack(
        [
            jnp.concatenate([rows_at(5 + 3 * i + p) for i in range(tensor_count)], axis=2)
            for p in range(3)
        ]
    ).transpose(0, 1, 3, 2)

    grad_normed_part = nt_dot(grad_raw[0], w_proj[0])
    grad_normed_part += nt_dot(grad_raw[1], w_proj[1])
    grad_normed_part += nt_dot(grad_raw[2], w_proj[2])
    grad_normed_mine, grad_normed_other = split_columns(grad_normed_part)
    grad_normed_other, out_first = step_end(grad_normed_other, out_first)
    sum_across(outs, 0)
    out_second = onward_sum(out_second, *second_of(outs, 3))
    grad_normed_cols = join_columns(grad_normed_mine, grad_normed_other)
    grad_normed_cols, out_second = step_end(grad_normed_cols, out_second)
    out_first = plus(onward_sum(out_first, outs["first"][3]), outs["first"][0])
    out_second = plus(out_second, *second_of(outs, 0))
    if pair:
        moe_cols = out_first.astype(jnp.float32) + other_side(out_second).astype(jnp.float32)
    else:
        moe_cols = own_columns(from_sides(out_first, out_second))
    layer_out = (mixed_cols + moe_cols).astype(half_type)
    grad_normed_cols += jnp.dot(
        grad_latent, columns_of(down_rows), preferred_element_type=jnp.float32
    )
    attention_gain_cols = columns_of(attention_norm_gain[None, :])
    hidden_cols = columns_of(layer_input).astype(jnp.float32)
    along_in = tensor_sum(
        jnp.sum(hidden_cols * attention_gain_cols * grad_normed_cols, axis=1, keepdims=True)
    )
    grad_input = (
        grad_mixed_cols
        + attention_gain_cols * hidden_scale * grad_normed_cols
        - hidden_cols * (hidden_scale * hidden_scale * hidden_scale * (along_in / MODEL_WIDTH))
    )
    return (
        layer_out,
        grad_input,
        sum_down_qkv,
        sum_up_qkv,
        rows_at(0).transpose(0, 2, 1),
        rows_at(1),
    )


def solution(mesh):
    return jax.shard_map(
        local,
        mesh=mesh,
        in_specs=(
            P("dp", None),
            P("dp", "tensor"),
            P(),
            P(),
            P(),
            P(),
            P(None, "tensor"),
            P(None, "tensor"),
            P(None, "tensor"),
            P("tensor", None),
            P(),
            P(None, None, None, "tensor"),
            P(None, "tensor", None),
            P(),
            P(),
            P("dp", None, "tensor"),
            P("dp", None, "tensor"),
            P("dp", "tensor", None),
            P("dp", None),
            P("dp"),
            P("dp", None),
        ),
        out_specs=(
            P("dp", "tensor"),
            P("dp", "tensor"),
            P(),
            P(None, None, None, "tensor"),
            P(None, "tensor", None),
            P(None, None, "tensor"),
        ),
        check_vma=False,
    )
```

```python
import functools

import jax
import jax.numpy as jnp
from jax import lax
from jax.experimental import pallas as pl
from jax.experimental.pallas import tpu as pltpu
from jax.sharding import PartitionSpec as P

MODEL_WIDTH = 2048
HEAD_WIDTH = 128
TOP = 8
LEN = 512
ADAPTER_RANK = 16
ADAPTER_CHOICES = 8
QUAD = 4

norm_eps = 1e-05
head_eps = 1e-06
rope_base = 50000.0
half_type = jnp.bfloat16
VMEM_LIMIT = 56 * 1024 * 1024


def rotation(positions):
    half_dim = HEAD_WIDTH // 2
    inverse = rope_base ** (-(jnp.arange(half_dim, dtype=jnp.float32) * 2.0 / HEAD_WIDTH))
    angles = positions.astype(jnp.float32)[:, None] * inverse[None, :]
    cosine, sine = jnp.cos(angles), jnp.sin(angles)
    return (
        jnp.concatenate([cosine, cosine], axis=1),
        jnp.concatenate([-sine, sine], axis=1),
    )


def nt_dot(left, right):
    return lax.dot_general(
        left, right, (((1,), (1,)), ((), ())), preferred_element_type=jnp.float32
    )


def tn_dot(left, right):
    return lax.dot_general(
        left, right, (((0,), (0,)), ((), ())), preferred_element_type=jnp.float32
    )


def head_prep(raw, gain, cosine, sine):
    scale = lax.rsqrt(jnp.mean(raw * raw, axis=-1, keepdims=True) + head_eps)
    scaled = raw * scale * gain
    return scaled * cosine + pltpu.roll(scaled, HEAD_WIDTH // 2, 1) * sine


def head_prep_back(grad, raw, gain, cosine, sine):
    scale = lax.rsqrt(jnp.mean(raw * raw, axis=-1, keepdims=True) + head_eps)
    turned = (grad * cosine - pltpu.roll(grad, HEAD_WIDTH // 2, 1) * sine) * gain
    along = jnp.mean(raw * turned, axis=-1, keepdims=True)
    return scale * turned - raw * (scale * scale * scale * along)


def masked_exp(queries, keys, docs_col, docs_row):
    scores = nt_dot(queries, keys) * HEAD_WIDTH ** (-0.5)
    scores = jnp.where(docs_col == docs_row, scores, -1e30)
    exp_scores = jnp.exp(scores - jnp.max(scores, axis=-1, keepdims=True))
    return exp_scores, jnp.sum(exp_scores, axis=-1, keepdims=True)


def attend_kernel(
    raw_q, raw_k, raw_v, cosine, sine, gain_q, gain_k, docs_col, docs_row, out, queries, keys, values
):
    q = head_prep(raw_q[...], gain_q[...], cosine[...], sine[...]).astype(half_type)
    k = head_prep(raw_k[...], gain_k[...], cosine[...], sine[...]).astype(half_type)
    v = raw_v[...].astype(half_type)
    queries[...], keys[...], values[...] = q, k, v
    exp_scores, total = masked_exp(q, k, docs_col[...], docs_row[...])
    probs = (exp_scores / total).astype(half_type)
    out[...] = jnp.dot(probs, v, preferred_element_type=jnp.float32).astype(half_type)


def attend_back_kernel(
    raw_q, raw_k, queries, keys, values, grad, cosine, sine, gain_q, gain_k, docs_col, docs_row,
    grad_q, grad_k, grad_v,
):
    q, k, v, g = queries[...], keys[...], values[...], grad[...]
    score_scale = HEAD_WIDTH ** (-0.5)
    exp_scores, total = masked_exp(q, k, docs_col[...], docs_row[...])
    probs = exp_scores / total
    grad_v[...] = tn_dot(probs.astype(half_type), g).astype(half_type)
    grad_probs = nt_dot(g, v)
    delta = jnp.sum(probs * grad_probs, axis=-1, keepdims=True)
    grad_scores = (probs * (grad_probs - delta)).astype(half_type)
    d_q = jnp.dot(grad_scores, k, preferred_element_type=jnp.float32) * score_scale
    d_k = tn_dot(grad_scores, q) * score_scale
    grad_q[...] = head_prep_back(d_q, raw_q[...], gain_q[...], cosine[...], sine[...]).astype(
        half_type
    )
    grad_k[...] = head_prep_back(d_k, raw_k[...], gain_k[...], cosine[...], sine[...]).astype(
        half_type
    )


def call_heads(kernel, name, by_head, shared, out_count):
    toks, width = by_head[0].shape
    head = pl.BlockSpec((toks, HEAD_WIDTH), lambda h: (0, h))
    return pl.pallas_call(
        kernel,
        out_shape=[jax.ShapeDtypeStruct((toks, width), half_type)] * out_count,
        grid=(width // HEAD_WIDTH,),
        in_specs=[head] * len(by_head)
        + [pl.BlockSpec(v.shape, lambda h: (0, 0)) for v in shared],
        out_specs=[head] * out_count,
        compiler_params=pltpu.CompilerParams(
            dimension_semantics=("arbitrary",), vmem_limit_bytes=VMEM_LIMIT
        ),
        cost_estimate=pl.CostEstimate(
            flops=10 * toks * toks * width, bytes_accessed=8 * toks * width, transcendentals=toks * toks
        ),
        name=name,
    )(*by_head, *shared)


def start_blocks(pieces, buffer_ref, sems, flip):
    for b in range(QUAD):
        for r in range(2):
            pltpu.make_async_copy(
                pieces[2 * b + r], buffer_ref.at[b, r ^ flip], sems.at[b, r]
            ).start()


def wait_block(pieces, buffer_ref, sems, b):
    for r in range(2):
        pltpu.make_async_copy(pieces[0], buffer_ref.at[b, r], sems.at[b, r]).wait()


def pick_rows(place_ref, half_at, rows_ref, b, experts, cap, tile):
    toks = half_at(0).shape[0]
    slot = lax.broadcasted_iota(jnp.int32, (cap, toks), 0)
    picks = jnp.concatenate(
        [jnp.where(slot == place_ref[b, e], 1.0, 0.0) for e in range(experts)], axis=0
    ).astype(half_type)
    half = rows_ref.shape[4]
    for h in range(rows_ref.shape[1]):
        for start in range(0, half, tile):
            rows = jnp.dot(
                picks,
                half_at(h)[:, start : start + tile],
                preferred_element_type=jnp.float32,
            ).astype(half_type)
            for e in range(experts):
                rows_ref[e, h, b, :, start : start + tile] = rows[e * cap : (e + 1) * cap]


def add_rows(target_ref, rows_ref, out_ref, b, flip, experts, cap, tile):
    target = target_ref[b]
    toks = target.shape[0]
    lane = lax.broadcasted_iota(jnp.int32, (toks, experts * cap), 1)
    hit = lane == target[:, 0:1]
    for e in range(1, experts):
        hit = jnp.logical_or(hit, lane == target[:, e : e + 1])
    spread = jnp.where(hit, 1.0, 0.0).astype(half_type)
    half = rows_ref.shape[4]
    for h in range(2):
        for start in range(0, half, tile):
            rows = jnp.concatenate(
                [rows_ref[e, h, b, :, start : start + tile] for e in range(experts)], axis=0
            )
            out_ref[0, h ^ flip, :toks, start : start + tile] = jnp.dot(
                spread, rows, preferred_element_type=jnp.float32
            ).astype(half_type)


def add_gates(dgate_ref, out_ref, b, device, experts):
    toks, half = dgate_ref.shape[3], out_ref.shape[3]
    extra = out_ref.shape[2] - toks
    per_row = half // toks
    row = lax.broadcasted_iota(jnp.int32, (extra, half), 0)
    values = jnp.zeros((extra, half), jnp.float32)
    for i in range(experts // per_row):
        line = jnp.concatenate(
            [dgate_ref[i * per_row + n, b] for n in range(per_row)], axis=1
        )
        values = jnp.where(row == device * (experts // per_row) + i, line, values)
    for h in range(2):
        out_ref[0, h, toks:, :] = values.astype(half_type)


def grad_rows_kernel(experts, cap, block_ids, place_ref, down_ref, block_ref, out_ref, rows_ref):
    step = pl.program_id(0)
    sides, blocks, part = rows_ref.shape[1], rows_ref.shape[2], rows_ref.shape[4]

    @pl.when(step < blocks)
    def _():
        pick_rows(
            place_ref,
            lambda h: block_ref.at[0, h],
            rows_ref,
            step,
            experts,
            cap,
            min(part, 512),
        )

    @pl.when(step >= blocks)
    def _():
        e = step - blocks
        total = nt_dot(rows_ref[e, 0].reshape(blocks * cap, part), down_ref[0, :, :part])
        for h in range(1, sides):
            total += nt_dot(
                rows_ref[e, h].reshape(blocks * cap, part),
                down_ref[0, :, h * part : (h + 1) * part],
            )
        out_ref[0] = total.astype(half_type)


def expert_kernel(
    experts,
    cap,
    flip_ref,
    place_ref,
    gate_ref,
    target_ref,
    wg_ref,
    wu_ref,
    dh_ref,
    own_first_ref,
    own_second_ref,
    core_first_ref,
    core_second_ref,
    across_first_ref,
    across_second_ref,
    far_first_ref,
    far_second_ref,
    send_ref,
    keep_ref,
    hidden_ref,
    buffer_ref,
    rows_ref,
    dgate_ref,
    wg_buffer,
    wu_buffer,
    sems,
    weight_sems,
):
    block_refs = [
        own_first_ref,
        own_second_ref,
        core_first_ref,
        core_second_ref,
        across_first_ref,
        across_second_ref,
        far_first_ref,
        far_second_ref,
    ]
    step = pl.program_id(0)
    half = buffer_ref.shape[3]
    toks = buffer_ref.shape[2]

    def weight_copies(e):
        return (
            pltpu.make_async_copy(wg_ref.at[e], wg_buffer.at[e], weight_sems.at[e, 0]),
            pltpu.make_async_copy(wu_ref.at[e], wu_buffer.at[e], weight_sems.at[e, 1]),
        )

    @pl.when(step == 0)
    def _():
        start_blocks(block_refs, buffer_ref, sems, flip_ref[0])

    @pl.when(step < experts)
    def _():
        for copy in weight_copies(step):
            copy.start()

    @pl.when(step < QUAD)
    def _():
        wait_block(block_refs, buffer_ref, sems, step)
        pick_rows(
            place_ref, lambda h: buffer_ref.at[step, h], rows_ref, step, experts, cap, 512
        )

    @pl.when(jnp.logical_and(step >= QUAD, step < QUAD + experts))
    def _():
        e = step - QUAD
        for copy in weight_copies(e):
            copy.wait()
        first = rows_ref[e, 0].reshape(QUAD * cap, half)
        second = rows_ref[e, 1].reshape(QUAD * cap, half)
        pre_gate = jnp.dot(first, wg_buffer[e, :half], preferred_element_type=jnp.float32)
        pre_gate += jnp.dot(second, wg_buffer[e, half:], preferred_element_type=jnp.float32)
        pre_up = jnp.dot(first, wu_buffer[e, :half], preferred_element_type=jnp.float32)
        pre_up += jnp.dot(second, wu_buffer[e, half:], preferred_element_type=jnp.float32)
        sig = lax.logistic(pre_gate)
        silu = pre_gate * sig
        act = silu * pre_up
        d_raw = dh_ref[0].astype(jnp.float32)
        slot = lax.broadcasted_iota(jnp.int32, (cap, toks), 0)
        gate_parts = []
        for b in range(QUAD):
            hit = slot == place_ref[b, e]
            gate_parts.append(
                jnp.sum(jnp.where(hit, gate_ref[b, e], 0.0), axis=1, keepdims=True)
            )
        gate_col = jnp.concatenate(gate_parts, axis=0)
        hidden_ref[0] = (act * gate_col).astype(half_type)
        d_col = jnp.sum(act * d_raw, axis=1, keepdims=True)
        for b in range(QUAD):
            hit = slot == place_ref[b, e]
            dgate_ref[e, b] = jnp.sum(
                jnp.where(hit, d_col[b * cap : (b + 1) * cap], 0.0), axis=0, keepdims=True
            )
        d_hidden = d_raw * gate_col
        d_up = (d_hidden * silu).astype(half_type)
        d_gate = (d_hidden * pre_up * (sig * (1.0 + pre_gate * (1.0 - sig)))).astype(half_type)
        for h in range(2):
            d_in = nt_dot(d_gate, wg_buffer[e, h * half : (h + 1) * half])
            d_in += nt_dot(d_up, wu_buffer[e, h * half : (h + 1) * half])
            rows_ref[e, h] = d_in.astype(half_type).reshape(QUAD, cap, half)

    for which, out_ref in ((0, send_ref), (1, keep_ref)):
        first_step = QUAD + experts + 2 * which

        @pl.when(jnp.logical_and(step >= first_step, step < first_step + 2))
        def _():
            b = 2 * (step - first_step) + 1 - which
            add_rows(target_ref, rows_ref, out_ref, b, flip_ref[0], experts, cap, 512)
            add_gates(dgate_ref, out_ref, b, flip_ref[1], experts)


def output_kernel(
    experts,
    cap,
    flip_ref,
    target_ref,
    down_ref,
    hidden_ref,
    send_ref,
    keep_ref,
    rows_ref,
    down_buffer,
    weight_sems,
):
    step = pl.program_id(0)
    half = rows_ref.shape[4]

    def weight_copy(e):
        return pltpu.make_async_copy(down_ref.at[e], down_buffer.at[e], weight_sems.at[e])

    @pl.when(step == 0)
    def _():
        for e in range(experts):
            weight_copy(e).start()

    @pl.when(step < experts)
    def _():
        weight_copy(step).wait()
        for h in range(2):
            out = jnp.dot(
                hidden_ref[step],
                down_buffer[step, :, h * half : (h + 1) * half],
                preferred_element_type=jnp.float32,
            )
            rows_ref[step, h] = out.astype(half_type).reshape(QUAD, cap, half)

    for which, out_ref in ((0, send_ref), (1, keep_ref)):
        first_step = experts + 2 * which

        @pl.when(jnp.logical_and(step >= first_step, step < first_step + 2))
        def _():
            b = 2 * (step - first_step) + 1 - which
            add_rows(target_ref, rows_ref, out_ref, b, flip_ref[0], experts, cap, 512)


def whole(shape):
    return pl.BlockSpec(shape, lambda i, *_: (0,) * len(shape), pipeline_mode=pl.Buffered(1))


def per_step(shape, first, count):
    return pl.BlockSpec(
        (1,) + shape[1:], lambda i, *_: (jnp.clip(i - first, 0, count - 1),) + (0,) * (len(shape) - 1)
    )


def call_grad_rows(block_ids, place, down, blocks, cap):
    experts, hidden_units, width = down.shape
    count, sides, toks, half = blocks.shape
    rows = count * cap
    return pl.pallas_call(
        functools.partial(grad_rows_kernel, experts, cap),
        out_shape=jax.ShapeDtypeStruct((experts, rows, hidden_units), half_type),
        grid_spec=pltpu.PrefetchScalarGridSpec(
            num_scalar_prefetch=1,
            grid=(count + experts,),
            in_specs=[
                whole(place.shape),
                per_step(down.shape, count, experts),
                pl.BlockSpec(
                    (1, sides, toks, half),
                    lambda i, ids: (ids[jnp.minimum(i, count - 1)], 0, 0, 0),
                ),
            ],
            out_specs=per_step((experts, rows, hidden_units), count, experts),
            scratch_shapes=[pltpu.VMEM((experts, sides, count, cap, half), half_type)],
        ),
        compiler_params=pltpu.CompilerParams(
            dimension_semantics=("arbitrary",), vmem_limit_bytes=VMEM_LIMIT
        ),
        cost_estimate=pl.CostEstimate(
            flops=4 * experts * rows * width * (toks + hidden_units),
            bytes_accessed=2 * (down.size + blocks.size + experts * rows * hidden_units),
            transcendentals=0,
        ),
        name="grad_rows",
    )(block_ids, place, down, blocks)


def call_experts(group, flip, place, gate, target, gate_w, up_w, d_raw, pieces, cap, extra):
    experts, width, hidden_units = gate_w.shape
    toks, half = pieces[0].shape
    rows = QUAD * cap
    blocks = (2, 2, toks + extra, half)
    return pl.pallas_call(
        functools.partial(expert_kernel, experts, cap),
        out_shape=(
            jax.ShapeDtypeStruct(blocks, half_type),
            jax.ShapeDtypeStruct(blocks, half_type),
            jax.ShapeDtypeStruct((experts, rows, hidden_units), half_type),
        ),
        grid_spec=pltpu.PrefetchScalarGridSpec(
            num_scalar_prefetch=1,
            grid=(2 * QUAD + experts,),
            in_specs=[
                whole(place.shape),
                whole(gate.shape),
                whole(target.shape),
                pl.BlockSpec(memory_space=pl.ANY),
                pl.BlockSpec(memory_space=pl.ANY),
                pl.BlockSpec(
                    (1, rows, hidden_units),
                    lambda i, *_: (jnp.clip(i - QUAD, 0, experts - 1), group, 0),
                ),
            ]
            + [pl.BlockSpec(memory_space=pl.ANY)] * len(pieces),
            out_specs=(
                per_step(blocks, QUAD + experts, 2),
                per_step(blocks, QUAD + experts + 2, 2),
                per_step((experts, rows, hidden_units), QUAD, experts),
            ),
            scratch_shapes=[
                pltpu.VMEM((QUAD, 2, toks, half), half_type),
                pltpu.VMEM((experts, 2, QUAD, cap, half), half_type),
                pltpu.VMEM((experts, QUAD, 1, toks), jnp.float32),
                pltpu.VMEM(gate_w.shape, half_type),
                pltpu.VMEM(up_w.shape, half_type),
                pltpu.SemaphoreType.DMA((QUAD, 2)),
                pltpu.SemaphoreType.DMA((experts, 2)),
            ],
        ),
        compiler_params=pltpu.CompilerParams(
            dimension_semantics=("arbitrary",), vmem_limit_bytes=VMEM_LIMIT
        ),
        cost_estimate=pl.CostEstimate(
            flops=6 * experts * rows * width * (toks + 2 * hidden_units),
            bytes_accessed=2 * (2 * gate_w.size + 4 * QUAD * toks * half),
            transcendentals=experts * rows * hidden_units,
        ),
        name="experts",
    )(flip, place, gate, target, gate_w, up_w, d_raw, *pieces)


def call_output(flip, target, down, hidden, cap, half):
    experts, hidden_units, width = down.shape
    toks = target.shape[1]
    rows = QUAD * cap
    blocks = (2, 2, toks, half)
    return pl.pallas_call(
        functools.partial(output_kernel, experts, cap),
        out_shape=(
            jax.ShapeDtypeStruct(blocks, half_type),
            jax.ShapeDtypeStruct(blocks, half_type),
        ),
        grid_spec=pltpu.PrefetchScalarGridSpec(
            num_scalar_prefetch=1,
            grid=(QUAD + experts,),
            in_specs=[
                whole(target.shape),
                pl.BlockSpec(memory_space=pl.ANY),
                whole(hidden.shape),
            ],
            out_specs=(per_step(blocks, experts, 2), per_step(blocks, experts + 2, 2)),
            scratch_shapes=[
                pltpu.VMEM((experts, 2, QUAD, cap, half), half_type),
                pltpu.VMEM(down.shape, half_type),
                pltpu.SemaphoreType.DMA((experts,)),
            ],
        ),
        compiler_params=pltpu.CompilerParams(
            dimension_semantics=("arbitrary",), vmem_limit_bytes=VMEM_LIMIT
        ),
        cost_estimate=pl.CostEstimate(
            flops=4 * experts * rows * width * (toks + hidden_units),
            bytes_accessed=2 * (down.size + 2 * QUAD * toks * half),
            transcendentals=0,
        ),
        name="outputs",
    )(flip, target, down, hidden)


def swap(values, data_count, bit):
    return lax.ppermute(values, "dp", [(i, i ^ bit) for i in range(data_count)])


def onward(values, data_count):
    return lax.ppermute(values, "dp", [(i, (i + QUAD) % data_count) for i in range(data_count)])


def other_side(values):
    return lax.ppermute(values, "tensor", [(0, 1), (1, 0)])


def fence(*values):
    return lax.optimization_barrier(values)


def plus(*terms):
    total = terms[0].astype(jnp.float32)
    for term in terms[1:]:
        total = total + term.astype(jnp.float32)
    return total.astype(half_type)


def local(
    layer_input,
    cotangent,
    attention_norm_gain,
    expert_norm_gain,
    query_norm_gain,
    key_norm_gain,
    query_weight_matrix,
    key_weight_matrix,
    value_weight_matrix,
    output_weight_matrix,
    adapter_projection_down,
    adapter_projection_up,
    adapter_output_down,
    adapter_output_up,
    router,
    expert_gate_weight,
    expert_up_weight,
    expert_down_weight,
    segments,
    sequence_adapter_index,
    routes,
):
    tok_count = layer_input.shape[0]
    tensor_count = lax.axis_size("tensor")
    data_count = lax.axis_size("dp")
    pair = tensor_count == 2
    ring_count = data_count // QUAD
    col_width = MODEL_WIDTH // tensor_count
    half_width = MODEL_WIDTH // 2
    side = lax.axis_index("tensor")
    col_start = side * col_width
    place_dp = lax.axis_index("dp")
    flip = side.astype(jnp.int32) if pair else jnp.int32(0)
    flip_arr = jnp.stack([flip, place_dp.astype(jnp.int32)])
    shard_local_width = query_weight_matrix.shape[1]
    local_experts = expert_gate_weight.shape[0]
    expert_total = local_experts * data_count
    capacity = 5 * tok_count * TOP // (4 * expert_total)
    token_ids = jnp.arange(tok_count, dtype=jnp.int32)
    positions = token_ids % LEN

    def to_sides(full):
        if pair:
            low_cols, high_cols = full[:, :half_width], full[:, half_width:]
            return (
                jnp.where(flip == 0, low_cols, high_cols),
                jnp.where(flip == 0, high_cols, low_cols),
            )
        return full[:, :half_width], full[:, half_width:]

    def from_sides(first, second):
        if pair:
            return jnp.concatenate(
                [jnp.where(flip == 0, first, second), jnp.where(flip == 0, second, first)], axis=1
            )
        return jnp.concatenate([first, second], axis=1)

    routes_t = routes.T
    expert_ids = jnp.arange(expert_total, dtype=jnp.int32)
    chosen_mask = jnp.any(routes_t[:, None, :] == expert_ids[None, :, None], axis=0)
    earlier = (token_ids[:, None] < token_ids[None, :]).astype(half_type)
    rank = jnp.dot(chosen_mask.astype(half_type), earlier, preferred_element_type=jnp.float32)
    place_own = jnp.where(chosen_mask, rank, -1.0).astype(jnp.int32)
    number = jnp.broadcast_to(sequence_adapter_index[:1, None], (data_count, 1, tok_count))
    place_own = jnp.concatenate(
        [place_own.reshape(data_count, local_experts, tok_count), number], axis=1
    )
    place_all = lax.all_to_all(place_own, "dp", 0, 0, tiled=True)
    numbers = place_all[:, local_experts, 0]
    place_all = place_all[:, :local_experts]
    ring_at, quad_at = place_dp // QUAD, place_dp % QUAD
    group_ids = jnp.arange(data_count, dtype=jnp.int32)
    order = ((ring_at - group_ids // QUAD) % ring_count) * QUAD + (quad_at ^ (group_ids % QUAD))
    place_all = place_all[order]
    target_all = jnp.where(
        place_all >= 0,
        place_all + capacity * jnp.arange(local_experts, dtype=jnp.int32)[None, :, None],
        -1,
    ).transpose(0, 2, 1)

    def group_of(values, j):
        return values[j * QUAD : (j + 1) * QUAD]

    adapter = sequence_adapter_index[0]

    def own_adapter(factors, axis):
        return lax.dynamic_index_in_dim(factors, adapter, axis, keepdims=False)

    down_rows = own_adapter(adapter_projection_down.transpose(0, 1, 3, 2), 1)
    down_rows = down_rows.reshape(3 * ADAPTER_RANK, MODEL_WIDTH)
    up_rows = own_adapter(adapter_projection_up, 1)
    out_down_rows = own_adapter(adapter_output_down.transpose(0, 2, 1), 0)
    out_up_rows = own_adapter(adapter_output_up, 0)
    doc_flat = segments.reshape(-1)
    hidden32 = layer_input.astype(jnp.float32)
    hidden_scale = lax.rsqrt(
        jnp.mean(hidden32 * hidden32, axis=-1, keepdims=True) + norm_eps
    )
    normed = (hidden32 * hidden_scale * attention_norm_gain).astype(half_type)
    w_proj = [query_weight_matrix, key_weight_matrix, value_weight_matrix]
    latents = nt_dot(normed, down_rows).astype(half_type)
    latents = [latents[:, p * ADAPTER_RANK : (p + 1) * ADAPTER_RANK] for p in range(3)]
    raw_proj = [
        jnp.dot(normed, w_proj[p], preferred_element_type=jnp.float32)
        + jnp.dot(latents[p], up_rows[p], preferred_element_type=jnp.float32)
        for p in range(3)
    ]
    g_all = lax.all_gather(cotangent, ("dp", "tensor"), axis=0)
    g_all = g_all.reshape(data_count, tensor_count, tok_count, col_width)
    raw_proj[0], place_all, target_all = fence(raw_proj[0], place_all, target_all)
    head_shared = [
        *rotation(positions),
        query_norm_gain[None, :],
        key_norm_gain[None, :],
        doc_flat[:, None],
        doc_flat[None, :],
    ]
    attended, queries, keys, values = call_heads(
        attend_kernel, "attend", raw_proj, head_shared, 4
    )
    proj_part = jnp.dot(attended, output_weight_matrix, preferred_element_type=jnp.float32)
    latent_part = nt_dot(attended, out_down_rows)

    def tensor_sum(part):
        if pair:
            return part.astype(jnp.float32) + other_side(part).astype(jnp.float32)
        return lax.psum(part, "tensor").astype(jnp.float32)

    def split_columns(part):
        if pair:
            mine, theirs = to_sides(part)
            return mine.astype(jnp.float32), theirs.astype(half_type)
        return None, part.astype(half_type)

    def join_columns(mine, theirs):
        if pair:
            return mine + other_side(theirs).astype(jnp.float32)
        return lax.psum_scatter(theirs, "tensor", scatter_dimension=1, tiled=True).astype(
            jnp.float32
        )

    def own_columns(part):
        return join_columns(*split_columns(part))

    def columns_of(full):
        if pair:
            return to_sides(full)[0]
        return lax.dynamic_slice_in_dim(full, col_start, col_width, full.ndim - 1)

    def both_halves(cols):
        if pair:
            return cols, other_side(cols)
        full = lax.all_gather(cols, "tensor", axis=1, tiled=True)
        return full[:, :half_width], full[:, half_width:]

    attn_cols = own_columns(proj_part)
    latent_total = tensor_sum(latent_part.astype(half_type))
    latent_out = latent_total.astype(half_type)
    mixed_cols = (
        columns_of(layer_input).astype(jnp.float32)
        + attn_cols
        + jnp.dot(latent_out, columns_of(out_up_rows), preferred_element_type=jnp.float32)
    )
    expert_gain_cols = columns_of(expert_norm_gain[None, :])
    square_sum = tensor_sum(jnp.sum(mixed_cols * mixed_cols, axis=1, keepdims=True))
    mixed_scale = lax.rsqrt(square_sum / MODEL_WIDTH + norm_eps)
    moe_cols_in = (mixed_cols * mixed_scale * expert_gain_cols).astype(half_type)

    def gates_of(first, second):
        moe_in = from_sides(first, second)
        logits_t = lax.dot_general(
            router, moe_in, (((0,), (1,)), ((), ())), preferred_element_type=jnp.float32
        )
        top_logit = jnp.max(jnp.where(chosen_mask, logits_t, -jnp.inf), axis=0, keepdims=True)
        gate_exp = jnp.where(chosen_mask, jnp.exp(jnp.minimum(logits_t - top_logit, 0.0)), 0.0)
        return gate_exp / jnp.sum(gate_exp, axis=0, keepdims=True)

    def experts_of(k, pieces):
        return call_experts(
            k,
            flip_arr,
            group_of(place_all, k)[:, :, None, :],
            group_of(gates_all, k)[:, :, None, :],
            group_of(target_all, k),
            expert_gate_weight,
            expert_up_weight,
            d_raw[0],
            pieces,
            capacity,
            expert_total * tok_count // half_width,
        )

    def outputs_of(k, hidden):
        return call_output(
            flip_arr,
            group_of(target_all, k),
            expert_down_weight,
            hidden,
            capacity,
            half_width,
        )

    quads = ring_count
    own0, own1, core0, core1 = ([None] * quads for _ in range(4))
    af, asec, ff, fs = ([None] * quads for _ in range(4))
    d_raw = [None]
    hidden = [None] * quads

    def make_sums():
        return {
            name: [None] * quads for name in ("send", "keep", "got", "near", "side_got", "arrived")
        }

    flat_groups = {"grads": (), "outs": (2,)} if pair else {"grads": range(4), "outs": range(4)}

    grads, outs = make_sums(), make_sums()

    def move_first(j):
        own0[j + 1] = onward(own0[j], data_count)

    def move_second(j):
        own1[j + 1] = onward(own1[j], data_count)

    def send_across(j):
        af[j] = swap(own0[j], data_count, 2)
        core0[j] = swap(own0[j], data_count, 1)

    def send_rest(j):
        asec[j] = (
            other_side(af[j]) if pair else swap(own1[j], data_count, 2)
        )
        core1[j] = swap(own1[j], data_count, 1)
        ff[j] = swap(af[j], data_count, 1)

    def send_last(j):
        fs[j] = swap(asec[j], data_count, 1)

    def run_experts(k):
        pieces = [own0[k], own1[k], core0[k], core1[k], af[k], asec[k], ff[k], fs[k]]
        grads["send"][k], grads["keep"][k], hidden[k] = experts_of(k, pieces)

    def run_outputs(k):
        outs["send"][k], outs["keep"][k] = outputs_of(k, hidden[k])

    def is_flat(sums, k):
        return k in flat_groups["grads" if sums is grads else "outs"]

    def sum_cores(sums, k):
        sums["got"][k] = swap(sums["send"][k], data_count, 1)

    def sum_sides(sums, k):
        keep, got = sums["keep"][k], sums["got"][k]
        away = plus(keep[1, 1], got[1, 1])
        sums["side_got"][k] = swap(away, data_count, 2) if is_flat(sums, k) else other_side(away)
        sums["near"][k] = plus(keep[1, 0], got[1, 0])

    def sum_across(sums, k):
        near = sums["near"][k]
        if not is_flat(sums, k):
            near = plus(near, sums["side_got"][k])
        sums["arrived"][k] = swap(near, data_count, 2)

    def first_of(sums, k):
        return [sums["keep"][k][0, 0], sums["got"][k][0, 0], sums["arrived"][k]]

    def second_of(sums, k):
        terms = [sums["keep"][k][0, 1], sums["got"][k][0, 1]]
        return terms + [sums["side_got"][k]] if is_flat(sums, k) else terms

    def onward_sum(*terms):
        return onward(plus(*terms), data_count)

    def step_end(*more):
        groups = (
            own0, own1, core0, core1, af, asec, ff, fs, d_raw, hidden,
            *grads.values(), *outs.values(),
        )
        fenced = fence(groups, more)
        for old, fresh in zip(groups, fenced[0]):
            old[:] = fresh
        return fenced[1]

    own0[0] = moe_cols_in if pair else both_halves(moe_cols_in)[0]
    own1[0] = both_halves(moe_cols_in)[1]
    move_first(0)
    send_across(0)
    step_end()
    gates_t = gates_of(own0[0], own1[0])
    gates_all = lax.all_to_all(
        gates_t.reshape(data_count, local_experts, tok_count), "dp", 0, 0, tiled=True
    )[order]
    move_second(0)
    send_rest(0)
    send_across(1)
    gates_t, gates_all = step_end(gates_t, gates_all)
    move_first(1)
    send_rest(1)
    send_last(0)
    d_raw[0] = call_grad_rows(
        order, place_all[:, :, None, :], expert_down_weight, g_all, capacity
    )
    step_end()
    move_second(1)
    send_across(2)
    send_last(1)
    run_experts(1)
    step_end()
    move_first(2)
    send_rest(2)
    sum_cores(grads, 1)
    run_experts(0)
    step_end()
    move_second(2)
    send_across(3)
    send_last(2)
    sum_sides(grads, 1)
    sum_cores(grads, 0)
    run_experts(2)
    step_end()
    second = onward_sum(*second_of(grads, 1))
    send_rest(3)
    sum_across(grads, 1)
    sum_cores(grads, 2)
    run_outputs(1)
    (second,) = step_end(second)
    send_last(3)
    sum_sides(grads, 2)
    second = onward_sum(second, *second_of(grads, 2))
    run_experts(3)
    (second,) = step_end(second)
    first = onward_sum(*first_of(grads, 1))
    sum_across(grads, 2)
    sum_sides(grads, 0)
    sum_cores(grads, 3)
    sum_cores(outs, 1)
    run_outputs(2)
    first, second = step_end(first, second)
    first = onward_sum(first, *first_of(grads, 2))
    sum_sides(grads, 3)
    sum_across(grads, 0)
    sum_cores(outs, 2)
    run_outputs(3)
    if pair:
        second = plus(second, *second_of(grads, 3))
    first, second = step_end(first, second)
    if not pair:
        second = plus(second, *second_of(grads, 3))
    second = onward(second, data_count)
    sum_across(grads, 3)
    sum_cores(outs, 3)
    sum_sides(outs, 1)
    run_outputs(0)
    first, second = step_end(first, plus(second, *second_of(grads, 0)))
    first = onward_sum(first, *first_of(grads, 3))
    sum_cores(outs, 0)
    sum_across(outs, 1)
    if pair:
        from_other = other_side(second).astype(jnp.float32)
        grad_moe_cols = first.astype(jnp.float32) + from_other
        for term in first_of(grads, 0):
            grad_moe_cols += term.astype(jnp.float32)
    else:
        first = plus(first, *first_of(grads, 0))
        grad_gates = tensor_sum(first[tok_count:])
        grad_moe_cols = own_columns(from_sides(first[:tok_count], second[:tok_count]))
        grad_moe_cols = jnp.pad(grad_moe_cols, ((0, 0), (0, half_width - col_width)))
        grad_moe_cols = jnp.concatenate([grad_moe_cols, grad_gates], axis=0)
    (grad_moe_cols,) = step_end(grad_moe_cols)
    sum_sides(outs, 2)
    out_second = onward_sum(*second_of(outs, 1))
    d_gate_home = grad_moe_cols[tok_count:].reshape(expert_total, tok_count)
    grad_moe_cols = grad_moe_cols[:tok_count, :col_width]

    weighted = gates_t * d_gate_home
    grad_logits_t = (
        gates_t * (d_gate_home - jnp.sum(weighted, axis=0, keepdims=True))
    ).astype(half_type)
    router_cols = router.T
    grad_moe_cols = grad_moe_cols + lax.dot_general(
        grad_logits_t,
        columns_of(router_cols),
        (((0,), (0,)), ((), ())),
        preferred_element_type=jnp.float32,
    )
    along = tensor_sum(
        jnp.sum(mixed_cols * expert_gain_cols * grad_moe_cols, axis=1, keepdims=True)
    )
    grad_mixed_cols = (
        cotangent.astype(jnp.float32)
        + expert_gain_cols * mixed_scale * grad_moe_cols
        - mixed_cols * (mixed_scale * mixed_scale * mixed_scale * (along / MODEL_WIDTH))
    )
    branch_cols = grad_mixed_cols.astype(half_type)
    grad_branch = from_sides(*both_halves(branch_cols))
    grad_branch, out_second = step_end(grad_branch, out_second)
    out_first = onward_sum(*first_of(outs, 1))
    sum_across(outs, 2)
    out_second = onward_sum(out_second, *second_of(outs, 2))
    sum_sides(outs, 3)

    grad_latent_out = nt_dot(grad_branch, out_up_rows).astype(half_type)
    grad_up_out = lax.dot_general(
        latent_out, branch_cols, (((0,), (0,)), ((), ())), preferred_element_type=jnp.float32
    )
    grad_attended = nt_dot(grad_branch, output_weight_matrix) + jnp.dot(
        grad_latent_out, out_down_rows, preferred_element_type=jnp.float32
    )
    grad_heads = grad_attended.astype(half_type)
    grad_down_out = lax.dot_general(
        grad_latent_out, attended, (((0,), (0,)), ((), ())), preferred_element_type=jnp.float32
    )

    grad_raw = call_heads(
        attend_back_kernel,
        "attend_back",
        [raw_proj[0], raw_proj[1], queries, keys, values, grad_heads],
        head_shared,
        3,
    )
    grad_raw, out_first, out_second = step_end(grad_raw, out_first, out_second)
    out_first = onward_sum(out_first, *first_of(outs, 2))
    sum_sides(outs, 0)
    sum_across(outs, 3)
    latent_parts = jnp.concatenate([nt_dot(grad_raw[p], up_rows[p]) for p in range(3)], axis=1)
    grad_latent = tensor_sum(latent_parts.astype(half_type)).astype(half_type)
    grad_up = [
        lax.dot_general(
            latents[p], grad_raw[p], (((0,), (0,)), ((), ())), preferred_element_type=jnp.float32
        )
        for p in range(3)
    ]
    grad_down = lax.dot_general(
        grad_latent, normed, (((0,), (0,)), ((), ())), preferred_element_type=jnp.float32
    )
    parts = [grad_down_out, grad_up_out] + grad_up
    parts += [
        grad_down[:, i * shard_local_width : (i + 1) * shard_local_width]
        for i in range(tensor_count)
    ]
    parts = jnp.concatenate([part.astype(half_type) for part in parts], axis=0)
    parts_all = lax.all_gather(parts, "dp", axis=0)
    holds = numbers[None, :] == jnp.arange(ADAPTER_CHOICES, dtype=jnp.int32)[:, None]
    adapter_sums = jnp.einsum(
        "as,src->arc", holds.astype(half_type), parts_all, preferred_element_type=jnp.float32
    )

    def rows_at(i):
        return adapter_sums[:, i * ADAPTER_RANK : (i + 1) * ADAPTER_RANK]

    sum_up_qkv = jnp.stack([rows_at(2 + p) for p in range(3)])
    sum_down_qkv = jnp.stack(
        [
            jnp.concatenate([rows_at(5 + 3 * i + p) for i in range(tensor_count)], axis=2)
            for p in range(3)
        ]
    ).transpose(0, 1, 3, 2)

    grad_normed_part = nt_dot(grad_raw[0], w_proj[0])
    grad_normed_part += nt_dot(grad_raw[1], w_proj[1])
    grad_normed_part += nt_dot(grad_raw[2], w_proj[2])
    grad_normed_mine, grad_normed_other = split_columns(grad_normed_part)
    grad_normed_other, out_first = step_end(grad_normed_other, out_first)
    out_second = onward_sum(out_second, *second_of(outs, 3))
    sum_across(outs, 0)
    grad_normed_cols = join_columns(grad_normed_mine, grad_normed_other)
    grad_normed_cols, out_second = step_end(grad_normed_cols, out_second)
    out_first = plus(onward_sum(out_first, *first_of(outs, 3)), *first_of(outs, 0))
    out_second = plus(out_second, *second_of(outs, 0))
    if pair:
        moe_cols = out_first.astype(jnp.float32) + other_side(out_second).astype(jnp.float32)
    else:
        moe_cols = own_columns(from_sides(out_first, out_second))
    layer_out = (mixed_cols + moe_cols).astype(half_type)
    grad_normed_cols += jnp.dot(
        grad_latent, columns_of(down_rows), preferred_element_type=jnp.float32
    )
    attention_gain_cols = columns_of(attention_norm_gain[None, :])
    hidden_cols = columns_of(layer_input).astype(jnp.float32)
    along_in = tensor_sum(
        jnp.sum(hidden_cols * attention_gain_cols * grad_normed_cols, axis=1, keepdims=True)
    )
    grad_input = (
        grad_mixed_cols
        + attention_gain_cols * hidden_scale * grad_normed_cols
        - hidden_cols * (hidden_scale * hidden_scale * hidden_scale * (along_in / MODEL_WIDTH))
    )
    return (
        layer_out,
        grad_input,
        sum_down_qkv,
        sum_up_qkv,
        rows_at(0).transpose(0, 2, 1),
        rows_at(1),
    )


def solution(mesh):
    return jax.shard_map(
        local,
        mesh=mesh,
        in_specs=(
            P("dp", None),
            P("dp", "tensor"),
            P(),
            P(),
            P(),
            P(),
            P(None, "tensor"),
            P(None, "tensor"),
            P(None, "tensor"),
            P("tensor", None),
            P(),
            P(None, None, None, "tensor"),
            P(None, "tensor", None),
            P(),
            P(),
            P("dp", None, "tensor"),
            P("dp", None, "tensor"),
            P("dp", "tensor", None),
            P("dp", None),
            P("dp"),
            P("dp", None),
        ),
        out_specs=(
            P("dp", "tensor"),
            P("dp", "tensor"),
            P(),
            P(None, None, None, "tensor"),
            P(None, "tensor", None),
            P(None, None, "tensor"),
        ),
        check_vma=False,
    )
```

```python
import functools

import jax
import jax.numpy as jnp
from jax import lax
from jax.experimental import pallas as pl
from jax.experimental.pallas import tpu as pltpu
from jax.sharding import PartitionSpec as P

MODEL_WIDTH = 2048
HEAD_WIDTH = 128
TOP = 8
LEN = 512
ADAPTER_RANK = 16
ADAPTER_CHOICES = 8
QUAD = 4

norm_eps = 1e-05
head_eps = 1e-06
rope_base = 50000.0
half_type = jnp.bfloat16
VMEM_LIMIT = 56 * 1024 * 1024


def rotation(positions):
    half_dim = HEAD_WIDTH // 2
    inverse = rope_base ** (-(jnp.arange(half_dim, dtype=jnp.float32) * 2.0 / HEAD_WIDTH))
    angles = positions.astype(jnp.float32)[:, None] * inverse[None, :]
    cosine, sine = jnp.cos(angles), jnp.sin(angles)
    return (
        jnp.concatenate([cosine, cosine], axis=1),
        jnp.concatenate([-sine, sine], axis=1),
    )


def nt_dot(left, right):
    return lax.dot_general(
        left, right, (((1,), (1,)), ((), ())), preferred_element_type=jnp.float32
    )


def tn_dot(left, right):
    return lax.dot_general(
        left, right, (((0,), (0,)), ((), ())), preferred_element_type=jnp.float32
    )


def head_prep(raw, gain, cosine, sine):
    scale = lax.rsqrt(jnp.mean(raw * raw, axis=-1, keepdims=True) + head_eps)
    scaled = raw * scale * gain
    return scaled * cosine + pltpu.roll(scaled, HEAD_WIDTH // 2, 1) * sine


def head_prep_back(grad, raw, gain, cosine, sine):
    scale = lax.rsqrt(jnp.mean(raw * raw, axis=-1, keepdims=True) + head_eps)
    turned = (grad * cosine - pltpu.roll(grad, HEAD_WIDTH // 2, 1) * sine) * gain
    along = jnp.mean(raw * turned, axis=-1, keepdims=True)
    return scale * turned - raw * (scale * scale * scale * along)


def masked_exp(queries, keys, docs_col, docs_row):
    scores = nt_dot(queries, keys) * HEAD_WIDTH ** (-0.5)
    scores = jnp.where(docs_col == docs_row, scores, -1e30)
    exp_scores = jnp.exp(scores - jnp.max(scores, axis=-1, keepdims=True))
    return exp_scores, jnp.sum(exp_scores, axis=-1, keepdims=True)


def attend_kernel(
    raw_q, raw_k, raw_v, cosine, sine, gain_q, gain_k, docs_col, docs_row, out, queries, keys, values
):
    q = head_prep(raw_q[...], gain_q[...], cosine[...], sine[...]).astype(half_type)
    k = head_prep(raw_k[...], gain_k[...], cosine[...], sine[...]).astype(half_type)
    v = raw_v[...].astype(half_type)
    queries[...], keys[...], values[...] = q, k, v
    exp_scores, total = masked_exp(q, k, docs_col[...], docs_row[...])
    probs = (exp_scores / total).astype(half_type)
    out[...] = jnp.dot(probs, v, preferred_element_type=jnp.float32).astype(half_type)


def attend_back_kernel(
    raw_q, raw_k, queries, keys, values, grad, cosine, sine, gain_q, gain_k, docs_col, docs_row,
    grad_q, grad_k, grad_v,
):
    q, k, v, g = queries[...], keys[...], values[...], grad[...]
    score_scale = HEAD_WIDTH ** (-0.5)
    exp_scores, total = masked_exp(q, k, docs_col[...], docs_row[...])
    probs = exp_scores / total
    grad_v[...] = tn_dot(probs.astype(half_type), g).astype(half_type)
    grad_probs = nt_dot(g, v)
    delta = jnp.sum(probs * grad_probs, axis=-1, keepdims=True)
    grad_scores = (probs * (grad_probs - delta)).astype(half_type)
    d_q = jnp.dot(grad_scores, k, preferred_element_type=jnp.float32) * score_scale
    d_k = tn_dot(grad_scores, q) * score_scale
    grad_q[...] = head_prep_back(d_q, raw_q[...], gain_q[...], cosine[...], sine[...]).astype(
        half_type
    )
    grad_k[...] = head_prep_back(d_k, raw_k[...], gain_k[...], cosine[...], sine[...]).astype(
        half_type
    )


def call_heads(kernel, name, by_head, shared, out_count):
    toks, width = by_head[0].shape
    head = pl.BlockSpec((toks, HEAD_WIDTH), lambda h: (0, h))
    return pl.pallas_call(
        kernel,
        out_shape=[jax.ShapeDtypeStruct((toks, width), half_type)] * out_count,
        grid=(width // HEAD_WIDTH,),
        in_specs=[head] * len(by_head)
        + [pl.BlockSpec(v.shape, lambda h: (0, 0)) for v in shared],
        out_specs=[head] * out_count,
        compiler_params=pltpu.CompilerParams(
            dimension_semantics=("arbitrary",), vmem_limit_bytes=VMEM_LIMIT
        ),
        cost_estimate=pl.CostEstimate(
            flops=10 * toks * toks * width, bytes_accessed=8 * toks * width, transcendentals=toks * toks
        ),
        name=name,
    )(*by_head, *shared)


def start_blocks(pieces, buffer_ref, sems, flip):
    for b in range(QUAD):
        for r in range(2):
            pltpu.make_async_copy(
                pieces[2 * b + r], buffer_ref.at[b, r ^ flip], sems.at[b, r]
            ).start()


def wait_block(pieces, buffer_ref, sems, b):
    for r in range(2):
        pltpu.make_async_copy(pieces[0], buffer_ref.at[b, r], sems.at[b, r]).wait()


def pick_rows(place_ref, half_at, rows_ref, b, experts, cap, tile):
    toks = half_at(0).shape[0]
    slot = lax.broadcasted_iota(jnp.int32, (cap, toks), 0)
    picks = jnp.concatenate(
        [jnp.where(slot == place_ref[b, e], 1.0, 0.0) for e in range(experts)], axis=0
    ).astype(half_type)
    half = rows_ref.shape[4]

    for h in range(rows_ref.shape[1]):
        for start in range(0, half, tile):
            rows = jnp.dot(
                picks,
                half_at(h)[:, start : start + tile],
                preferred_element_type=jnp.float32,
            ).astype(half_type)
            for e in range(experts):
                rows_ref[e, h, b, :, start : start + tile] = rows[e * cap : (e + 1) * cap]


def add_rows(target_ref, rows_ref, out_ref, b, flip, experts, cap, tile):
    target = target_ref[b]
    toks = target.shape[0]
    lane = lax.broadcasted_iota(jnp.int32, (toks, experts * cap), 1)
    hit = lane == target[:, 0:1]
    for e in range(1, experts):
        hit = jnp.logical_or(hit, lane == target[:, e : e + 1])
    spread = jnp.where(hit, 1.0, 0.0).astype(half_type)
    half = rows_ref.shape[4]

    for h in range(2):
        for start in range(0, half, tile):
            rows = jnp.concatenate(
                [rows_ref[e, h, b, :, start : start + tile] for e in range(experts)], axis=0
            )
            out_ref[0, h ^ flip, :toks, start : start + tile] = jnp.dot(
                spread, rows, preferred_element_type=jnp.float32
            ).astype(half_type)


def add_gates(dgate_ref, out_ref, b, device, experts):
    toks, half = dgate_ref.shape[3], out_ref.shape[3]
    extra = out_ref.shape[2] - toks
    per_row = half // toks
    row = lax.broadcasted_iota(jnp.int32, (extra, half), 0)
    values = jnp.zeros((extra, half), jnp.float32)
    for i in range(experts // per_row):
        line = jnp.concatenate(
            [dgate_ref[i * per_row + n, b] for n in range(per_row)], axis=1
        )
        values = jnp.where(row == device * (experts // per_row) + i, line, values)
    for h in range(2):
        out_ref[0, h, toks:, :] = values.astype(half_type)


def grad_rows_kernel(experts, cap, block_ids, place_ref, down_ref, block_ref, out_ref, rows_ref):
    step = pl.program_id(0)
    sides, blocks, part = rows_ref.shape[1], rows_ref.shape[2], rows_ref.shape[4]

    @pl.when(step < blocks)
    def _():
        pick_rows(
            place_ref,
            lambda h: block_ref.at[0, h],
            rows_ref,
            step,
            experts,
            cap,
            min(part, 512),
        )

    @pl.when(step >= blocks)
    def _():
        e = step - blocks
        total = nt_dot(rows_ref[e, 0].reshape(blocks * cap, part), down_ref[0, :, :part])
        for h in range(1, sides):
            total += nt_dot(
                rows_ref[e, h].reshape(blocks * cap, part),
                down_ref[0, :, h * part : (h + 1) * part],
            )
        out_ref[0] = total.astype(half_type)


def expert_kernel(
    experts,
    cap,
    flip_ref,
    place_ref,
    gate_ref,
    target_ref,
    wg_ref,
    wu_ref,
    dh_ref,
    own_first_ref,
    own_second_ref,
    core_first_ref,
    core_second_ref,
    across_first_ref,
    across_second_ref,
    far_first_ref,
    far_second_ref,
    send_ref,
    keep_ref,
    hidden_ref,
    buffer_ref,
    rows_ref,
    dgate_ref,
    wg_buffer,
    wu_buffer,
    sems,
    weight_sems,
):
    block_refs = [
        own_first_ref,
        own_second_ref,
        core_first_ref,
        core_second_ref,
        across_first_ref,
        across_second_ref,
        far_first_ref,
        far_second_ref,
    ]
    step = pl.program_id(0)
    half = buffer_ref.shape[3]
    toks = buffer_ref.shape[2]

    def weight_copies(e):
        return (
            pltpu.make_async_copy(wg_ref.at[e], wg_buffer.at[e], weight_sems.at[e, 0]),
            pltpu.make_async_copy(wu_ref.at[e], wu_buffer.at[e], weight_sems.at[e, 1]),
        )

    @pl.when(step == 0)
    def _():
        start_blocks(block_refs, buffer_ref, sems, flip_ref[0])

    @pl.when(step < experts)
    def _():
        for copy in weight_copies(step):
            copy.start()

    @pl.when(step < QUAD)
    def _():
        wait_block(block_refs, buffer_ref, sems, step)
        pick_rows(
            place_ref, lambda h: buffer_ref.at[step, h], rows_ref, step, experts, cap, 512
        )

    @pl.when(jnp.logical_and(step >= QUAD, step < QUAD + experts))
    def _():
        e = step - QUAD
        for copy in weight_copies(e):
            copy.wait()
        first = rows_ref[e, 0].reshape(QUAD * cap, half)
        second = rows_ref[e, 1].reshape(QUAD * cap, half)
        pre_gate = jnp.dot(first, wg_buffer[e, :half], preferred_element_type=jnp.float32)
        pre_gate += jnp.dot(second, wg_buffer[e, half:], preferred_element_type=jnp.float32)
        pre_up = jnp.dot(first, wu_buffer[e, :half], preferred_element_type=jnp.float32)
        pre_up += jnp.dot(second, wu_buffer[e, half:], preferred_element_type=jnp.float32)
        sig = lax.logistic(pre_gate)
        silu = pre_gate * sig
        act = silu * pre_up
        d_raw = dh_ref[0].astype(jnp.float32)
        slot = lax.broadcasted_iota(jnp.int32, (cap, toks), 0)
        gate_parts = []
        for b in range(QUAD):
            hit = slot == place_ref[b, e]
            gate_parts.append(
                jnp.sum(jnp.where(hit, gate_ref[b, e], 0.0), axis=1, keepdims=True)
            )
        gate_col = jnp.concatenate(gate_parts, axis=0)
        hidden_ref[0] = (act * gate_col).astype(half_type)
        d_col = jnp.sum(act * d_raw, axis=1, keepdims=True)
        for b in range(QUAD):
            hit = slot == place_ref[b, e]
            dgate_ref[e, b] = jnp.sum(
                jnp.where(hit, d_col[b * cap : (b + 1) * cap], 0.0), axis=0, keepdims=True
            )
        d_hidden = d_raw * gate_col
        d_up = (d_hidden * silu).astype(half_type)
        d_gate = (d_hidden * pre_up * (sig * (1.0 + pre_gate * (1.0 - sig)))).astype(half_type)
        for h in range(2):
            d_in = nt_dot(d_gate, wg_buffer[e, h * half : (h + 1) * half])
            d_in += nt_dot(d_up, wu_buffer[e, h * half : (h + 1) * half])
            rows_ref[e, h] = d_in.astype(half_type).reshape(QUAD, cap, half)

    for which, out_ref in ((0, send_ref), (1, keep_ref)):
        first_step = QUAD + experts + 2 * which

        @pl.when(jnp.logical_and(step >= first_step, step < first_step + 2))
        def _():
            b = 2 * (step - first_step) + 1 - which
            add_rows(target_ref, rows_ref, out_ref, b, flip_ref[0], experts, cap, 512)
            add_gates(dgate_ref, out_ref, b, flip_ref[1], experts)


def output_kernel(
    experts,
    cap,
    flip_ref,
    target_ref,
    down_ref,
    hidden_ref,
    send_ref,
    keep_ref,
    rows_ref,
    down_buffer,
    weight_sems,
):
    step = pl.program_id(0)
    half = rows_ref.shape[4]

    def weight_copy(e):
        return pltpu.make_async_copy(down_ref.at[e], down_buffer.at[e], weight_sems.at[e])

    @pl.when(step == 0)
    def _():
        for e in range(experts):
            weight_copy(e).start()

    @pl.when(step < experts)
    def _():
        weight_copy(step).wait()
        for h in range(2):
            out = jnp.dot(
                hidden_ref[step],
                down_buffer[step, :, h * half : (h + 1) * half],
                preferred_element_type=jnp.float32,
            )
            rows_ref[step, h] = out.astype(half_type).reshape(QUAD, cap, half)

    for which, out_ref in ((0, send_ref), (1, keep_ref)):
        first_step = experts + 2 * which

        @pl.when(jnp.logical_and(step >= first_step, step < first_step + 2))
        def _():
            b = 2 * (step - first_step) + 1 - which
            add_rows(target_ref, rows_ref, out_ref, b, flip_ref[0], experts, cap, 512)


def whole(shape):
    return pl.BlockSpec(shape, lambda i, *_: (0,) * len(shape), pipeline_mode=pl.Buffered(1))


def per_step(shape, first, count):
    return pl.BlockSpec(
        (1,) + shape[1:], lambda i, *_: (jnp.clip(i - first, 0, count - 1),) + (0,) * (len(shape) - 1)
    )


def call_grad_rows(block_ids, place, down, blocks, cap):
    experts, hidden_units, width = down.shape
    count, sides, toks, half = blocks.shape
    rows = count * cap
    return pl.pallas_call(
        functools.partial(grad_rows_kernel, experts, cap),
        out_shape=jax.ShapeDtypeStruct((experts, rows, hidden_units), half_type),
        grid_spec=pltpu.PrefetchScalarGridSpec(
            num_scalar_prefetch=1,
            grid=(count + experts,),
            in_specs=[
                whole(place.shape),
                per_step(down.shape, count, experts),
                pl.BlockSpec(
                    (1, sides, toks, half),
                    lambda i, ids: (ids[jnp.minimum(i, count - 1)], 0, 0, 0),
                ),
            ],
            out_specs=per_step((experts, rows, hidden_units), count, experts),
            scratch_shapes=[pltpu.VMEM((experts, sides, count, cap, half), half_type)],
        ),
        compiler_params=pltpu.CompilerParams(
            dimension_semantics=("arbitrary",), vmem_limit_bytes=VMEM_LIMIT
        ),
        cost_estimate=pl.CostEstimate(
            flops=4 * experts * rows * width * (toks + hidden_units),
            bytes_accessed=2 * (down.size + blocks.size + experts * rows * hidden_units),
            transcendentals=0,
        ),
        name="grad_rows",
    )(block_ids, place, down, blocks)


def call_experts(group, flip, place, gate, target, gate_w, up_w, d_raw, pieces, cap, extra):
    experts, width, hidden_units = gate_w.shape
    toks, half = pieces[0].shape
    rows = QUAD * cap
    blocks = (2, 2, toks + extra, half)
    return pl.pallas_call(
        functools.partial(expert_kernel, experts, cap),
        out_shape=(
            jax.ShapeDtypeStruct(blocks, half_type),
            jax.ShapeDtypeStruct(blocks, half_type),
            jax.ShapeDtypeStruct((experts, rows, hidden_units), half_type),
        ),
        grid_spec=pltpu.PrefetchScalarGridSpec(
            num_scalar_prefetch=1,
            grid=(2 * QUAD + experts,),
            in_specs=[
                whole(place.shape),
                whole(gate.shape),
                whole(target.shape),
                pl.BlockSpec(memory_space=pl.ANY),
                pl.BlockSpec(memory_space=pl.ANY),
                pl.BlockSpec(
                    (1, rows, hidden_units),
                    lambda i, *_: (jnp.clip(i - QUAD, 0, experts - 1), group, 0),
                ),
            ]
            + [pl.BlockSpec(memory_space=pl.ANY)] * len(pieces),
            out_specs=(
                per_step(blocks, QUAD + experts, 2),
                per_step(blocks, QUAD + experts + 2, 2),
                per_step((experts, rows, hidden_units), QUAD, experts),
            ),
            scratch_shapes=[
                pltpu.VMEM((QUAD, 2, toks, half), half_type),
                pltpu.VMEM((experts, 2, QUAD, cap, half), half_type),
                pltpu.VMEM((experts, QUAD, 1, toks), jnp.float32),
                pltpu.VMEM(gate_w.shape, half_type),
                pltpu.VMEM(up_w.shape, half_type),
                pltpu.SemaphoreType.DMA((QUAD, 2)),
                pltpu.SemaphoreType.DMA((experts, 2)),
            ],
        ),
        compiler_params=pltpu.CompilerParams(
            dimension_semantics=("arbitrary",), vmem_limit_bytes=VMEM_LIMIT
        ),
        cost_estimate=pl.CostEstimate(
            flops=6 * experts * rows * width * (toks + 2 * hidden_units),
            bytes_accessed=2 * (2 * gate_w.size + 4 * QUAD * toks * half),
            transcendentals=experts * rows * hidden_units,
        ),
        name="experts",
    )(flip, place, gate, target, gate_w, up_w, d_raw, *pieces)


def call_output(flip, target, down, hidden, cap, half):
    experts, hidden_units, width = down.shape
    toks = target.shape[1]
    rows = QUAD * cap
    blocks = (2, 2, toks, half)
    return pl.pallas_call(
        functools.partial(output_kernel, experts, cap),
        out_shape=(
            jax.ShapeDtypeStruct(blocks, half_type),
            jax.ShapeDtypeStruct(blocks, half_type),
        ),
        grid_spec=pltpu.PrefetchScalarGridSpec(
            num_scalar_prefetch=1,
            grid=(QUAD + experts,),
            in_specs=[
                whole(target.shape),
                pl.BlockSpec(memory_space=pl.ANY),
                whole(hidden.shape),
            ],
            out_specs=(per_step(blocks, experts, 2), per_step(blocks, experts + 2, 2)),
            scratch_shapes=[
                pltpu.VMEM((experts, 2, QUAD, cap, half), half_type),
                pltpu.VMEM(down.shape, half_type),
                pltpu.SemaphoreType.DMA((experts,)),
            ],
        ),
        compiler_params=pltpu.CompilerParams(
            dimension_semantics=("arbitrary",), vmem_limit_bytes=VMEM_LIMIT
        ),
        cost_estimate=pl.CostEstimate(
            flops=4 * experts * rows * width * (toks + hidden_units),
            bytes_accessed=2 * (down.size + 2 * QUAD * toks * half),
            transcendentals=0,
        ),
        name="outputs",
    )(flip, target, down, hidden)


def swap(values, data_count, bit):
    return lax.ppermute(values, "dp", [(i, i ^ bit) for i in range(data_count)])


def onward(values, data_count):
    return lax.ppermute(values, "dp", [(i, (i + QUAD) % data_count) for i in range(data_count)])


def other_side(values):
    return lax.ppermute(values, "tensor", [(0, 1), (1, 0)])


def fence(*values):
    return lax.optimization_barrier(values)


def plus(*terms):
    total = terms[0].astype(jnp.float32)
    for term in terms[1:]:
        total = total + term.astype(jnp.float32)
    return total.astype(half_type)


def local(
    layer_input,
    cotangent,
    attention_norm_gain,
    expert_norm_gain,
    query_norm_gain,
    key_norm_gain,
    query_weight_matrix,
    key_weight_matrix,
    value_weight_matrix,
    output_weight_matrix,
    adapter_projection_down,
    adapter_projection_up,
    adapter_output_down,
    adapter_output_up,
    router,
    expert_gate_weight,
    expert_up_weight,
    expert_down_weight,
    segments,
    sequence_adapter_index,
    routes,
):
    tok_count = layer_input.shape[0]
    tensor_count = lax.axis_size("tensor")
    data_count = lax.axis_size("dp")
    pair = tensor_count == 2
    ring_count = data_count // QUAD
    col_width = MODEL_WIDTH // tensor_count
    half_width = MODEL_WIDTH // 2
    side = lax.axis_index("tensor")
    col_start = side * col_width
    place_dp = lax.axis_index("dp")
    flip = side.astype(jnp.int32) if pair else jnp.int32(0)
    flip_arr = jnp.stack([flip, place_dp.astype(jnp.int32)])
    shard_local_width = query_weight_matrix.shape[1]
    local_experts = expert_gate_weight.shape[0]
    expert_total = local_experts * data_count
    capacity = 5 * tok_count * TOP // (4 * expert_total)
    token_ids = jnp.arange(tok_count, dtype=jnp.int32)
    positions = token_ids % LEN

    def to_sides(full):
        if pair:
            low_cols, high_cols = full[:, :half_width], full[:, half_width:]
            return (
                jnp.where(flip == 0, low_cols, high_cols),
                jnp.where(flip == 0, high_cols, low_cols),
            )
        return full[:, :half_width], full[:, half_width:]

    def from_sides(first, second):
        if pair:
            return jnp.concatenate(
                [jnp.where(flip == 0, first, second), jnp.where(flip == 0, second, first)], axis=1
            )
        return jnp.concatenate([first, second], axis=1)

    routes_t = routes.T
    expert_ids = jnp.arange(expert_total, dtype=jnp.int32)
    chosen_mask = jnp.any(routes_t[:, None, :] == expert_ids[None, :, None], axis=0)
    earlier = (token_ids[:, None] < token_ids[None, :]).astype(half_type)
    rank = jnp.dot(chosen_mask.astype(half_type), earlier, preferred_element_type=jnp.float32)
    place_own = jnp.where(chosen_mask, rank, -1.0).astype(jnp.int32)
    number = jnp.broadcast_to(sequence_adapter_index[:1, None], (data_count, 1, tok_count))
    place_own = jnp.concatenate(
        [place_own.reshape(data_count, local_experts, tok_count), number], axis=1
    )
    place_all = lax.all_to_all(place_own, "dp", 0, 0, tiled=True)
    numbers = place_all[:, local_experts, 0]
    place_all = place_all[:, :local_experts]
    ring_at, quad_at = place_dp // QUAD, place_dp % QUAD
    group_ids = jnp.arange(data_count, dtype=jnp.int32)
    order = ((ring_at - group_ids // QUAD) % ring_count) * QUAD + (quad_at ^ (group_ids % QUAD))
    place_all = place_all[order]
    target_all = jnp.where(
        place_all >= 0,
        place_all + capacity * jnp.arange(local_experts, dtype=jnp.int32)[None, :, None],
        -1,
    ).transpose(0, 2, 1)

    def group_of(values, j):
        return values[j * QUAD : (j + 1) * QUAD]

    adapter = sequence_adapter_index[0]

    def own_adapter(factors, axis):
        return lax.dynamic_index_in_dim(factors, adapter, axis, keepdims=False)

    down_rows = own_adapter(adapter_projection_down.transpose(0, 1, 3, 2), 1)
    down_rows = down_rows.reshape(3 * ADAPTER_RANK, MODEL_WIDTH)
    up_rows = own_adapter(adapter_projection_up, 1)
    out_down_rows = own_adapter(adapter_output_down.transpose(0, 2, 1), 0)
    out_up_rows = own_adapter(adapter_output_up, 0)
    doc_flat = segments.reshape(-1)
    hidden32 = layer_input.astype(jnp.float32)
    hidden_scale = lax.rsqrt(
        jnp.mean(hidden32 * hidden32, axis=-1, keepdims=True) + norm_eps
    )
    normed = (hidden32 * hidden_scale * attention_norm_gain).astype(half_type)
    w_proj = [query_weight_matrix, key_weight_matrix, value_weight_matrix]
    latents = nt_dot(normed, down_rows).astype(half_type)
    latents = [latents[:, p * ADAPTER_RANK : (p + 1) * ADAPTER_RANK] for p in range(3)]
    raw_proj = [
        jnp.dot(normed, w_proj[p], preferred_element_type=jnp.float32)
        + jnp.dot(latents[p], up_rows[p], preferred_element_type=jnp.float32)
        for p in range(3)
    ]
    g_all = lax.all_gather(cotangent, ("dp", "tensor"), axis=0)
    g_all = g_all.reshape(data_count, tensor_count, tok_count, col_width)
    raw_proj[0], place_all, target_all = fence(raw_proj[0], place_all, target_all)
    head_shared = [
        *rotation(positions),
        query_norm_gain[None, :],
        key_norm_gain[None, :],
        doc_flat[:, None],
        doc_flat[None, :],
    ]
    attended, queries, keys, values = call_heads(
        attend_kernel, "attend", raw_proj, head_shared, 4
    )
    proj_part = jnp.dot(attended, output_weight_matrix, preferred_element_type=jnp.float32)
    latent_part = nt_dot(attended, out_down_rows)

    def tensor_sum(part):
        if pair:
            return part.astype(jnp.float32) + other_side(part).astype(jnp.float32)
        return lax.psum(part, "tensor").astype(jnp.float32)

    def split_columns(part):
        if pair:
            mine, theirs = to_sides(part)
            return mine.astype(jnp.float32), theirs.astype(half_type)
        return None, part.astype(half_type)

    def join_columns(mine, theirs):
        if pair:
            return mine + other_side(theirs).astype(jnp.float32)
        return lax.psum_scatter(theirs, "tensor", scatter_dimension=1, tiled=True).astype(
            jnp.float32
        )

    def own_columns(part):
        return join_columns(*split_columns(part))

    def columns_of(full):
        if pair:
            return to_sides(full)[0]
        return lax.dynamic_slice_in_dim(full, col_start, col_width, full.ndim - 1)

    def both_halves(cols):
        if pair:
            return cols, other_side(cols)
        full = lax.all_gather(cols, "tensor", axis=1, tiled=True)
        return full[:, :half_width], full[:, half_width:]

    attn_cols = own_columns(proj_part)
    latent_total = tensor_sum(latent_part.astype(half_type))
    latent_out = latent_total.astype(half_type)
    mixed_cols = (
        columns_of(layer_input).astype(jnp.float32)
        + attn_cols
        + jnp.dot(latent_out, columns_of(out_up_rows), preferred_element_type=jnp.float32)
    )
    expert_gain_cols = columns_of(expert_norm_gain[None, :])
    square_sum = tensor_sum(jnp.sum(mixed_cols * mixed_cols, axis=1, keepdims=True))
    mixed_scale = lax.rsqrt(square_sum / MODEL_WIDTH + norm_eps)
    moe_cols_in = (mixed_cols * mixed_scale * expert_gain_cols).astype(half_type)

    def gates_of(first, second):
        moe_in = from_sides(first, second)
        logits_t = lax.dot_general(
            router, moe_in, (((0,), (1,)), ((), ())), preferred_element_type=jnp.float32
        )
        top_logit = jnp.max(jnp.where(chosen_mask, logits_t, -jnp.inf), axis=0, keepdims=True)
        gate_exp = jnp.where(chosen_mask, jnp.exp(jnp.minimum(logits_t - top_logit, 0.0)), 0.0)
        return gate_exp / jnp.sum(gate_exp, axis=0, keepdims=True)

    def experts_of(k, pieces):
        return call_experts(
            k,
            flip_arr,
            group_of(place_all, k)[:, :, None, :],
            group_of(gates_all, k)[:, :, None, :],
            group_of(target_all, k),
            expert_gate_weight,
            expert_up_weight,
            d_raw[0],
            pieces,
            capacity,
            expert_total * tok_count // half_width,
        )

    def outputs_of(k, hidden):
        return call_output(
            flip_arr,
            group_of(target_all, k),
            expert_down_weight,
            hidden,
            capacity,
            half_width,
        )

    quads = ring_count
    own0, own1, core0, core1 = ([None] * quads for _ in range(4))
    af, asec, ff, fs = ([None] * quads for _ in range(4))
    d_raw = [None]
    hidden = [None] * quads

    def make_sums():
        return {
            name: [None] * quads for name in ("send", "keep", "got", "side_got", "arrived")
        }

    flat_groups = {"grads": (), "outs": (2,)} if pair else {"grads": range(4), "outs": range(4)}

    grads, outs = make_sums(), make_sums()

    def move_first(j):
        own0[j + 1] = onward(own0[j], data_count)

    def move_second(j):
        own1[j + 1] = onward(own1[j], data_count)

    def send_across(j):
        af[j] = swap(own0[j], data_count, 2)
        core0[j] = swap(own0[j], data_count, 1)

    def send_rest(j):
        asec[j] = (
            other_side(af[j]) if pair else swap(own1[j], data_count, 2)
        )
        core1[j] = swap(own1[j], data_count, 1)
        ff[j] = swap(af[j], data_count, 1)

    def send_last(j):
        fs[j] = swap(asec[j], data_count, 1)

    def run_experts(k):
        pieces = [own0[k], own1[k], core0[k], core1[k], af[k], asec[k], ff[k], fs[k]]
        grads["send"][k], grads["keep"][k], hidden[k] = experts_of(k, pieces)

    def run_outputs(k):
        outs["send"][k], outs["keep"][k] = outputs_of(k, hidden[k])

    def is_flat(sums, k):
        return k in flat_groups["grads" if sums is grads else "outs"]

    def sum_cores(sums, k):
        sums["got"][k] = swap(sums["send"][k], data_count, 1)

    def sum_sides(sums, k):
        keep, got = sums["keep"][k], sums["got"][k]
        away = plus(keep[1, 1], got[1, 1])
        sums["side_got"][k] = swap(away, data_count, 2) if is_flat(sums, k) else other_side(away)

    def sum_across(sums, k):
        near = [sums["keep"][k][1, 0], sums["got"][k][1, 0]]
        if not is_flat(sums, k):
            near.append(sums["side_got"][k])
        sums["arrived"][k] = swap(plus(*near), data_count, 2)

    def first_of(sums, k):
        return [sums["keep"][k][0, 0], sums["got"][k][0, 0], sums["arrived"][k]]

    def second_of(sums, k):
        terms = [sums["keep"][k][0, 1], sums["got"][k][0, 1]]
        return terms + [sums["side_got"][k]] if is_flat(sums, k) else terms

    def onward_sum(*terms):
        return onward(plus(*terms), data_count)

    def step_end(*more):
        groups = (
            own0, own1, core0, core1, af, asec, ff, fs, d_raw, hidden,
            *grads.values(), *outs.values(),
        )
        fenced = fence(groups, more)
        for old, fresh in zip(groups, fenced[0]):
            old[:] = fresh
        return fenced[1]

    own0[0] = moe_cols_in if pair else both_halves(moe_cols_in)[0]
    own1[0] = both_halves(moe_cols_in)[1]
    move_first(0)
    send_across(0)
    step_end()
    gates_t = gates_of(own0[0], own1[0])
    gates_all = lax.all_to_all(
        gates_t.reshape(data_count, local_experts, tok_count), "dp", 0, 0, tiled=True
    )[order]
    move_second(0)
    send_rest(0)
    send_across(1)
    gates_t, gates_all, g_all = step_end(gates_t, gates_all, g_all)
    move_first(1)
    send_rest(1)
    send_last(0)
    d_raw[0] = call_grad_rows(
        order, place_all[:, :, None, :], expert_down_weight, g_all, capacity
    )
    step_end()
    move_second(1)
    send_across(2)
    send_last(1)
    run_experts(1)
    step_end()
    move_first(2)
    send_rest(2)
    sum_cores(grads, 1)
    run_experts(0)
    step_end()
    move_second(2)
    send_across(3)
    send_last(2)
    sum_sides(grads, 1)
    sum_cores(grads, 0)
    run_experts(2)
    step_end()
    second = onward_sum(*second_of(grads, 1))
    send_rest(3)
    sum_across(grads, 1)
    sum_cores(grads, 2)
    run_outputs(1)
    (second,) = step_end(second)
    send_last(3)
    sum_sides(grads, 2)
    second = onward_sum(second, *second_of(grads, 2))
    run_experts(3)
    (second,) = step_end(second)
    first = onward_sum(*first_of(grads, 1))
    sum_across(grads, 2)
    sum_sides(grads, 0)
    sum_cores(grads, 3)
    sum_cores(outs, 1)
    run_outputs(2)
    first, second = step_end(first, second)
    first = onward_sum(first, *first_of(grads, 2))
    sum_sides(grads, 3)
    sum_across(grads, 0)
    sum_cores(outs, 2)
    run_outputs(3)
    if pair:
        second = plus(second, *second_of(grads, 3))
    first, second = step_end(first, second)
    if not pair:
        second = plus(second, *second_of(grads, 3))
    second = onward(second, data_count)
    sum_across(grads, 3)
    sum_cores(outs, 3)
    sum_sides(outs, 1)
    run_outputs(0)
    first, second = step_end(first, plus(second, *second_of(grads, 0)))
    first = onward_sum(first, *first_of(grads, 3))
    sum_cores(outs, 0)
    sum_across(outs, 1)
    if pair:
        from_other = other_side(second).astype(jnp.float32)
        grad_moe_cols = first.astype(jnp.float32) + from_other
        for term in first_of(grads, 0):
            grad_moe_cols += term.astype(jnp.float32)
    else:
        first = plus(first, *first_of(grads, 0))
        grad_gates = tensor_sum(first[tok_count:])
        grad_moe_cols = own_columns(from_sides(first[:tok_count], second[:tok_count]))
        grad_moe_cols = jnp.pad(grad_moe_cols, ((0, 0), (0, half_width - col_width)))
        grad_moe_cols = jnp.concatenate([grad_moe_cols, grad_gates], axis=0)
    (grad_moe_cols,) = step_end(grad_moe_cols)
    sum_sides(outs, 2)
    out_second = onward_sum(*second_of(outs, 1))
    d_gate_home = grad_moe_cols[tok_count:].reshape(expert_total, tok_count)
    grad_moe_cols = grad_moe_cols[:tok_count, :col_width]

    weighted = gates_t * d_gate_home
    grad_logits_t = (
        gates_t * (d_gate_home - jnp.sum(weighted, axis=0, keepdims=True))
    ).astype(half_type)
    router_cols = router.T
    grad_moe_cols = grad_moe_cols + lax.dot_general(
        grad_logits_t,
        columns_of(router_cols),
        (((0,), (0,)), ((), ())),
        preferred_element_type=jnp.float32,
    )
    along = tensor_sum(
        jnp.sum(mixed_cols * expert_gain_cols * grad_moe_cols, axis=1, keepdims=True)
    )
    grad_mixed_cols = (
        cotangent.astype(jnp.float32)
        + expert_gain_cols * mixed_scale * grad_moe_cols
        - mixed_cols * (mixed_scale * mixed_scale * mixed_scale * (along / MODEL_WIDTH))
    )
    branch_cols = grad_mixed_cols.astype(half_type)
    grad_branch = from_sides(*both_halves(branch_cols))
    grad_branch, out_second = step_end(grad_branch, out_second)
    out_first = onward_sum(*first_of(outs, 1))
    sum_across(outs, 2)
    out_second = onward_sum(out_second, *second_of(outs, 2))
    sum_sides(outs, 3)

    grad_latent_out = nt_dot(grad_branch, out_up_rows).astype(half_type)
    grad_up_out = lax.dot_general(
        latent_out, branch_cols, (((0,), (0,)), ((), ())), preferred_element_type=jnp.float32
    )
    grad_attended = nt_dot(grad_branch, output_weight_matrix) + jnp.dot(
        grad_latent_out, out_down_rows, preferred_element_type=jnp.float32
    )
    grad_heads = grad_attended.astype(half_type)
    grad_down_out = lax.dot_general(
        grad_latent_out, attended, (((0,), (0,)), ((), ())), preferred_element_type=jnp.float32
    )

    grad_raw = call_heads(
        attend_back_kernel,
        "attend_back",
        [raw_proj[0], raw_proj[1], queries, keys, values, grad_heads],
        head_shared,
        3,
    )
    grad_raw, out_first, out_second = step_end(grad_raw, out_first, out_second)
    out_first = onward_sum(out_first, *first_of(outs, 2))
    sum_sides(outs, 0)
    sum_across(outs, 3)
    latent_parts = jnp.concatenate([nt_dot(grad_raw[p], up_rows[p]) for p in range(3)], axis=1)
    grad_latent = tensor_sum(latent_parts.astype(half_type)).astype(half_type)
    grad_up = [
        lax.dot_general(
            latents[p], grad_raw[p], (((0,), (0,)), ((), ())), preferred_element_type=jnp.float32
        )
        for p in range(3)
    ]
    grad_down = lax.dot_general(
        grad_latent, normed, (((0,), (0,)), ((), ())), preferred_element_type=jnp.float32
    )
    parts = [grad_down_out, grad_up_out] + grad_up
    parts += [
        grad_down[:, i * shard_local_width : (i + 1) * shard_local_width]
        for i in range(tensor_count)
    ]
    parts = jnp.concatenate([part.astype(half_type) for part in parts], axis=0)
    parts_all = lax.all_gather(parts, "dp", axis=0)
    holds = numbers[None, :] == jnp.arange(ADAPTER_CHOICES, dtype=jnp.int32)[:, None]
    adapter_sums = jnp.einsum(
        "as,src->arc", holds.astype(half_type), parts_all, preferred_element_type=jnp.float32
    )

    def rows_at(i):
        return adapter_sums[:, i * ADAPTER_RANK : (i + 1) * ADAPTER_RANK]

    sum_up_qkv = jnp.stack([rows_at(2 + p) for p in range(3)])
    sum_down_qkv = jnp.stack(
        [
            jnp.concatenate([rows_at(5 + 3 * i + p) for i in range(tensor_count)], axis=2)
            for p in range(3)
        ]
    ).transpose(0, 1, 3, 2)

    grad_normed_part = nt_dot(grad_raw[0], w_proj[0])
    grad_normed_part += nt_dot(grad_raw[1], w_proj[1])
    grad_normed_part += nt_dot(grad_raw[2], w_proj[2])
    grad_normed_mine, grad_normed_other = split_columns(grad_normed_part)
    grad_normed_other, out_first = step_end(grad_normed_other, out_first)
    out_second = onward_sum(out_second, *second_of(outs, 3))
    sum_across(outs, 0)
    grad_normed_cols = join_columns(grad_normed_mine, grad_normed_other)
    grad_normed_cols += jnp.dot(
        grad_latent, columns_of(down_rows), preferred_element_type=jnp.float32
    )
    attention_gain_cols = columns_of(attention_norm_gain[None, :])
    hidden_cols = columns_of(layer_input).astype(jnp.float32)
    along_in = tensor_sum(
        jnp.sum(hidden_cols * attention_gain_cols * grad_normed_cols, axis=1, keepdims=True)
    )
    along_in, out_second = step_end(along_in, out_second)
    out_first = plus(onward_sum(out_first, *first_of(outs, 3)), *first_of(outs, 0))
    out_second = plus(out_second, *second_of(outs, 0))
    if pair:
        moe_cols = out_first.astype(jnp.float32) + other_side(out_second).astype(jnp.float32)
    else:
        moe_cols = own_columns(from_sides(out_first, out_second))
    layer_out = (mixed_cols + moe_cols).astype(half_type)
    grad_input = (
        grad_mixed_cols
        + attention_gain_cols * hidden_scale * grad_normed_cols
        - hidden_cols * (hidden_scale * hidden_scale * hidden_scale * (along_in / MODEL_WIDTH))
    )
    return (
        layer_out,
        grad_input,
        sum_down_qkv,
        sum_up_qkv,
        rows_at(0).transpose(0, 2, 1),
        rows_at(1),
    )


def solution(mesh):
    return jax.shard_map(
        local,
        mesh=mesh,
        in_specs=(
            P("dp", None),
            P("dp", "tensor"),
            P(),
            P(),
            P(),
            P(),
            P(None, "tensor"),
            P(None, "tensor"),
            P(None, "tensor"),
            P("tensor", None),
            P(),
            P(None, None, None, "tensor"),
            P(None, "tensor", None),
            P(),
            P(),
            P("dp", None, "tensor"),
            P("dp", None, "tensor"),
            P("dp", "tensor", None),
            P("dp", None),
            P("dp"),
            P("dp", None),
        ),
        out_specs=(
            P("dp", "tensor"),
            P("dp", "tensor"),
            P(),
            P(None, None, None, "tensor"),
            P(None, "tensor", None),
            P(None, None, "tensor"),
        ),
        check_vma=False,
    )
```

```python
import functools

import jax
import jax.numpy as jnp
from jax import lax
from jax.experimental import pallas as pl
from jax.experimental.pallas import tpu as pltpu
from jax.sharding import PartitionSpec as P

MODEL_WIDTH = 2048
HEAD_WIDTH = 128
TOP = 8
LEN = 512
ADAPTER_RANK = 16
ADAPTER_CHOICES = 8
QUAD = 4

norm_eps = 1e-05
head_eps = 1e-06
rope_base = 50000.0
half_type = jnp.bfloat16
VMEM_LIMIT = 56 * 1024 * 1024


def rotation(positions):
    half_dim = HEAD_WIDTH // 2
    inverse = rope_base ** (-(jnp.arange(half_dim, dtype=jnp.float32) * 2.0 / HEAD_WIDTH))
    angles = positions.astype(jnp.float32)[:, None] * inverse[None, :]
    cosine, sine = jnp.cos(angles), jnp.sin(angles)
    return (
        jnp.concatenate([cosine, cosine], axis=1),
        jnp.concatenate([-sine, sine], axis=1),
    )


def nt_dot(left, right):
    return lax.dot_general(
        left, right, (((1,), (1,)), ((), ())), preferred_element_type=jnp.float32
    )


def tn_dot(left, right):
    return lax.dot_general(
        left, right, (((0,), (0,)), ((), ())), preferred_element_type=jnp.float32
    )


def head_prep(raw, gain, cosine, sine):
    scale = lax.rsqrt(jnp.mean(raw * raw, axis=-1, keepdims=True) + head_eps)
    scaled = raw * scale * gain
    return scaled * cosine + pltpu.roll(scaled, HEAD_WIDTH // 2, 1) * sine


def head_prep_back(grad, raw, gain, cosine, sine):
    scale = lax.rsqrt(jnp.mean(raw * raw, axis=-1, keepdims=True) + head_eps)
    turned = (grad * cosine - pltpu.roll(grad, HEAD_WIDTH // 2, 1) * sine) * gain
    along = jnp.mean(raw * turned, axis=-1, keepdims=True)
    return scale * turned - raw * (scale * scale * scale * along)


def masked_exp(queries, keys, docs_col, docs_row):
    scores = nt_dot(queries, keys) * HEAD_WIDTH ** (-0.5)
    scores = jnp.where(docs_col == docs_row, scores, -1e30)
    exp_scores = jnp.exp(scores - jnp.max(scores, axis=-1, keepdims=True))
    return exp_scores, jnp.sum(exp_scores, axis=-1, keepdims=True)


def attend_kernel(
    raw_q, raw_k, raw_v, cosine, sine, gain_q, gain_k, docs_col, docs_row, out, queries, keys, values
):
    q = head_prep(raw_q[...], gain_q[...], cosine[...], sine[...]).astype(half_type)
    k = head_prep(raw_k[...], gain_k[...], cosine[...], sine[...]).astype(half_type)
    v = raw_v[...].astype(half_type)
    queries[...], keys[...], values[...] = q, k, v
    exp_scores, total = masked_exp(q, k, docs_col[...], docs_row[...])
    probs = (exp_scores / total).astype(half_type)
    out[...] = jnp.dot(probs, v, preferred_element_type=jnp.float32).astype(half_type)


def attend_back_kernel(
    raw_q, raw_k, queries, keys, values, grad, cosine, sine, gain_q, gain_k, docs_col, docs_row,
    grad_q, grad_k, grad_v,
):
    q, k, v, g = queries[...], keys[...], values[...], grad[...]
    score_scale = HEAD_WIDTH ** (-0.5)
    exp_scores, total = masked_exp(q, k, docs_col[...], docs_row[...])
    probs = exp_scores / total
    grad_v[...] = tn_dot(probs.astype(half_type), g).astype(half_type)
    grad_probs = nt_dot(g, v)
    delta = jnp.sum(probs * grad_probs, axis=-1, keepdims=True)
    grad_scores = (probs * (grad_probs - delta)).astype(half_type)
    d_q = jnp.dot(grad_scores, k, preferred_element_type=jnp.float32) * score_scale
    d_k = tn_dot(grad_scores, q) * score_scale
    grad_q[...] = head_prep_back(d_q, raw_q[...], gain_q[...], cosine[...], sine[...]).astype(
        half_type
    )
    grad_k[...] = head_prep_back(d_k, raw_k[...], gain_k[...], cosine[...], sine[...]).astype(
        half_type
    )


def call_heads(kernel, name, by_head, shared, out_count):
    toks, width = by_head[0].shape
    head = pl.BlockSpec((toks, HEAD_WIDTH), lambda h: (0, h))
    return pl.pallas_call(
        kernel,
        out_shape=[jax.ShapeDtypeStruct((toks, width), half_type)] * out_count,
        grid=(width // HEAD_WIDTH,),
        in_specs=[head] * len(by_head)
        + [pl.BlockSpec(v.shape, lambda h: (0, 0)) for v in shared],
        out_specs=[head] * out_count,
        compiler_params=pltpu.CompilerParams(
            dimension_semantics=("arbitrary",), vmem_limit_bytes=VMEM_LIMIT
        ),
        cost_estimate=pl.CostEstimate(
            flops=10 * toks * toks * width, bytes_accessed=8 * toks * width, transcendentals=toks * toks
        ),
        name=name,
    )(*by_head, *shared)


def start_blocks(pieces, buffer_ref, sems, flip):
    for b in range(QUAD):
        for r in range(2):
            pltpu.make_async_copy(
                pieces[2 * b + r], buffer_ref.at[b, r ^ flip], sems.at[b, r]
            ).start()


def wait_block(pieces, buffer_ref, sems, b):
    for r in range(2):
        pltpu.make_async_copy(pieces[0], buffer_ref.at[b, r], sems.at[b, r]).wait()


def pick_rows(place_ref, half_at, rows_ref, b, experts, cap, tile):
    toks = half_at(0).shape[0]
    slot = lax.broadcasted_iota(jnp.int32, (cap, toks), 0)
    picks = jnp.concatenate(
        [jnp.where(slot == place_ref[b, e], 1.0, 0.0) for e in range(experts)], axis=0
    ).astype(half_type)
    half = rows_ref.shape[4]

    for h in range(rows_ref.shape[1]):
        for start in range(0, half, tile):
            rows = jnp.dot(
                picks,
                half_at(h)[:, start : start + tile],
                preferred_element_type=jnp.float32,
            ).astype(half_type)
            for e in range(experts):
                rows_ref[e, h, b, :, start : start + tile] = rows[e * cap : (e + 1) * cap]


def add_rows(target_ref, rows_ref, out_ref, b, flip, experts, cap, tile):
    target = target_ref[b]
    toks = target.shape[0]
    lane = lax.broadcasted_iota(jnp.int32, (toks, experts * cap), 1)
    hit = lane == target[:, 0:1]
    for e in range(1, experts):
        hit = jnp.logical_or(hit, lane == target[:, e : e + 1])
    spread = jnp.where(hit, 1.0, 0.0).astype(half_type)
    half = rows_ref.shape[4]

    for h in range(2):
        for start in range(0, half, tile):
            rows = jnp.concatenate(
                [rows_ref[e, h, b, :, start : start + tile] for e in range(experts)], axis=0
            )
            out_ref[0, h ^ flip, :toks, start : start + tile] = jnp.dot(
                spread, rows, preferred_element_type=jnp.float32
            ).astype(half_type)


def add_gates(dgate_ref, out_ref, b, device, experts):
    toks, half = dgate_ref.shape[3], out_ref.shape[3]
    extra = out_ref.shape[2] - toks
    per_row = half // toks
    row = lax.broadcasted_iota(jnp.int32, (extra, half), 0)
    values = jnp.zeros((extra, half), jnp.float32)
    for i in range(experts // per_row):
        line = jnp.concatenate(
            [dgate_ref[i * per_row + n, b] for n in range(per_row)], axis=1
        )
        values = jnp.where(row == device * (experts // per_row) + i, line, values)
    for h in range(2):
        out_ref[0, h, toks:, :] = values.astype(half_type)


def grad_rows_kernel(experts, cap, block_ids, place_ref, down_ref, block_ref, out_ref, rows_ref):
    step = pl.program_id(0)
    sides, blocks, part = rows_ref.shape[1], rows_ref.shape[2], rows_ref.shape[4]

    @pl.when(step < blocks)
    def _():
        pick_rows(
            place_ref,
            lambda h: block_ref.at[0, h],
            rows_ref,
            step,
            experts,
            cap,
            min(part, 512),
        )

    @pl.when(step >= blocks)
    def _():
        e = step - blocks
        total = nt_dot(rows_ref[e, 0].reshape(blocks * cap, part), down_ref[0, :, :part])
        for h in range(1, sides):
            total += nt_dot(
                rows_ref[e, h].reshape(blocks * cap, part),
                down_ref[0, :, h * part : (h + 1) * part],
            )
        out_ref[0] = total.astype(half_type)


def expert_kernel(
    experts,
    cap,
    flip_ref,
    place_ref,
    gate_ref,
    target_ref,
    wg_ref,
    wu_ref,
    dh_ref,
    own_first_ref,
    own_second_ref,
    core_first_ref,
    core_second_ref,
    across_first_ref,
    across_second_ref,
    far_first_ref,
    far_second_ref,
    send_ref,
    keep_ref,
    hidden_ref,
    buffer_ref,
    rows_ref,
    dgate_ref,
    wg_buffer,
    wu_buffer,
    sems,
    weight_sems,
):
    block_refs = [
        own_first_ref,
        own_second_ref,
        core_first_ref,
        core_second_ref,
        across_first_ref,
        across_second_ref,
        far_first_ref,
        far_second_ref,
    ]
    step = pl.program_id(0)
    half = buffer_ref.shape[3]
    toks = buffer_ref.shape[2]

    def weight_copies(e):
        return (
            pltpu.make_async_copy(wg_ref.at[e], wg_buffer.at[e], weight_sems.at[e, 0]),
            pltpu.make_async_copy(wu_ref.at[e], wu_buffer.at[e], weight_sems.at[e, 1]),
        )

    @pl.when(step == 0)
    def _():
        start_blocks(block_refs, buffer_ref, sems, flip_ref[0])

    @pl.when(step < experts)
    def _():
        for copy in weight_copies(step):
            copy.start()

    @pl.when(step < QUAD)
    def _():
        wait_block(block_refs, buffer_ref, sems, step)
        pick_rows(
            place_ref, lambda h: buffer_ref.at[step, h], rows_ref, step, experts, cap, 512
        )

    @pl.when(jnp.logical_and(step >= QUAD, step < QUAD + experts))
    def _():
        e = step - QUAD
        for copy in weight_copies(e):
            copy.wait()
        first = rows_ref[e, 0].reshape(QUAD * cap, half)
        second = rows_ref[e, 1].reshape(QUAD * cap, half)
        pre_gate = jnp.dot(first, wg_buffer[e, :half], preferred_element_type=jnp.float32)
        pre_gate += jnp.dot(second, wg_buffer[e, half:], preferred_element_type=jnp.float32)
        pre_up = jnp.dot(first, wu_buffer[e, :half], preferred_element_type=jnp.float32)
        pre_up += jnp.dot(second, wu_buffer[e, half:], preferred_element_type=jnp.float32)
        sig = lax.logistic(pre_gate)
        silu = pre_gate * sig
        act = silu * pre_up
        d_raw = dh_ref[0].astype(jnp.float32)
        slot = lax.broadcasted_iota(jnp.int32, (cap, toks), 0)
        gate_parts = []
        for b in range(QUAD):
            hit = slot == place_ref[b, e]
            gate_parts.append(
                jnp.sum(jnp.where(hit, gate_ref[b, e], 0.0), axis=1, keepdims=True)
            )
        gate_col = jnp.concatenate(gate_parts, axis=0)
        hidden_ref[0] = (act * gate_col).astype(half_type)
        d_col = jnp.sum(act * d_raw, axis=1, keepdims=True)
        for b in range(QUAD):
            hit = slot == place_ref[b, e]
            dgate_ref[e, b] = jnp.sum(
                jnp.where(hit, d_col[b * cap : (b + 1) * cap], 0.0), axis=0, keepdims=True
            )
        d_hidden = d_raw * gate_col
        d_up = (d_hidden * silu).astype(half_type)
        d_gate = (d_hidden * pre_up * (sig * (1.0 + pre_gate * (1.0 - sig)))).astype(half_type)
        for h in range(2):
            d_in = nt_dot(d_gate, wg_buffer[e, h * half : (h + 1) * half])
            d_in += nt_dot(d_up, wu_buffer[e, h * half : (h + 1) * half])
            rows_ref[e, h] = d_in.astype(half_type).reshape(QUAD, cap, half)

    for which, out_ref in ((0, send_ref), (1, keep_ref)):
        first_step = QUAD + experts + 2 * which

        @pl.when(jnp.logical_and(step >= first_step, step < first_step + 2))
        def _():
            b = 2 * (step - first_step) + 1 - which
            add_rows(target_ref, rows_ref, out_ref, b, flip_ref[0], experts, cap, 512)
            add_gates(dgate_ref, out_ref, b, flip_ref[1], experts)


def output_kernel(
    experts,
    cap,
    flip_ref,
    target_ref,
    down_ref,
    hidden_ref,
    send_ref,
    keep_ref,
    rows_ref,
    down_buffer,
    weight_sems,
):
    step = pl.program_id(0)
    half = rows_ref.shape[4]

    def weight_copy(e):
        return pltpu.make_async_copy(down_ref.at[e], down_buffer.at[e], weight_sems.at[e])

    @pl.when(step == 0)
    def _():
        for e in range(experts):
            weight_copy(e).start()

    @pl.when(step < experts)
    def _():
        weight_copy(step).wait()
        for h in range(2):
            out = jnp.dot(
                hidden_ref[step],
                down_buffer[step, :, h * half : (h + 1) * half],
                preferred_element_type=jnp.float32,
            )
            rows_ref[step, h] = out.astype(half_type).reshape(QUAD, cap, half)

    for which, out_ref in ((0, send_ref), (1, keep_ref)):
        first_step = experts + 2 * which

        @pl.when(jnp.logical_and(step >= first_step, step < first_step + 2))
        def _():
            b = 2 * (step - first_step) + 1 - which
            add_rows(target_ref, rows_ref, out_ref, b, flip_ref[0], experts, cap, 512)


def whole(shape):
    return pl.BlockSpec(shape, lambda i, *_: (0,) * len(shape), pipeline_mode=pl.Buffered(1))


def per_step(shape, first, count):
    return pl.BlockSpec(
        (1,) + shape[1:], lambda i, *_: (jnp.clip(i - first, 0, count - 1),) + (0,) * (len(shape) - 1)
    )


def call_grad_rows(block_ids, place, down, blocks, cap):
    experts, hidden_units, width = down.shape
    count, sides, toks, half = blocks.shape
    rows = count * cap
    return pl.pallas_call(
        functools.partial(grad_rows_kernel, experts, cap),
        out_shape=jax.ShapeDtypeStruct((experts, rows, hidden_units), half_type),
        grid_spec=pltpu.PrefetchScalarGridSpec(
            num_scalar_prefetch=1,
            grid=(count + experts,),
            in_specs=[
                whole(place.shape),
                per_step(down.shape, count, experts),
                pl.BlockSpec(
                    (1, sides, toks, half),
                    lambda i, ids: (ids[jnp.minimum(i, count - 1)], 0, 0, 0),
                ),
            ],
            out_specs=per_step((experts, rows, hidden_units), count, experts),
            scratch_shapes=[pltpu.VMEM((experts, sides, count, cap, half), half_type)],
        ),
        compiler_params=pltpu.CompilerParams(
            dimension_semantics=("arbitrary",), vmem_limit_bytes=VMEM_LIMIT
        ),
        cost_estimate=pl.CostEstimate(
            flops=4 * experts * rows * width * (toks + hidden_units),
            bytes_accessed=2 * (down.size + blocks.size + experts * rows * hidden_units),
            transcendentals=0,
        ),
        name="grad_rows",
    )(block_ids, place, down, blocks)


def call_experts(group, flip, place, gate, target, gate_w, up_w, d_raw, pieces, cap, extra):
    experts, width, hidden_units = gate_w.shape
    toks, half = pieces[0].shape
    rows = QUAD * cap
    blocks = (2, 2, toks + extra, half)
    return pl.pallas_call(
        functools.partial(expert_kernel, experts, cap),
        out_shape=(
            jax.ShapeDtypeStruct(blocks, half_type),
            jax.ShapeDtypeStruct(blocks, half_type),
            jax.ShapeDtypeStruct((experts, rows, hidden_units), half_type),
        ),
        grid_spec=pltpu.PrefetchScalarGridSpec(
            num_scalar_prefetch=1,
            grid=(2 * QUAD + experts,),
            in_specs=[
                whole(place.shape),
                whole(gate.shape),
                whole(target.shape),
                pl.BlockSpec(memory_space=pl.ANY),
                pl.BlockSpec(memory_space=pl.ANY),
                pl.BlockSpec(
                    (1, rows, hidden_units),
                    lambda i, *_: (jnp.clip(i - QUAD, 0, experts - 1), group, 0),
                ),
            ]
            + [pl.BlockSpec(memory_space=pl.ANY)] * len(pieces),
            out_specs=(
                per_step(blocks, QUAD + experts, 2),
                per_step(blocks, QUAD + experts + 2, 2),
                per_step((experts, rows, hidden_units), QUAD, experts),
            ),
            scratch_shapes=[
                pltpu.VMEM((QUAD, 2, toks, half), half_type),
                pltpu.VMEM((experts, 2, QUAD, cap, half), half_type),
                pltpu.VMEM((experts, QUAD, 1, toks), jnp.float32),
                pltpu.VMEM(gate_w.shape, half_type),
                pltpu.VMEM(up_w.shape, half_type),
                pltpu.SemaphoreType.DMA((QUAD, 2)),
                pltpu.SemaphoreType.DMA((experts, 2)),
            ],
        ),
        compiler_params=pltpu.CompilerParams(
            dimension_semantics=("arbitrary",), vmem_limit_bytes=VMEM_LIMIT
        ),
        cost_estimate=pl.CostEstimate(
            flops=6 * experts * rows * width * (toks + 2 * hidden_units),
            bytes_accessed=2 * (2 * gate_w.size + 4 * QUAD * toks * half),
            transcendentals=experts * rows * hidden_units,
        ),
        name="experts",
    )(flip, place, gate, target, gate_w, up_w, d_raw, *pieces)


def call_output(flip, target, down, hidden, cap, half):
    experts, hidden_units, width = down.shape
    toks = target.shape[1]
    rows = QUAD * cap
    blocks = (2, 2, toks, half)
    return pl.pallas_call(
        functools.partial(output_kernel, experts, cap),
        out_shape=(
            jax.ShapeDtypeStruct(blocks, half_type),
            jax.ShapeDtypeStruct(blocks, half_type),
        ),
        grid_spec=pltpu.PrefetchScalarGridSpec(
            num_scalar_prefetch=1,
            grid=(QUAD + experts,),
            in_specs=[
                whole(target.shape),
                pl.BlockSpec(memory_space=pl.ANY),
                whole(hidden.shape),
            ],
            out_specs=(per_step(blocks, experts, 2), per_step(blocks, experts + 2, 2)),
            scratch_shapes=[
                pltpu.VMEM((experts, 2, QUAD, cap, half), half_type),
                pltpu.VMEM(down.shape, half_type),
                pltpu.SemaphoreType.DMA((experts,)),
            ],
        ),
        compiler_params=pltpu.CompilerParams(
            dimension_semantics=("arbitrary",), vmem_limit_bytes=VMEM_LIMIT
        ),
        cost_estimate=pl.CostEstimate(
            flops=4 * experts * rows * width * (toks + hidden_units),
            bytes_accessed=2 * (down.size + 2 * QUAD * toks * half),
            transcendentals=0,
        ),
        name="outputs",
    )(flip, target, down, hidden)


def swap(values, data_count, bit):
    return lax.ppermute(values, "dp", [(i, i ^ bit) for i in range(data_count)])


def onward(values, data_count):
    return lax.ppermute(values, "dp", [(i, (i + QUAD) % data_count) for i in range(data_count)])


def other_side(values):
    return lax.ppermute(values, "tensor", [(0, 1), (1, 0)])


def fence(*values):
    return lax.optimization_barrier(values)


def plus(*terms):
    total = terms[0].astype(jnp.float32)
    for term in terms[1:]:
        total = total + term.astype(jnp.float32)
    return total.astype(half_type)


def local(
    layer_input,
    cotangent,
    attention_norm_gain,
    expert_norm_gain,
    query_norm_gain,
    key_norm_gain,
    query_weight_matrix,
    key_weight_matrix,
    value_weight_matrix,
    output_weight_matrix,
    adapter_projection_down,
    adapter_projection_up,
    adapter_output_down,
    adapter_output_up,
    router,
    expert_gate_weight,
    expert_up_weight,
    expert_down_weight,
    segments,
    sequence_adapter_index,
    routes,
):
    tok_count = layer_input.shape[0]
    tensor_count = lax.axis_size("tensor")
    data_count = lax.axis_size("dp")
    pair = tensor_count == 2
    ring_count = data_count // QUAD
    col_width = MODEL_WIDTH // tensor_count
    half_width = MODEL_WIDTH // 2
    side = lax.axis_index("tensor")
    col_start = side * col_width
    place_dp = lax.axis_index("dp")
    flip = side.astype(jnp.int32) if pair else jnp.int32(0)
    flip_arr = jnp.stack([flip, place_dp.astype(jnp.int32)])
    shard_local_width = query_weight_matrix.shape[1]
    local_experts = expert_gate_weight.shape[0]
    expert_total = local_experts * data_count
    capacity = 5 * tok_count * TOP // (4 * expert_total)
    token_ids = jnp.arange(tok_count, dtype=jnp.int32)
    positions = token_ids % LEN

    def to_sides(full):
        if pair:
            low_cols, high_cols = full[:, :half_width], full[:, half_width:]
            return (
                jnp.where(flip == 0, low_cols, high_cols),
                jnp.where(flip == 0, high_cols, low_cols),
            )
        return full[:, :half_width], full[:, half_width:]

    def from_sides(first, second):
        if pair:
            return jnp.concatenate(
                [jnp.where(flip == 0, first, second), jnp.where(flip == 0, second, first)], axis=1
            )
        return jnp.concatenate([first, second], axis=1)

    routes_t = routes.T
    expert_ids = jnp.arange(expert_total, dtype=jnp.int32)
    chosen_mask = jnp.any(routes_t[:, None, :] == expert_ids[None, :, None], axis=0)
    earlier = (token_ids[:, None] < token_ids[None, :]).astype(half_type)
    rank = jnp.dot(chosen_mask.astype(half_type), earlier, preferred_element_type=jnp.float32)
    place_own = jnp.where(chosen_mask, rank, -1.0).astype(jnp.int32)
    number = jnp.broadcast_to(sequence_adapter_index[:1, None], (data_count, 1, tok_count))
    place_own = jnp.concatenate(
        [place_own.reshape(data_count, local_experts, tok_count), number], axis=1
    )
    place_all = lax.all_to_all(place_own, "dp", 0, 0, tiled=True)
    numbers = place_all[:, local_experts, 0]
    place_all = place_all[:, :local_experts]
    ring_at, quad_at = place_dp // QUAD, place_dp % QUAD
    group_ids = jnp.arange(data_count, dtype=jnp.int32)
    order = ((ring_at - group_ids // QUAD) % ring_count) * QUAD + (quad_at ^ (group_ids % QUAD))
    place_all = place_all[order]
    target_all = jnp.where(
        place_all >= 0,
        place_all + capacity * jnp.arange(local_experts, dtype=jnp.int32)[None, :, None],
        -1,
    ).transpose(0, 2, 1)

    def group_of(values, j):
        return values[j * QUAD : (j + 1) * QUAD]

    adapter = sequence_adapter_index[0]

    def own_adapter(factors, axis):
        return lax.dynamic_index_in_dim(factors, adapter, axis, keepdims=False)

    down_rows = own_adapter(adapter_projection_down.transpose(0, 1, 3, 2), 1)
    down_rows = down_rows.reshape(3 * ADAPTER_RANK, MODEL_WIDTH)
    up_rows = own_adapter(adapter_projection_up, 1)
    out_down_rows = own_adapter(adapter_output_down.transpose(0, 2, 1), 0)
    out_up_rows = own_adapter(adapter_output_up, 0)
    doc_flat = segments.reshape(-1)
    hidden32 = layer_input.astype(jnp.float32)
    hidden_scale = lax.rsqrt(
        jnp.mean(hidden32 * hidden32, axis=-1, keepdims=True) + norm_eps
    )
    normed = (hidden32 * hidden_scale * attention_norm_gain).astype(half_type)
    w_proj = [query_weight_matrix, key_weight_matrix, value_weight_matrix]
    latents = nt_dot(normed, down_rows).astype(half_type)
    latents = [latents[:, p * ADAPTER_RANK : (p + 1) * ADAPTER_RANK] for p in range(3)]
    raw_proj = [
        jnp.dot(normed, w_proj[p], preferred_element_type=jnp.float32)
        + jnp.dot(latents[p], up_rows[p], preferred_element_type=jnp.float32)
        for p in range(3)
    ]
    g_all = lax.all_gather(cotangent, ("dp", "tensor"), axis=0)
    g_all = g_all.reshape(data_count, tensor_count, tok_count, col_width)
    raw_proj[0], place_all, target_all = fence(raw_proj[0], place_all, target_all)
    head_shared = [
        *rotation(positions),
        query_norm_gain[None, :],
        key_norm_gain[None, :],
        doc_flat[:, None],
        doc_flat[None, :],
    ]
    attended, queries, keys, values = call_heads(
        attend_kernel, "attend", raw_proj, head_shared, 4
    )
    proj_part = jnp.dot(attended, output_weight_matrix, preferred_element_type=jnp.float32)
    latent_part = nt_dot(attended, out_down_rows)

    def tensor_sum(part):
        if pair:
            return part.astype(jnp.float32) + other_side(part).astype(jnp.float32)
        return lax.psum(part, "tensor").astype(jnp.float32)

    def split_columns(part):
        if pair:
            mine, theirs = to_sides(part)
            return mine.astype(jnp.float32), theirs.astype(half_type)
        return None, part.astype(half_type)

    def join_columns(mine, theirs):
        if pair:
            return mine + other_side(theirs).astype(jnp.float32)
        return lax.psum_scatter(theirs, "tensor", scatter_dimension=1, tiled=True).astype(
            jnp.float32
        )

    def own_columns(part):
        return join_columns(*split_columns(part))

    def columns_of(full):
        if pair:
            return to_sides(full)[0]
        return lax.dynamic_slice_in_dim(full, col_start, col_width, full.ndim - 1)

    def both_halves(cols):
        if pair:
            return cols, other_side(cols)
        full = lax.all_gather(cols, "tensor", axis=1, tiled=True)
        return full[:, :half_width], full[:, half_width:]

    attn_cols = own_columns(proj_part)
    latent_total = tensor_sum(latent_part.astype(half_type))
    latent_out = latent_total.astype(half_type)
    mixed_cols = (
        columns_of(layer_input).astype(jnp.float32)
        + attn_cols
        + jnp.dot(latent_out, columns_of(out_up_rows), preferred_element_type=jnp.float32)
    )
    expert_gain_cols = columns_of(expert_norm_gain[None, :])
    square_sum = tensor_sum(jnp.sum(mixed_cols * mixed_cols, axis=1, keepdims=True))
    mixed_scale = lax.rsqrt(square_sum / MODEL_WIDTH + norm_eps)
    moe_cols_in = (mixed_cols * mixed_scale * expert_gain_cols).astype(half_type)

    def gates_of(first, second):
        moe_in = from_sides(first, second)
        logits_t = lax.dot_general(
            router, moe_in, (((0,), (1,)), ((), ())), preferred_element_type=jnp.float32
        )
        top_logit = jnp.max(jnp.where(chosen_mask, logits_t, -jnp.inf), axis=0, keepdims=True)
        gate_exp = jnp.where(chosen_mask, jnp.exp(jnp.minimum(logits_t - top_logit, 0.0)), 0.0)
        return gate_exp / jnp.sum(gate_exp, axis=0, keepdims=True)

    def experts_of(k, pieces):
        return call_experts(
            k,
            flip_arr,
            group_of(place_all, k)[:, :, None, :],
            group_of(gates_all, k)[:, :, None, :],
            group_of(target_all, k),
            expert_gate_weight,
            expert_up_weight,
            d_raw[0],
            pieces,
            capacity,
            expert_total * tok_count // half_width,
        )

    def outputs_of(k, hidden):
        return call_output(
            flip_arr,
            group_of(target_all, k),
            expert_down_weight,
            hidden,
            capacity,
            half_width,
        )

    quads = ring_count
    own0, own1, core0, core1 = ([None] * quads for _ in range(4))
    af, asec, ff, fs = ([None] * quads for _ in range(4))
    d_raw = [None]
    hidden = [None] * quads

    def make_sums():
        return {
            name: [None] * quads for name in ("send", "keep", "got", "side_got", "arrived")
        }

    flat_groups = {"grads": (), "outs": (2,)} if pair else {"grads": range(4), "outs": range(4)}

    grads, outs = make_sums(), make_sums()

    def move_first(j):
        own0[j + 1] = onward(own0[j], data_count)

    def move_second(j):
        own1[j + 1] = onward(own1[j], data_count)

    def send_across(j):
        af[j] = swap(own0[j], data_count, 2)
        core0[j] = swap(own0[j], data_count, 1)

    def send_rest(j):
        asec[j] = (
            other_side(af[j]) if pair else swap(own1[j], data_count, 2)
        )
        core1[j] = swap(own1[j], data_count, 1)
        ff[j] = swap(af[j], data_count, 1)

    def send_last(j):
        fs[j] = swap(asec[j], data_count, 1)

    def run_experts(k):
        pieces = [own0[k], own1[k], core0[k], core1[k], af[k], asec[k], ff[k], fs[k]]
        grads["send"][k], grads["keep"][k], hidden[k] = experts_of(k, pieces)

    def run_outputs(k):
        outs["send"][k], outs["keep"][k] = outputs_of(k, hidden[k])

    def is_flat(sums, k):
        return k in flat_groups["grads" if sums is grads else "outs"]

    def sum_cores(sums, k):
        sums["got"][k] = swap(sums["send"][k], data_count, 1)

    def away_of(sums, k):
        return plus(sums["keep"][k][1, 1], sums["got"][k][1, 1])

    def near_of(sums, k):
        near = [sums["keep"][k][1, 0], sums["got"][k][1, 0]]
        return plus(*near) if is_flat(sums, k) else plus(*near, sums["side_got"][k])

    def sum_sides(sums, k, away=None):
        away = away_of(sums, k) if away is None else away
        sums["side_got"][k] = swap(away, data_count, 2) if is_flat(sums, k) else other_side(away)

    def sum_across(sums, k, near=None):
        near = near_of(sums, k) if near is None else near
        sums["arrived"][k] = swap(near, data_count, 2)

    def first_of(sums, k):
        return [sums["keep"][k][0, 0], sums["got"][k][0, 0], sums["arrived"][k]]

    def second_of(sums, k):
        terms = [sums["keep"][k][0, 1], sums["got"][k][0, 1]]
        return terms + [sums["side_got"][k]] if is_flat(sums, k) else terms

    def onward_sum(*terms):
        return onward(plus(*terms), data_count)

    def step_end(*more):
        groups = (
            own0, own1, core0, core1, af, asec, ff, fs, d_raw, hidden,
            *grads.values(), *outs.values(),
        )
        fenced = fence(groups, more)
        for old, fresh in zip(groups, fenced[0]):
            old[:] = fresh
        return fenced[1]

    own0[0] = moe_cols_in if pair else both_halves(moe_cols_in)[0]
    own1[0] = both_halves(moe_cols_in)[1]
    move_first(0)
    send_across(0)
    step_end()
    gates_t = gates_of(own0[0], own1[0])
    gates_all = lax.all_to_all(
        gates_t.reshape(data_count, local_experts, tok_count), "dp", 0, 0, tiled=True
    )[order]
    move_second(0)
    send_rest(0)
    send_across(1)
    gates_t, gates_all, g_all = step_end(gates_t, gates_all, g_all)
    move_first(1)
    send_rest(1)
    send_last(0)
    d_raw[0] = call_grad_rows(
        order, place_all[:, :, None, :], expert_down_weight, g_all, capacity
    )
    step_end()
    move_second(1)
    send_across(2)
    send_last(1)
    run_experts(1)
    step_end()
    move_first(2)
    send_rest(2)
    sum_cores(grads, 1)
    run_experts(0)
    step_end()
    move_second(2)
    send_across(3)
    send_last(2)
    sum_sides(grads, 1)
    sum_cores(grads, 0)
    run_experts(2)
    step_end()
    second = onward_sum(*second_of(grads, 1))
    send_rest(3)
    sum_across(grads, 1)
    sum_cores(grads, 2)
    run_outputs(1)
    (second,) = step_end(second)
    send_last(3)
    sum_sides(grads, 2)
    second = onward_sum(second, *second_of(grads, 2))
    run_experts(3)
    (second,) = step_end(second)
    first = onward_sum(*first_of(grads, 1))
    sum_across(grads, 2)
    sum_sides(grads, 0)
    sum_cores(grads, 3)
    sum_cores(outs, 1)
    run_outputs(2)
    first, second = step_end(first, second)
    first = onward_sum(first, *first_of(grads, 2))
    sum_sides(grads, 3)
    sum_across(grads, 0)
    sum_cores(outs, 2)
    run_outputs(3)
    if pair:
        second = plus(second, *second_of(grads, 3))
    first, second = step_end(first, second)
    if not pair:
        second = plus(second, *second_of(grads, 3))
    second = onward(second, data_count)
    sum_across(grads, 3)
    sum_cores(outs, 3)
    sum_sides(outs, 1)
    run_outputs(0)
    first, second = step_end(first, plus(second, *second_of(grads, 0)))
    first = onward_sum(first, *first_of(grads, 3))
    sum_cores(outs, 0)
    sum_across(outs, 1)
    if pair:
        from_other = other_side(second).astype(jnp.float32)
        grad_moe_cols = first.astype(jnp.float32) + from_other
        for term in first_of(grads, 0):
            grad_moe_cols += term.astype(jnp.float32)
    else:
        first = plus(first, *first_of(grads, 0))
        grad_gates = tensor_sum(first[tok_count:])
        grad_moe_cols = own_columns(from_sides(first[:tok_count], second[:tok_count]))
        grad_moe_cols = jnp.pad(grad_moe_cols, ((0, 0), (0, half_width - col_width)))
        grad_moe_cols = jnp.concatenate([grad_moe_cols, grad_gates], axis=0)
    out_second = plus(*second_of(outs, 1))
    grad_moe_cols, out_second = step_end(grad_moe_cols, out_second)
    sum_sides(outs, 2)
    out_second = onward(out_second, data_count)
    out_first = onward_sum(*first_of(outs, 1))
    near_next, away_next = near_of(outs, 2), away_of(outs, 3)
    d_gate_home = grad_moe_cols[tok_count:].reshape(expert_total, tok_count)
    grad_moe_cols = grad_moe_cols[:tok_count, :col_width]

    weighted = gates_t * d_gate_home
    grad_logits_t = (
        gates_t * (d_gate_home - jnp.sum(weighted, axis=0, keepdims=True))
    ).astype(half_type)
    router_cols = router.T
    grad_moe_cols = grad_moe_cols + lax.dot_general(
        grad_logits_t,
        columns_of(router_cols),
        (((0,), (0,)), ((), ())),
        preferred_element_type=jnp.float32,
    )
    along = tensor_sum(
        jnp.sum(mixed_cols * expert_gain_cols * grad_moe_cols, axis=1, keepdims=True)
    )
    grad_mixed_cols = (
        cotangent.astype(jnp.float32)
        + expert_gain_cols * mixed_scale * grad_moe_cols
        - mixed_cols * (mixed_scale * mixed_scale * mixed_scale * (along / MODEL_WIDTH))
    )
    branch_cols = grad_mixed_cols.astype(half_type)
    grad_branch = from_sides(*both_halves(branch_cols))
    grad_branch, out_first, out_second, near_next, away_next = step_end(
        grad_branch, out_first, out_second, near_next, away_next
    )
    sum_across(outs, 2, near_next)
    out_second = onward_sum(out_second, *second_of(outs, 2))
    sum_sides(outs, 3, away_next)
    away_next = away_of(outs, 0)

    grad_latent_out = nt_dot(grad_branch, out_up_rows).astype(half_type)
    grad_up_out = lax.dot_general(
        latent_out, branch_cols, (((0,), (0,)), ((), ())), preferred_element_type=jnp.float32
    )
    grad_attended = nt_dot(grad_branch, output_weight_matrix) + jnp.dot(
        grad_latent_out, out_down_rows, preferred_element_type=jnp.float32
    )
    grad_heads = grad_attended.astype(half_type)
    grad_down_out = lax.dot_general(
        grad_latent_out, attended, (((0,), (0,)), ((), ())), preferred_element_type=jnp.float32
    )

    grad_raw = call_heads(
        attend_back_kernel,
        "attend_back",
        [raw_proj[0], raw_proj[1], queries, keys, values, grad_heads],
        head_shared,
        3,
    )
    grad_raw, out_first, out_second, away_next = step_end(
        grad_raw, out_first, out_second, away_next
    )
    out_first = onward_sum(out_first, *first_of(outs, 2))
    sum_sides(outs, 0, away_next)
    sum_across(outs, 3)
    out_second = plus(out_second, *second_of(outs, 3))
    latent_parts = jnp.concatenate([nt_dot(grad_raw[p], up_rows[p]) for p in range(3)], axis=1)
    grad_latent = tensor_sum(latent_parts.astype(half_type)).astype(half_type)
    grad_up = [
        lax.dot_general(
            latents[p], grad_raw[p], (((0,), (0,)), ((), ())), preferred_element_type=jnp.float32
        )
        for p in range(3)
    ]
    grad_down = lax.dot_general(
        grad_latent, normed, (((0,), (0,)), ((), ())), preferred_element_type=jnp.float32
    )
    parts = [grad_down_out, grad_up_out] + grad_up
    parts += [
        grad_down[:, i * shard_local_width : (i + 1) * shard_local_width]
        for i in range(tensor_count)
    ]
    parts = jnp.concatenate([part.astype(half_type) for part in parts], axis=0)
    parts_all = lax.all_gather(parts, "dp", axis=0)
    holds = numbers[None, :] == jnp.arange(ADAPTER_CHOICES, dtype=jnp.int32)[:, None]
    adapter_sums = jnp.einsum(
        "as,src->arc", holds.astype(half_type), parts_all, preferred_element_type=jnp.float32
    )

    def rows_at(i):
        return adapter_sums[:, i * ADAPTER_RANK : (i + 1) * ADAPTER_RANK]

    sum_down_out, sum_up_out = rows_at(0).transpose(0, 2, 1), rows_at(1)
    sum_up_qkv = jnp.stack([rows_at(2 + p) for p in range(3)])
    sum_down_qkv = jnp.stack(
        [
            jnp.concatenate([rows_at(5 + 3 * i + p) for i in range(tensor_count)], axis=2)
            for p in range(3)
        ]
    ).transpose(0, 1, 3, 2)

    grad_normed_part = nt_dot(grad_raw[0], w_proj[0])
    grad_normed_part += nt_dot(grad_raw[1], w_proj[1])
    grad_normed_part += nt_dot(grad_raw[2], w_proj[2])
    grad_normed_mine, grad_normed_other = split_columns(grad_normed_part)
    grad_normed_other, out_first, out_second = step_end(grad_normed_other, out_first, out_second)
    out_second = onward(out_second, data_count)
    sum_across(outs, 0)
    grad_normed_cols = join_columns(grad_normed_mine, grad_normed_other)
    grad_normed_cols += jnp.dot(
        grad_latent, columns_of(down_rows), preferred_element_type=jnp.float32
    )
    attention_gain_cols = columns_of(attention_norm_gain[None, :])
    hidden_cols = columns_of(layer_input).astype(jnp.float32)
    along_in = tensor_sum(
        jnp.sum(hidden_cols * attention_gain_cols * grad_normed_cols, axis=1, keepdims=True)
    )
    along_in, out_second = step_end(along_in, out_second)
    out_first = onward_sum(out_first, *first_of(outs, 3))
    out_first, sum_down_qkv, sum_up_qkv, sum_down_out, sum_up_out = fence(
        out_first, sum_down_qkv, sum_up_qkv, sum_down_out, sum_up_out
    )
    out_first = plus(out_first, *first_of(outs, 0))
    out_second = plus(out_second, *second_of(outs, 0))
    if pair:
        moe_cols = out_first.astype(jnp.float32) + other_side(out_second).astype(jnp.float32)
    else:
        moe_cols = own_columns(from_sides(out_first, out_second))
    layer_out = (mixed_cols + moe_cols).astype(half_type)
    grad_input = (
        grad_mixed_cols
        + attention_gain_cols * hidden_scale * grad_normed_cols
        - hidden_cols * (hidden_scale * hidden_scale * hidden_scale * (along_in / MODEL_WIDTH))
    )
    return (
        layer_out,
        grad_input,
        sum_down_qkv,
        sum_up_qkv,
        sum_down_out,
        sum_up_out,
    )


def solution(mesh):
    return jax.shard_map(
        local,
        mesh=mesh,
        in_specs=(
            P("dp", None),
            P("dp", "tensor"),
            P(),
            P(),
            P(),
            P(),
            P(None, "tensor"),
            P(None, "tensor"),
            P(None, "tensor"),
            P("tensor", None),
            P(),
            P(None, None, None, "tensor"),
            P(None, "tensor", None),
            P(),
            P(),
            P("dp", None, "tensor"),
            P("dp", None, "tensor"),
            P("dp", "tensor", None),
            P("dp", None),
            P("dp"),
            P("dp", None),
        ),
        out_specs=(
            P("dp", "tensor"),
            P("dp", "tensor"),
            P(),
            P(None, None, None, "tensor"),
            P(None, "tensor", None),
            P(None, None, "tensor"),
        ),
        check_vma=False,
    )
```

```python
import functools

import jax
import jax.numpy as jnp
from jax import lax
from jax.experimental import pallas as pl
from jax.experimental.pallas import tpu as pltpu
from jax.sharding import PartitionSpec as P

MODEL_WIDTH = 2048
HEAD_WIDTH = 128
TOP = 8
LEN = 512
ADAPTER_RANK = 16
ADAPTER_CHOICES = 8
QUAD = 4

norm_eps = 1e-05
head_eps = 1e-06
rope_base = 50000.0
half_type = jnp.bfloat16
VMEM_LIMIT = 56 * 1024 * 1024


def rotation(positions):
    half_dim = HEAD_WIDTH // 2
    inverse = rope_base ** (-(jnp.arange(half_dim, dtype=jnp.float32) * 2.0 / HEAD_WIDTH))
    angles = positions.astype(jnp.float32)[:, None] * inverse[None, :]
    cosine, sine = jnp.cos(angles), jnp.sin(angles)
    return (
        jnp.concatenate([cosine, cosine], axis=1),
        jnp.concatenate([-sine, sine], axis=1),
    )


def nt_dot(left, right):
    return lax.dot_general(
        left, right, (((1,), (1,)), ((), ())), preferred_element_type=jnp.float32
    )


def tn_dot(left, right):
    return lax.dot_general(
        left, right, (((0,), (0,)), ((), ())), preferred_element_type=jnp.float32
    )


def head_prep(raw, gain, cosine, sine):
    scale = lax.rsqrt(jnp.mean(raw * raw, axis=-1, keepdims=True) + head_eps)
    scaled = raw * scale * gain
    return scaled * cosine + pltpu.roll(scaled, HEAD_WIDTH // 2, 1) * sine


def head_prep_back(grad, raw, gain, cosine, sine):
    scale = lax.rsqrt(jnp.mean(raw * raw, axis=-1, keepdims=True) + head_eps)
    turned = (grad * cosine - pltpu.roll(grad, HEAD_WIDTH // 2, 1) * sine) * gain
    along = jnp.mean(raw * turned, axis=-1, keepdims=True)
    return scale * turned - raw * (scale * scale * scale * along)


def masked_exp(queries, keys, docs_col, docs_row):
    scores = nt_dot(queries, keys) * HEAD_WIDTH ** (-0.5)
    scores = jnp.where(docs_col == docs_row, scores, -1e30)
    exp_scores = jnp.exp(scores - jnp.max(scores, axis=-1, keepdims=True))
    return exp_scores, jnp.sum(exp_scores, axis=-1, keepdims=True)


def attend_kernel(
    raw_q, raw_k, raw_v, cosine, sine, gain_q, gain_k, docs_col, docs_row, out, queries, keys, values
):
    q = head_prep(raw_q[...], gain_q[...], cosine[...], sine[...]).astype(half_type)
    k = head_prep(raw_k[...], gain_k[...], cosine[...], sine[...]).astype(half_type)
    v = raw_v[...].astype(half_type)
    queries[...], keys[...], values[...] = q, k, v
    exp_scores, total = masked_exp(q, k, docs_col[...], docs_row[...])
    probs = (exp_scores / total).astype(half_type)
    out[...] = jnp.dot(probs, v, preferred_element_type=jnp.float32).astype(half_type)


def attend_back_kernel(
    raw_q, raw_k, queries, keys, values, grad, cosine, sine, gain_q, gain_k, docs_col, docs_row,
    grad_q, grad_k, grad_v,
):
    q, k, v, g = queries[...], keys[...], values[...], grad[...]
    score_scale = HEAD_WIDTH ** (-0.5)
    exp_scores, total = masked_exp(q, k, docs_col[...], docs_row[...])
    probs = exp_scores / total
    grad_v[...] = tn_dot(probs.astype(half_type), g).astype(half_type)
    grad_probs = nt_dot(g, v)
    delta = jnp.sum(probs * grad_probs, axis=-1, keepdims=True)
    grad_scores = (probs * (grad_probs - delta)).astype(half_type)
    d_q = jnp.dot(grad_scores, k, preferred_element_type=jnp.float32) * score_scale
    d_k = tn_dot(grad_scores, q) * score_scale
    grad_q[...] = head_prep_back(d_q, raw_q[...], gain_q[...], cosine[...], sine[...]).astype(
        half_type
    )
    grad_k[...] = head_prep_back(d_k, raw_k[...], gain_k[...], cosine[...], sine[...]).astype(
        half_type
    )


def call_heads(kernel, name, by_head, shared, out_count):
    toks, width = by_head[0].shape
    head = pl.BlockSpec((toks, HEAD_WIDTH), lambda h: (0, h))
    return pl.pallas_call(
        kernel,
        out_shape=[jax.ShapeDtypeStruct((toks, width), half_type)] * out_count,
        grid=(width // HEAD_WIDTH,),
        in_specs=[head] * len(by_head)
        + [pl.BlockSpec(v.shape, lambda h: (0, 0)) for v in shared],
        out_specs=[head] * out_count,
        compiler_params=pltpu.CompilerParams(
            dimension_semantics=("arbitrary",), vmem_limit_bytes=VMEM_LIMIT
        ),
        cost_estimate=pl.CostEstimate(
            flops=10 * toks * toks * width, bytes_accessed=8 * toks * width, transcendentals=toks * toks
        ),
        name=name,
    )(*by_head, *shared)


def start_blocks(pieces, buffer_ref, sems, flip):
    for b in range(QUAD):
        for r in range(2):
            pltpu.make_async_copy(
                pieces[2 * b + r], buffer_ref.at[b, r ^ flip], sems.at[b, r]
            ).start()


def wait_block(pieces, buffer_ref, sems, b):
    for r in range(2):
        pltpu.make_async_copy(pieces[0], buffer_ref.at[b, r], sems.at[b, r]).wait()


def pick_rows(place_ref, half_at, rows_ref, b, experts, cap, tile):
    toks = half_at(0).shape[0]
    slot = lax.broadcasted_iota(jnp.int32, (cap, toks), 0)
    picks = jnp.concatenate(
        [jnp.where(slot == place_ref[b, e], 1.0, 0.0) for e in range(experts)], axis=0
    ).astype(half_type)
    half = rows_ref.shape[4]

    for h in range(rows_ref.shape[1]):
        for start in range(0, half, tile):
            rows = jnp.dot(
                picks,
                half_at(h)[:, start : start + tile],
                preferred_element_type=jnp.float32,
            ).astype(half_type)
            for e in range(experts):
                rows_ref[e, h, b, :, start : start + tile] = rows[e * cap : (e + 1) * cap]


def add_rows(target_ref, rows_ref, out_ref, b, flip, experts, cap, tile):
    target = target_ref[b]
    toks = target.shape[0]
    lane = lax.broadcasted_iota(jnp.int32, (toks, experts * cap), 1)
    hit = lane == target[:, 0:1]
    for e in range(1, experts):
        hit = jnp.logical_or(hit, lane == target[:, e : e + 1])
    spread = jnp.where(hit, 1.0, 0.0).astype(half_type)
    half = rows_ref.shape[4]

    for h in range(2):
        for start in range(0, half, tile):
            rows = jnp.concatenate(
                [rows_ref[e, h, b, :, start : start + tile] for e in range(experts)], axis=0
            )
            out_ref[0, h ^ flip, :toks, start : start + tile] = jnp.dot(
                spread, rows, preferred_element_type=jnp.float32
            ).astype(half_type)


def add_gates(dgate_ref, out_ref, b, device, experts):
    toks, half = dgate_ref.shape[3], out_ref.shape[3]
    extra = out_ref.shape[2] - toks
    per_row = half // toks
    row = lax.broadcasted_iota(jnp.int32, (extra, half), 0)
    values = jnp.zeros((extra, half), jnp.float32)
    for i in range(experts // per_row):
        line = jnp.concatenate(
            [dgate_ref[i * per_row + n, b] for n in range(per_row)], axis=1
        )
        values = jnp.where(row == device * (experts // per_row) + i, line, values)
    for h in range(2):
        out_ref[0, h, toks:, :] = values.astype(half_type)


def grad_rows_kernel(experts, cap, block_ids, place_ref, down_ref, block_ref, out_ref, rows_ref):
    step = pl.program_id(0)
    sides, blocks, part = rows_ref.shape[1], rows_ref.shape[2], rows_ref.shape[4]

    @pl.when(step < blocks)
    def _():
        pick_rows(
            place_ref,
            lambda h: block_ref.at[0, h],
            rows_ref,
            step,
            experts,
            cap,
            min(part, 512),
        )

    @pl.when(step >= blocks)
    def _():
        e = step - blocks
        total = nt_dot(rows_ref[e, 0].reshape(blocks * cap, part), down_ref[0, :, :part])
        for h in range(1, sides):
            total += nt_dot(
                rows_ref[e, h].reshape(blocks * cap, part),
                down_ref[0, :, h * part : (h + 1) * part],
            )
        out_ref[0] = total.astype(half_type)


def expert_kernel(
    experts,
    cap,
    flip_ref,
    place_ref,
    gate_ref,
    target_ref,
    wg_ref,
    wu_ref,
    dh_ref,
    own_first_ref,
    own_second_ref,
    core_first_ref,
    core_second_ref,
    across_first_ref,
    across_second_ref,
    far_first_ref,
    far_second_ref,
    send_ref,
    keep_ref,
    hidden_ref,
    buffer_ref,
    rows_ref,
    dgate_ref,
    wg_buffer,
    wu_buffer,
    sems,
    weight_sems,
):
    block_refs = [
        own_first_ref,
        own_second_ref,
        core_first_ref,
        core_second_ref,
        across_first_ref,
        across_second_ref,
        far_first_ref,
        far_second_ref,
    ]
    step = pl.program_id(0)
    half = buffer_ref.shape[3]
    toks = buffer_ref.shape[2]

    def weight_copies(e):
        return (
            pltpu.make_async_copy(wg_ref.at[e], wg_buffer.at[e], weight_sems.at[e, 0]),
            pltpu.make_async_copy(wu_ref.at[e], wu_buffer.at[e], weight_sems.at[e, 1]),
        )

    @pl.when(step == 0)
    def _():
        start_blocks(block_refs, buffer_ref, sems, flip_ref[0])

    @pl.when(step < experts)
    def _():
        for copy in weight_copies(step):
            copy.start()

    @pl.when(step < QUAD)
    def _():
        wait_block(block_refs, buffer_ref, sems, step)
        pick_rows(
            place_ref, lambda h: buffer_ref.at[step, h], rows_ref, step, experts, cap, 512
        )

    @pl.when(jnp.logical_and(step >= QUAD, step < QUAD + experts))
    def _():
        e = step - QUAD
        for copy in weight_copies(e):
            copy.wait()
        first = rows_ref[e, 0].reshape(QUAD * cap, half)
        second = rows_ref[e, 1].reshape(QUAD * cap, half)
        pre_gate = jnp.dot(first, wg_buffer[e, :half], preferred_element_type=jnp.float32)
        pre_gate += jnp.dot(second, wg_buffer[e, half:], preferred_element_type=jnp.float32)
        pre_up = jnp.dot(first, wu_buffer[e, :half], preferred_element_type=jnp.float32)
        pre_up += jnp.dot(second, wu_buffer[e, half:], preferred_element_type=jnp.float32)
        sig = lax.logistic(pre_gate)
        silu = pre_gate * sig
        act = silu * pre_up
        d_raw = dh_ref[0].astype(jnp.float32)
        slot = lax.broadcasted_iota(jnp.int32, (cap, toks), 0)
        gate_parts = []
        for b in range(QUAD):
            hit = slot == place_ref[b, e]
            gate_parts.append(
                jnp.sum(jnp.where(hit, gate_ref[b, e], 0.0), axis=1, keepdims=True)
            )
        gate_col = jnp.concatenate(gate_parts, axis=0)
        hidden_ref[0] = (act * gate_col).astype(half_type)
        d_col = jnp.sum(act * d_raw, axis=1, keepdims=True)
        for b in range(QUAD):
            hit = slot == place_ref[b, e]
            dgate_ref[e, b] = jnp.sum(
                jnp.where(hit, d_col[b * cap : (b + 1) * cap], 0.0), axis=0, keepdims=True
            )
        d_hidden = d_raw * gate_col
        d_up = (d_hidden * silu).astype(half_type)
        d_gate = (d_hidden * pre_up * (sig * (1.0 + pre_gate * (1.0 - sig)))).astype(half_type)
        for h in range(2):
            d_in = nt_dot(d_gate, wg_buffer[e, h * half : (h + 1) * half])
            d_in += nt_dot(d_up, wu_buffer[e, h * half : (h + 1) * half])
            rows_ref[e, h] = d_in.astype(half_type).reshape(QUAD, cap, half)

    for which, out_ref in ((0, send_ref), (1, keep_ref)):
        first_step = QUAD + experts + 2 * which

        @pl.when(jnp.logical_and(step >= first_step, step < first_step + 2))
        def _():
            b = 2 * (step - first_step) + 1 - which
            add_rows(target_ref, rows_ref, out_ref, b, flip_ref[0], experts, cap, 512)
            add_gates(dgate_ref, out_ref, b, flip_ref[1], experts)


def output_kernel(
    experts,
    cap,
    flip_ref,
    target_ref,
    down_ref,
    hidden_ref,
    send_ref,
    keep_ref,
    rows_ref,
    down_buffer,
    weight_sems,
):
    step = pl.program_id(0)
    half = rows_ref.shape[4]

    def weight_copy(e):
        return pltpu.make_async_copy(down_ref.at[e], down_buffer.at[e], weight_sems.at[e])

    @pl.when(step == 0)
    def _():
        for e in range(experts):
            weight_copy(e).start()

    @pl.when(step < experts)
    def _():
        weight_copy(step).wait()
        for h in range(2):
            out = jnp.dot(
                hidden_ref[step],
                down_buffer[step, :, h * half : (h + 1) * half],
                preferred_element_type=jnp.float32,
            )
            rows_ref[step, h] = out.astype(half_type).reshape(QUAD, cap, half)

    for which, out_ref in ((0, send_ref), (1, keep_ref)):
        first_step = experts + 2 * which

        @pl.when(jnp.logical_and(step >= first_step, step < first_step + 2))
        def _():
            b = 2 * (step - first_step) + 1 - which
            add_rows(target_ref, rows_ref, out_ref, b, flip_ref[0], experts, cap, 512)


def whole(shape):
    return pl.BlockSpec(shape, lambda i, *_: (0,) * len(shape), pipeline_mode=pl.Buffered(1))


def per_step(shape, first, count):
    return pl.BlockSpec(
        (1,) + shape[1:], lambda i, *_: (jnp.clip(i - first, 0, count - 1),) + (0,) * (len(shape) - 1)
    )


def call_grad_rows(block_ids, place, down, blocks, cap):
    experts, hidden_units, width = down.shape
    count, sides, toks, half = blocks.shape
    rows = count * cap
    return pl.pallas_call(
        functools.partial(grad_rows_kernel, experts, cap),
        out_shape=jax.ShapeDtypeStruct((experts, rows, hidden_units), half_type),
        grid_spec=pltpu.PrefetchScalarGridSpec(
            num_scalar_prefetch=1,
            grid=(count + experts,),
            in_specs=[
                whole(place.shape),
                per_step(down.shape, count, experts),
                pl.BlockSpec(
                    (1, sides, toks, half),
                    lambda i, ids: (ids[jnp.minimum(i, count - 1)], 0, 0, 0),
                ),
            ],
            out_specs=per_step((experts, rows, hidden_units), count, experts),
            scratch_shapes=[pltpu.VMEM((experts, sides, count, cap, half), half_type)],
        ),
        compiler_params=pltpu.CompilerParams(
            dimension_semantics=("arbitrary",), vmem_limit_bytes=VMEM_LIMIT
        ),
        cost_estimate=pl.CostEstimate(
            flops=4 * experts * rows * width * (toks + hidden_units),
            bytes_accessed=2 * (down.size + blocks.size + experts * rows * hidden_units),
            transcendentals=0,
        ),
        name="grad_rows",
    )(block_ids, place, down, blocks)


def call_experts(group, flip, place, gate, target, gate_w, up_w, d_raw, pieces, cap, extra):
    experts, width, hidden_units = gate_w.shape
    toks, half = pieces[0].shape
    rows = QUAD * cap
    blocks = (2, 2, toks + extra, half)
    return pl.pallas_call(
        functools.partial(expert_kernel, experts, cap),
        out_shape=(
            jax.ShapeDtypeStruct(blocks, half_type),
            jax.ShapeDtypeStruct(blocks, half_type),
            jax.ShapeDtypeStruct((experts, rows, hidden_units), half_type),
        ),
        grid_spec=pltpu.PrefetchScalarGridSpec(
            num_scalar_prefetch=1,
            grid=(2 * QUAD + experts,),
            in_specs=[
                whole(place.shape),
                whole(gate.shape),
                whole(target.shape),
                pl.BlockSpec(memory_space=pl.ANY),
                pl.BlockSpec(memory_space=pl.ANY),
                pl.BlockSpec(
                    (1, rows, hidden_units),
                    lambda i, *_: (jnp.clip(i - QUAD, 0, experts - 1), group, 0),
                ),
            ]
            + [pl.BlockSpec(memory_space=pl.ANY)] * len(pieces),
            out_specs=(
                per_step(blocks, QUAD + experts, 2),
                per_step(blocks, QUAD + experts + 2, 2),
                per_step((experts, rows, hidden_units), QUAD, experts),
            ),
            scratch_shapes=[
                pltpu.VMEM((QUAD, 2, toks, half), half_type),
                pltpu.VMEM((experts, 2, QUAD, cap, half), half_type),
                pltpu.VMEM((experts, QUAD, 1, toks), jnp.float32),
                pltpu.VMEM(gate_w.shape, half_type),
                pltpu.VMEM(up_w.shape, half_type),
                pltpu.SemaphoreType.DMA((QUAD, 2)),
                pltpu.SemaphoreType.DMA((experts, 2)),
            ],
        ),
        compiler_params=pltpu.CompilerParams(
            dimension_semantics=("arbitrary",), vmem_limit_bytes=VMEM_LIMIT
        ),
        cost_estimate=pl.CostEstimate(
            flops=6 * experts * rows * width * (toks + 2 * hidden_units),
            bytes_accessed=2 * (2 * gate_w.size + 4 * QUAD * toks * half),
            transcendentals=experts * rows * hidden_units,
        ),
        name="experts",
    )(flip, place, gate, target, gate_w, up_w, d_raw, *pieces)


def call_output(flip, target, down, hidden, cap, half):
    experts, hidden_units, width = down.shape
    toks = target.shape[1]
    rows = QUAD * cap
    blocks = (2, 2, toks, half)
    return pl.pallas_call(
        functools.partial(output_kernel, experts, cap),
        out_shape=(
            jax.ShapeDtypeStruct(blocks, half_type),
            jax.ShapeDtypeStruct(blocks, half_type),
        ),
        grid_spec=pltpu.PrefetchScalarGridSpec(
            num_scalar_prefetch=1,
            grid=(QUAD + experts,),
            in_specs=[
                whole(target.shape),
                pl.BlockSpec(memory_space=pl.ANY),
                whole(hidden.shape),
            ],
            out_specs=(per_step(blocks, experts, 2), per_step(blocks, experts + 2, 2)),
            scratch_shapes=[
                pltpu.VMEM((experts, 2, QUAD, cap, half), half_type),
                pltpu.VMEM(down.shape, half_type),
                pltpu.SemaphoreType.DMA((experts,)),
            ],
        ),
        compiler_params=pltpu.CompilerParams(
            dimension_semantics=("arbitrary",), vmem_limit_bytes=VMEM_LIMIT
        ),
        cost_estimate=pl.CostEstimate(
            flops=4 * experts * rows * width * (toks + hidden_units),
            bytes_accessed=2 * (down.size + 2 * QUAD * toks * half),
            transcendentals=0,
        ),
        name="outputs",
    )(flip, target, down, hidden)


def swap(values, data_count, bit):
    return lax.ppermute(values, "dp", [(i, i ^ bit) for i in range(data_count)])


def onward(values, data_count):
    return lax.ppermute(values, "dp", [(i, (i + QUAD) % data_count) for i in range(data_count)])


def other_side(values):
    return lax.ppermute(values, "tensor", [(0, 1), (1, 0)])


def fence(*values):
    return lax.optimization_barrier(values)


def plus(*terms):
    total = terms[0].astype(jnp.float32)
    for term in terms[1:]:
        total = total + term.astype(jnp.float32)
    return total.astype(half_type)


def local(
    layer_input,
    cotangent,
    attention_norm_gain,
    expert_norm_gain,
    query_norm_gain,
    key_norm_gain,
    query_weight_matrix,
    key_weight_matrix,
    value_weight_matrix,
    output_weight_matrix,
    adapter_projection_down,
    adapter_projection_up,
    adapter_output_down,
    adapter_output_up,
    router,
    expert_gate_weight,
    expert_up_weight,
    expert_down_weight,
    segments,
    sequence_adapter_index,
    routes,
):
    tok_count = layer_input.shape[0]
    tensor_count = lax.axis_size("tensor")
    data_count = lax.axis_size("dp")
    pair = tensor_count == 2
    ring_count = data_count // QUAD
    col_width = MODEL_WIDTH // tensor_count
    half_width = MODEL_WIDTH // 2
    side = lax.axis_index("tensor")
    col_start = side * col_width
    place_dp = lax.axis_index("dp")
    flip = side.astype(jnp.int32) if pair else jnp.int32(0)
    flip_arr = jnp.stack([flip, place_dp.astype(jnp.int32)])
    shard_local_width = query_weight_matrix.shape[1]
    local_experts = expert_gate_weight.shape[0]
    expert_total = local_experts * data_count
    capacity = 5 * tok_count * TOP // (4 * expert_total)
    token_ids = jnp.arange(tok_count, dtype=jnp.int32)
    positions = token_ids % LEN

    def to_sides(full):
        if pair:
            low_cols, high_cols = full[:, :half_width], full[:, half_width:]
            return (
                jnp.where(flip == 0, low_cols, high_cols),
                jnp.where(flip == 0, high_cols, low_cols),
            )
        return full[:, :half_width], full[:, half_width:]

    def from_sides(first, second):
        if pair:
            return jnp.concatenate(
                [jnp.where(flip == 0, first, second), jnp.where(flip == 0, second, first)], axis=1
            )
        return jnp.concatenate([first, second], axis=1)

    routes_t = routes.T
    expert_ids = jnp.arange(expert_total, dtype=jnp.int32)
    chosen_mask = jnp.any(routes_t[:, None, :] == expert_ids[None, :, None], axis=0)
    earlier = (token_ids[:, None] < token_ids[None, :]).astype(half_type)
    rank = jnp.dot(chosen_mask.astype(half_type), earlier, preferred_element_type=jnp.float32)
    place_own = jnp.where(chosen_mask, rank, -1.0).astype(jnp.int32)
    number = jnp.broadcast_to(sequence_adapter_index[:1, None], (data_count, 1, tok_count))
    place_own = jnp.concatenate(
        [place_own.reshape(data_count, local_experts, tok_count), number], axis=1
    )
    place_all = lax.all_to_all(place_own, "dp", 0, 0, tiled=True)
    numbers = place_all[:, local_experts, 0]
    place_all = place_all[:, :local_experts]
    ring_at, quad_at = place_dp // QUAD, place_dp % QUAD
    group_ids = jnp.arange(data_count, dtype=jnp.int32)
    order = ((ring_at - group_ids // QUAD) % ring_count) * QUAD + (quad_at ^ (group_ids % QUAD))
    place_all = place_all[order]
    target_all = jnp.where(
        place_all >= 0,
        place_all + capacity * jnp.arange(local_experts, dtype=jnp.int32)[None, :, None],
        -1,
    ).transpose(0, 2, 1)

    def group_of(values, j):
        return values[j * QUAD : (j + 1) * QUAD]

    adapter = sequence_adapter_index[0]

    def own_adapter(factors, axis):
        return lax.dynamic_index_in_dim(factors, adapter, axis, keepdims=False)

    down_rows = own_adapter(adapter_projection_down.transpose(0, 1, 3, 2), 1)
    down_rows = down_rows.reshape(3 * ADAPTER_RANK, MODEL_WIDTH)
    up_rows = own_adapter(adapter_projection_up, 1)
    out_down_rows = own_adapter(adapter_output_down.transpose(0, 2, 1), 0)
    out_up_rows = own_adapter(adapter_output_up, 0)
    doc_flat = segments.reshape(-1)
    hidden32 = layer_input.astype(jnp.float32)
    hidden_scale = lax.rsqrt(
        jnp.mean(hidden32 * hidden32, axis=-1, keepdims=True) + norm_eps
    )
    normed = (hidden32 * hidden_scale * attention_norm_gain).astype(half_type)
    w_proj = [query_weight_matrix, key_weight_matrix, value_weight_matrix]
    latents = nt_dot(normed, down_rows).astype(half_type)
    latents = [latents[:, p * ADAPTER_RANK : (p + 1) * ADAPTER_RANK] for p in range(3)]
    raw_proj = [
        jnp.dot(normed, w_proj[p], preferred_element_type=jnp.float32)
        + jnp.dot(latents[p], up_rows[p], preferred_element_type=jnp.float32)
        for p in range(3)
    ]
    g_all = lax.all_gather(cotangent, ("dp", "tensor"), axis=0)
    g_all = g_all.reshape(data_count, tensor_count, tok_count, col_width)
    raw_proj[0], place_all, target_all = fence(raw_proj[0], place_all, target_all)
    head_shared = [
        *rotation(positions),
        query_norm_gain[None, :],
        key_norm_gain[None, :],
        doc_flat[:, None],
        doc_flat[None, :],
    ]
    attended, queries, keys, values = call_heads(
        attend_kernel, "attend", raw_proj, head_shared, 4
    )
    proj_part = jnp.dot(attended, output_weight_matrix, preferred_element_type=jnp.float32)
    latent_part = nt_dot(attended, out_down_rows)

    def tensor_sum(part):
        if pair:
            return part.astype(jnp.float32) + other_side(part).astype(jnp.float32)
        return lax.psum(part, "tensor").astype(jnp.float32)

    def split_columns(part):
        if pair:
            mine, theirs = to_sides(part)
            return mine.astype(jnp.float32), theirs.astype(half_type)
        return None, part.astype(half_type)

    def join_columns(mine, theirs):
        if pair:
            return mine + other_side(theirs).astype(jnp.float32)
        return lax.psum_scatter(theirs, "tensor", scatter_dimension=1, tiled=True).astype(
            jnp.float32
        )

    def own_columns(part):
        return join_columns(*split_columns(part))

    def columns_of(full):
        if pair:
            return to_sides(full)[0]
        return lax.dynamic_slice_in_dim(full, col_start, col_width, full.ndim - 1)

    def both_halves(cols):
        if pair:
            return cols, other_side(cols)
        full = lax.all_gather(cols, "tensor", axis=1, tiled=True)
        return full[:, :half_width], full[:, half_width:]

    attn_cols = own_columns(proj_part)
    latent_total = tensor_sum(latent_part.astype(half_type))
    latent_out = latent_total.astype(half_type)
    mixed_cols = (
        columns_of(layer_input).astype(jnp.float32)
        + attn_cols
        + jnp.dot(latent_out, columns_of(out_up_rows), preferred_element_type=jnp.float32)
    )
    expert_gain_cols = columns_of(expert_norm_gain[None, :])
    square_sum = tensor_sum(jnp.sum(mixed_cols * mixed_cols, axis=1, keepdims=True))
    mixed_scale = lax.rsqrt(square_sum / MODEL_WIDTH + norm_eps)
    moe_cols_in = (mixed_cols * mixed_scale * expert_gain_cols).astype(half_type)

    def gates_of(first, second):
        moe_in = from_sides(first, second)
        logits_t = lax.dot_general(
            router, moe_in, (((0,), (1,)), ((), ())), preferred_element_type=jnp.float32
        )
        top_logit = jnp.max(jnp.where(chosen_mask, logits_t, -jnp.inf), axis=0, keepdims=True)
        gate_exp = jnp.where(chosen_mask, jnp.exp(jnp.minimum(logits_t - top_logit, 0.0)), 0.0)
        return gate_exp / jnp.sum(gate_exp, axis=0, keepdims=True)

    def experts_of(k, pieces):
        return call_experts(
            k,
            flip_arr,
            group_of(place_all, k)[:, :, None, :],
            group_of(gates_all, k)[:, :, None, :],
            group_of(target_all, k),
            expert_gate_weight,
            expert_up_weight,
            d_raw[0],
            pieces,
            capacity,
            expert_total * tok_count // half_width,
        )

    def outputs_of(k, hidden):
        return call_output(
            flip_arr,
            group_of(target_all, k),
            expert_down_weight,
            hidden,
            capacity,
            half_width,
        )

    quads = ring_count
    own0, own1, core0, core1 = ([None] * quads for _ in range(4))
    af, asec, ff, fs = ([None] * quads for _ in range(4))
    d_raw = [None]
    hidden = [None] * quads

    def make_sums():
        return {
            name: [None] * quads for name in ("send", "keep", "got", "side_got", "arrived")
        }

    flat_groups = {"grads": (), "outs": (2,)} if pair else {"grads": range(4), "outs": range(4)}

    grads, outs = make_sums(), make_sums()

    def move_first(j):
        own0[j + 1] = onward(own0[j], data_count)

    def move_second(j):
        own1[j + 1] = onward(own1[j], data_count)

    def send_across(j):
        af[j] = swap(own0[j], data_count, 2)
        core0[j] = swap(own0[j], data_count, 1)

    def send_rest(j):
        asec[j] = (
            other_side(af[j]) if pair else swap(own1[j], data_count, 2)
        )
        core1[j] = swap(own1[j], data_count, 1)
        ff[j] = swap(af[j], data_count, 1)

    def send_last(j):
        fs[j] = swap(asec[j], data_count, 1)

    def run_experts(k):
        pieces = [own0[k], own1[k], core0[k], core1[k], af[k], asec[k], ff[k], fs[k]]
        grads["send"][k], grads["keep"][k], hidden[k] = experts_of(k, pieces)

    def run_outputs(k):
        outs["send"][k], outs["keep"][k] = outputs_of(k, hidden[k])

    def is_flat(sums, k):
        return k in flat_groups["grads" if sums is grads else "outs"]

    def sum_cores(sums, k):
        sums["got"][k] = swap(sums["send"][k], data_count, 1)

    def away_of(sums, k):
        return plus(sums["keep"][k][1, 1], sums["got"][k][1, 1])

    def near_of(sums, k):
        near = [sums["keep"][k][1, 0], sums["got"][k][1, 0]]
        return plus(*near) if is_flat(sums, k) else plus(*near, sums["side_got"][k])

    def sum_sides(sums, k, away=None):
        away = away_of(sums, k) if away is None else away
        sums["side_got"][k] = swap(away, data_count, 2) if is_flat(sums, k) else other_side(away)

    def sum_across(sums, k, near=None):
        near = near_of(sums, k) if near is None else near
        sums["arrived"][k] = swap(near, data_count, 2)

    def first_of(sums, k):
        return [sums["keep"][k][0, 0], sums["got"][k][0, 0], sums["arrived"][k]]

    def second_of(sums, k):
        terms = [sums["keep"][k][0, 1], sums["got"][k][0, 1]]
        return terms + [sums["side_got"][k]] if is_flat(sums, k) else terms

    def onward_sum(*terms):
        return onward(plus(*terms), data_count)

    def step_end(*more):
        groups = (
            own0, own1, core0, core1, af, asec, ff, fs, d_raw, hidden,
            *grads.values(), *outs.values(),
        )
        fenced = fence(groups, more)
        for old, fresh in zip(groups, fenced[0]):
            old[:] = fresh
        return fenced[1]

    own0[0] = moe_cols_in if pair else both_halves(moe_cols_in)[0]
    own1[0] = both_halves(moe_cols_in)[1]
    move_first(0)
    send_across(0)
    step_end()
    gates_t = gates_of(own0[0], own1[0])
    gates_all = lax.all_to_all(
        gates_t.reshape(data_count, local_experts, tok_count), "dp", 0, 0, tiled=True
    )[order]
    move_second(0)
    send_rest(0)
    send_across(1)
    gates_t, gates_all, g_all = step_end(gates_t, gates_all, g_all)
    move_first(1)
    send_rest(1)
    send_last(0)
    d_raw[0] = call_grad_rows(
        order, place_all[:, :, None, :], expert_down_weight, g_all, capacity
    )
    step_end()
    move_second(1)
    send_across(2)
    send_last(1)
    run_experts(1)
    step_end()
    move_first(2)
    send_rest(2)
    sum_cores(grads, 1)
    run_experts(0)
    step_end()
    move_second(2)
    send_across(3)
    send_last(2)
    sum_sides(grads, 1)
    sum_cores(grads, 0)
    run_experts(2)
    step_end()
    second = onward_sum(*second_of(grads, 1))
    send_rest(3)
    sum_across(grads, 1)
    sum_cores(grads, 2)
    run_outputs(1)
    (second,) = step_end(second)
    send_last(3)
    sum_sides(grads, 2)
    second = onward_sum(second, *second_of(grads, 2))
    run_experts(3)
    (second,) = step_end(second)
    first = onward_sum(*first_of(grads, 1))
    sum_across(grads, 2)
    sum_sides(grads, 0)
    sum_cores(grads, 3)
    sum_cores(outs, 1)
    run_outputs(2)
    first, second = step_end(first, second)
    first = onward_sum(first, *first_of(grads, 2))
    sum_sides(grads, 3)
    sum_across(grads, 0)
    sum_cores(outs, 2)
    run_outputs(3)
    if pair:
        second = plus(second, *second_of(grads, 3))
    first, second = step_end(first, second)
    if not pair:
        second = plus(second, *second_of(grads, 3))
    second = onward(second, data_count)
    sum_across(grads, 3)
    sum_cores(outs, 3)
    sum_sides(outs, 1)
    run_outputs(0)
    first, second = step_end(first, plus(second, *second_of(grads, 0)))
    first = onward_sum(first, *first_of(grads, 3))
    sum_cores(outs, 0)
    sum_across(outs, 1)
    if pair:
        from_other = other_side(second).astype(jnp.float32)
        grad_moe_cols = first.astype(jnp.float32) + from_other
        for term in first_of(grads, 0):
            grad_moe_cols += term.astype(jnp.float32)
    else:
        first = plus(first, *first_of(grads, 0))
        grad_gates = tensor_sum(first[tok_count:])
        grad_moe_cols = own_columns(from_sides(first[:tok_count], second[:tok_count]))
        grad_moe_cols = jnp.pad(grad_moe_cols, ((0, 0), (0, half_width - col_width)))
        grad_moe_cols = jnp.concatenate([grad_moe_cols, grad_gates], axis=0)
    out_second = plus(*second_of(outs, 1))
    grad_moe_cols, out_second = step_end(grad_moe_cols, out_second)
    sum_sides(outs, 2)
    out_second = onward(out_second, data_count)
    out_first = onward_sum(*first_of(outs, 1))
    near_next, away_next = near_of(outs, 2), away_of(outs, 3)
    d_gate_home = grad_moe_cols[tok_count:].reshape(expert_total, tok_count)
    grad_moe_cols = grad_moe_cols[:tok_count, :col_width]

    weighted = gates_t * d_gate_home
    grad_logits_t = (
        gates_t * (d_gate_home - jnp.sum(weighted, axis=0, keepdims=True))
    ).astype(half_type)
    router_cols = router.T
    grad_moe_cols = grad_moe_cols + lax.dot_general(
        grad_logits_t,
        columns_of(router_cols),
        (((0,), (0,)), ((), ())),
        preferred_element_type=jnp.float32,
    )
    along = tensor_sum(
        jnp.sum(mixed_cols * expert_gain_cols * grad_moe_cols, axis=1, keepdims=True)
    )
    grad_mixed_cols = (
        cotangent.astype(jnp.float32)
        + expert_gain_cols * mixed_scale * grad_moe_cols
        - mixed_cols * (mixed_scale * mixed_scale * mixed_scale * (along / MODEL_WIDTH))
    )
    branch_cols = grad_mixed_cols.astype(half_type)
    grad_branch = from_sides(*both_halves(branch_cols))
    grad_branch, out_second, near_next, away_next = step_end(
        grad_branch, out_second, near_next, away_next
    )
    sum_across(outs, 2, near_next)
    out_second = onward_sum(out_second, *second_of(outs, 2))
    sum_sides(outs, 3, away_next)
    away_next = away_of(outs, 0)

    grad_latent_out = nt_dot(grad_branch, out_up_rows).astype(half_type)
    grad_up_out = lax.dot_general(
        latent_out, branch_cols, (((0,), (0,)), ((), ())), preferred_element_type=jnp.float32
    )
    grad_attended = nt_dot(grad_branch, output_weight_matrix) + jnp.dot(
        grad_latent_out, out_down_rows, preferred_element_type=jnp.float32
    )
    grad_heads = grad_attended.astype(half_type)
    grad_down_out = lax.dot_general(
        grad_latent_out, attended, (((0,), (0,)), ((), ())), preferred_element_type=jnp.float32
    )

    grad_raw = call_heads(
        attend_back_kernel,
        "attend_back",
        [raw_proj[0], raw_proj[1], queries, keys, values, grad_heads],
        head_shared,
        3,
    )
    grad_raw, out_first, out_second, away_next = step_end(
        grad_raw, out_first, out_second, away_next
    )
    out_first = onward_sum(out_first, *first_of(outs, 2))
    sum_sides(outs, 0, away_next)
    sum_across(outs, 3)
    out_second = plus(out_second, *second_of(outs, 3))
    latent_parts = jnp.concatenate([nt_dot(grad_raw[p], up_rows[p]) for p in range(3)], axis=1)
    grad_latent = tensor_sum(latent_parts.astype(half_type)).astype(half_type)
    grad_up = [
        lax.dot_general(
            latents[p], grad_raw[p], (((0,), (0,)), ((), ())), preferred_element_type=jnp.float32
        )
        for p in range(3)
    ]
    grad_down = lax.dot_general(
        grad_latent, normed, (((0,), (0,)), ((), ())), preferred_element_type=jnp.float32
    )
    parts = [grad_down_out, grad_up_out] + grad_up
    parts += [
        grad_down[:, i * shard_local_width : (i + 1) * shard_local_width]
        for i in range(tensor_count)
    ]
    parts = jnp.concatenate([part.astype(half_type) for part in parts], axis=0)
    parts_all = lax.all_gather(parts, "dp", axis=0)
    holds = numbers[None, :] == jnp.arange(ADAPTER_CHOICES, dtype=jnp.int32)[:, None]
    adapter_sums = jnp.einsum(
        "as,src->arc", holds.astype(half_type), parts_all, preferred_element_type=jnp.float32
    )

    def rows_at(i):
        return adapter_sums[:, i * ADAPTER_RANK : (i + 1) * ADAPTER_RANK]

    sum_down_out, sum_up_out = rows_at(0).transpose(0, 2, 1), rows_at(1)
    sum_up_qkv = jnp.stack([rows_at(2 + p) for p in range(3)])
    sum_down_qkv = jnp.stack(
        [
            jnp.concatenate([rows_at(5 + 3 * i + p) for i in range(tensor_count)], axis=2)
            for p in range(3)
        ]
    ).transpose(0, 1, 3, 2)

    grad_normed_part = nt_dot(grad_raw[0], w_proj[0])
    grad_normed_part += nt_dot(grad_raw[1], w_proj[1])
    grad_normed_part += nt_dot(grad_raw[2], w_proj[2])
    grad_normed_mine, grad_normed_other = split_columns(grad_normed_part)
    grad_normed_other, out_first, out_second = step_end(grad_normed_other, out_first, out_second)
    out_second = onward(out_second, data_count)
    sum_across(outs, 0)
    grad_normed_cols = join_columns(grad_normed_mine, grad_normed_other)
    grad_normed_cols += jnp.dot(
        grad_latent, columns_of(down_rows), preferred_element_type=jnp.float32
    )
    attention_gain_cols = columns_of(attention_norm_gain[None, :])
    hidden_cols = columns_of(layer_input).astype(jnp.float32)
    along_in = tensor_sum(
        jnp.sum(hidden_cols * attention_gain_cols * grad_normed_cols, axis=1, keepdims=True)
    )
    along_in, out_second = step_end(along_in, out_second)
    out_first = onward_sum(out_first, *first_of(outs, 3))
    out_first, sum_down_qkv, sum_up_qkv, sum_down_out, sum_up_out = fence(
        out_first, sum_down_qkv, sum_up_qkv, sum_down_out, sum_up_out
    )
    out_first = plus(out_first, *first_of(outs, 0))
    out_second = plus(out_second, *second_of(outs, 0))
    if pair:
        moe_cols = out_first.astype(jnp.float32) + other_side(out_second).astype(jnp.float32)
    else:
        moe_cols = own_columns(from_sides(out_first, out_second))
    layer_out = (mixed_cols + moe_cols).astype(half_type)
    grad_input = (
        grad_mixed_cols
        + attention_gain_cols * hidden_scale * grad_normed_cols
        - hidden_cols * (hidden_scale * hidden_scale * hidden_scale * (along_in / MODEL_WIDTH))
    )
    return (
        layer_out,
        grad_input,
        sum_down_qkv,
        sum_up_qkv,
        sum_down_out,
        sum_up_out,
    )


def solution(mesh):
    return jax.shard_map(
        local,
        mesh=mesh,
        in_specs=(
            P("dp", None),
            P("dp", "tensor"),
            P(),
            P(),
            P(),
            P(),
            P(None, "tensor"),
            P(None, "tensor"),
            P(None, "tensor"),
            P("tensor", None),
            P(),
            P(None, None, None, "tensor"),
            P(None, "tensor", None),
            P(),
            P(),
            P("dp", None, "tensor"),
            P("dp", None, "tensor"),
            P("dp", "tensor", None),
            P("dp", None),
            P("dp"),
            P("dp", None),
        ),
        out_specs=(
            P("dp", "tensor"),
            P("dp", "tensor"),
            P(),
            P(None, None, None, "tensor"),
            P(None, "tensor", None),
            P(None, None, "tensor"),
        ),
        check_vma=False,
    )
```
